256 devices in a mesh: req: 32 (over y, x, core), wgt: 8 (over z).
Axes of the slice: x: 4, y: 4, z: 8, core: 2. Of those that a mesh axis runs over, the one named last changes fastest.
Arguments:
- arrivals: bfloat16 [128, 48, 6144], P('req', None, 'wgt'), may hold values from -6 to 6
- group_of: int32 [128], replicated, may hold values from 0 to 31, as said below
- lengths: int32 [128], P('req'), may hold values from 1 to 2048, as said below
- page_table: int32 [128, 16], P('req'), may hold values from 0 to 39, as said below
- ln_gain: bfloat16 [6144], replicated, may hold values from 0.25 to 1.75
- ln_bias: bfloat16 [6144], replicated, may hold values from -1.5 to 1.5
- w_qkv: bfloat16 [6144, 9216], P('req', 'wgt'), may hold values from -0.078125 to 0.078125
- qkv_bias: bfloat16 [9216], P('wgt'), may hold values from -4.5 to 4.5
- key_pool: bfloat16 [1280, 128, 3072], P('req', None, 'wgt'), may hold values from -8 to 8
- value_pool: bfloat16 [1280, 128, 3072], P('req', None, 'wgt'), may hold values from -6 to 6
Outputs:
- attended: bfloat16 [128, 48, 3072], P('req', None, 'wgt')
- new_keys: bfloat16 [128, 48, 3072], P('req', None, 'wgt')
- new_values: bfloat16 [128, 48, 3072], P('req', None, 'wgt')
The draws below stay inside these ranges and needn't reach their ends.
Inputs may be any that keep to these rules, and one draw needn't show every extreme that they name: `group_of`: every group number is named by exactly 4 requests; the requests that arrive at one group (consecutive blocks of 4 in arrival order) name different groups. `lengths`: in each group at most one request has more than 1024 cached tokens; some request has exactly 2048. `page_table`: entries name pages of the request's group's own pool of 40; the pages that hold cached tokens of one group's requests are all different.
All inputs are finite; a program needn't handle non-finite values.
Results may differ from the reference program's by a relative error of at most 0.0066.
Values may be sent and summed in bfloat16 or wider, within the bound.
A program may use at most 128 MiB of HBM per device.

```python
import math
import jax
import jax.numpy as jnp
from jax import lax

D = 6144
HEADS = 32
HEAD = 96
ROT = 24
FRESH = 48
PAGE = 128
MAXP = 16
REQ_DEV = 4
REQS = 128
POOL_DEV = 40
POOLS = 1280


def draw_group_of(key, part):
    groups_all = REQS // REQ_DEV
    base = jax.random.fold_in(key, 3)
    key_sigma, key_tau, key_offset, key_slot = jax.random.split(base, 4)
    sigma = jax.random.permutation(key_sigma, groups_all)
    tau = jax.random.permutation(key_tau, groups_all)
    offsets = jax.random.permutation(key_offset, groups_all)[:REQ_DEV]

    def slot_order(index):
        return jax.random.permutation(jax.random.fold_in(key_slot, index), REQ_DEV)
    slots = jax.vmap(slot_order)(jnp.arange(groups_all))
    target = sigma[(tau[:, None] + offsets[slots]) % groups_all]
    return target.reshape(REQS).astype(jnp.int32)


def layout(key):
    anchor = jax.random.fold_in(key, 11)
    key_short, key_long, key_place, key_peak, key_perm, key_fill = jax.random.split(anchor, 6)
    groups_all = REQS // REQ_DEV
    longest = MAXP * PAGE
    shorter = jax.random.randint(key_short, (groups_all, REQ_DEV), 1, longest // 2 + 1)
    longer = jax.random.randint(key_long, (groups_all, 1), longest // 2 + 1, longest + 1)
    placed = jax.random.randint(key_place, (groups_all, 1), 0, REQ_DEV)
    is_long = jnp.arange(REQ_DEV)[None, :] == placed
    cached = jnp.where(is_long, longer, shorter)
    peak_group = jax.random.randint(key_peak, (), 0, groups_all)
    cached = jnp.where((jnp.arange(groups_all)[:, None] == peak_group) & is_long, longest, cached)
    needed = (cached + PAGE - 1) // PAGE
    begins = jnp.cumsum(needed, axis=1) - needed

    def shuffle_one(index):
        return jax.random.permutation(jax.random.fold_in(key_perm, index), POOL_DEV)
    orders = jax.vmap(shuffle_one)(jnp.arange(groups_all))
    offsets = (begins[:, :, None] + jnp.arange(MAXP)[None, None, :]) % POOL_DEV

    def lookup(order_row, offset_rows):
        return order_row[offset_rows]
    used_pages = jax.vmap(lookup)(orders, offsets)
    filler = jax.random.randint(key_fill, (groups_all, REQ_DEV, MAXP), 0, POOL_DEV)
    table = jnp.where(jnp.arange(MAXP)[None, None, :] < needed[:, :, None], used_pages, filler)
    return (cached.reshape(REQS).astype(jnp.int32), table.reshape(REQS, MAXP).astype(jnp.int32))


def draw_lengths(key, part):
    return layout(key)[0]


def draw_page_table(key, part):
    return layout(key)[1]


def draw_qkv_bias(key, part):
    noise = jnp.clip(0.3 * jax.random.normal(jax.random.fold_in(key, 601), (HEADS, 3, HEAD), jnp.float32), -1.5, 1.5)
    return noise.reshape(3 * HEADS * HEAD).astype(jnp.bfloat16)


def draw_key_pool(key, part):
    values = jnp.clip(jax.random.normal(jax.random.fold_in(key, 701), (POOLS, PAGE, HEADS * HEAD), jnp.float32), -6.0, 6.0)
    return values.astype(jnp.bfloat16)


def level_of(own_key, extent, pieces, smallest, top_value):
    def one(position, shards_of):
        draws = jax.random.uniform(jax.random.fold_in(jax.random.fold_in(own_key, 6), position), (shards_of,), jnp.float32, smallest / len(pieces), top_value / len(pieces))
        return jnp.repeat(jnp.exp(draws), extent[position] // shards_of).reshape((-1,) + (1,) * (len(extent) - position - 1))

    loudness = one(*pieces[0])
    for cut in pieces[1:]:
        loudness = loudness * one(*cut)
    return loudness


def bell_draw(key, shape, deviation, reach, cuts=(), kind=jnp.bfloat16):
    values = deviation * jax.random.normal(key, shape, jnp.float32)
    if cuts:
        values = values * level_of(key, shape, cuts, -0.22, 0.18)
    return jnp.clip(values, -reach, reach).astype(kind)


def setup_inputs(seed: int = 0) -> dict:
    arg_keys = jax.random.split(jax.random.key(seed), 11)
    return {
        "arrivals": bell_draw(arg_keys[0], (REQS, FRESH, D), 1.0, 6.0, ((0, 32), (2, 8))),
        "group_of": draw_group_of(jax.random.fold_in(arg_keys[10], 71), 0),
        "lengths": draw_lengths(jax.random.fold_in(arg_keys[10], 71), 0),
        "page_table": draw_page_table(jax.random.fold_in(arg_keys[10], 71), 0),
        "ln_gain": jnp.clip(1.0 + 0.15 * jax.random.normal(arg_keys[4], (D,), jnp.float32), 0.25, 1.75).astype(jnp.bfloat16),
        "ln_bias": bell_draw(arg_keys[5], (D,), 0.3, 1.5),
        "w_qkv": bell_draw(arg_keys[6], (D, 3 * HEADS * HEAD), D ** -0.5, 0.078125, ((0, 32), (1, 8))),
        "qkv_bias": draw_qkv_bias(jax.random.fold_in(arg_keys[10], 71), 0),
        "key_pool": draw_key_pool(jax.random.fold_in(arg_keys[10], 71), 0),
        "value_pool": bell_draw(arg_keys[9], (POOLS, PAGE, HEADS * HEAD), 1.0, 6.0, ((0, 32), (2, 8))),
    }


EPS = 1e-05

def rotary(block, positions):
    half_rot = ROT // 2
    inverse = jnp.power(10000.0, -jnp.arange(half_rot, dtype=jnp.float32) * 2.0 / ROT)
    angles = positions[:, :, None] * inverse[None, None, :]
    cosine = jnp.cos(angles)[:, :, None, :]
    sine = jnp.sin(angles)[:, :, None, :]
    first = block[..., :half_rot]
    second = block[..., half_rot:ROT]
    return jnp.concatenate([first * cosine - second * sine, second * cosine + first * sine, block[..., ROT:]], axis=-1)

def reference(arrivals, group_of, lengths, page_table, ln_gain, ln_bias, w_qkv, qkv_bias, key_pool, value_pool):
    order = jnp.argsort(group_of, stable=True).astype(jnp.int32)
    tokens = arrivals[order].astype(jnp.float32)
    center = lax.optimization_barrier(jnp.mean(tokens, axis=-1, keepdims=True))
    spread = lax.optimization_barrier(jnp.mean(jnp.square(tokens - center), axis=-1, keepdims=True))
    normed = ((tokens - center) * lax.rsqrt(spread + EPS) * ln_gain.astype(jnp.float32) + ln_bias.astype(jnp.float32)).astype(jnp.bfloat16)
    projected = jnp.dot(normed.reshape(REQS * FRESH, D), w_qkv, preferred_element_type=jnp.float32) + qkv_bias.astype(jnp.float32)
    projected = projected.reshape(REQS, FRESH, HEADS, 3, HEAD)
    positions = (lengths[:, None] + jnp.arange(FRESH, dtype=jnp.int32)[None, :]).astype(jnp.float32)
    queries = rotary(projected[:, :, :, 0], positions).astype(jnp.bfloat16)
    new_keys = rotary(projected[:, :, :, 1], positions).astype(jnp.bfloat16)
    new_values = projected[:, :, :, 2].astype(jnp.bfloat16)
    owners = ((jnp.arange(REQS, dtype=jnp.int32) // REQ_DEV)[:, None] * POOL_DEV + page_table).astype(jnp.int32)
    scale = 1.0 / math.sqrt(HEAD)
    span = MAXP * PAGE

    def attend(items):
        query, key_new, value_new, length, pages = items
        cached_k = key_pool[pages].reshape(span, HEADS, HEAD).astype(jnp.float32)
        cached_v = value_pool[pages].reshape(span, HEADS, HEAD).astype(jnp.float32)
        query_f = query.astype(jnp.float32)
        scores_old = jnp.einsum('qhd,khd->hqk', query_f, cached_k) * scale
        visible = jnp.arange(span, dtype=jnp.int32)[None, None, :] < length
        scores_old = jnp.where(visible, scores_old, -1e+30)
        scores_new = jnp.einsum('qhd,khd->hqk', query_f, key_new.astype(jnp.float32)) * scale
        causal = jnp.arange(FRESH)[None, :, None] >= jnp.arange(FRESH)[None, None, :]
        scores_new = jnp.where(causal, scores_new, -1e+30)
        peak = jnp.maximum(lax.optimization_barrier(jnp.max(scores_old, axis=-1, keepdims=True)), lax.optimization_barrier(jnp.max(scores_new, axis=-1, keepdims=True)))
        exp_old = jnp.exp(scores_old - peak)
        exp_new = jnp.exp(scores_new - peak)
        denom = lax.optimization_barrier(jnp.sum(exp_old, axis=-1, keepdims=True)) + lax.optimization_barrier(jnp.sum(exp_new, axis=-1, keepdims=True))
        weight_old = (exp_old / denom).astype(jnp.bfloat16)
        weight_new = (exp_new / denom).astype(jnp.bfloat16)
        mixed = jnp.einsum('hqk,khd->qhd', weight_old.astype(jnp.float32), cached_v)
        mixed = mixed + jnp.einsum('hqk,khd->qhd', weight_new.astype(jnp.float32), value_new.astype(jnp.float32))
        return mixed.astype(jnp.bfloat16)
    attended = lax.map(attend, (queries, new_keys, new_values, lengths, owners))
    return (attended.reshape(REQS, FRESH, HEADS * HEAD), new_keys.reshape(REQS, FRESH, HEADS * HEAD), new_values.reshape(REQS, FRESH, HEADS * HEAD))
```

```python
import functools
import math

import jax
import jax.numpy as jnp
from jax import lax
from jax.experimental import pallas as pl
from jax.experimental.pallas import tpu as pltpu
from jax.sharding import PartitionSpec as P

HEAD = 96
ROT = 24
EPS = 1e-05
CHUNK_PAGES = 4


def rotary(block, positions):
    half_rot = ROT // 2
    inverse = jnp.power(10000.0, -jnp.arange(half_rot, dtype=jnp.float32) * 2.0 / ROT)
    angles = positions[:, :, None] * inverse[None, None, :]
    cosine = jnp.cos(angles)[:, :, None, :]
    sine = jnp.sin(angles)[:, :, None, :]
    first = block[..., :half_rot]
    second = block[..., half_rot:ROT]
    return jnp.concatenate(
        [first * cosine - second * sine, second * cosine + first * sine, block[..., ROT:]], axis=-1
    )


def attention_kernel(
    lengths, table, q_ref, k_ref, v_ref, key_pool, value_pool, out_ref, nk_ref, nv_ref, kbuf, vbuf, sems
):
    req_count, maxp = table.shape
    page, width = kbuf.shape[1], kbuf.shape[2]
    fresh = q_ref.shape[0] // req_count
    heads = width // HEAD
    rows = heads * fresh
    span = CHUNK_PAGES * page
    factor = math.log2(math.e) / math.sqrt(HEAD)

    def chunks_of(r):
        return (lengths[r] + (span - 1)) // span

    def copies(r, p):
        slot = r * maxp + p
        number = table[r, p]
        return (
            pltpu.make_async_copy(key_pool.at[number], kbuf.at[slot], sems.at[0, slot]),
            pltpu.make_async_copy(value_pool.at[number], vbuf.at[slot], sems.at[1, slot]),
        )

    for r in range(req_count):

        @pl.loop(0, chunks_of(r) * CHUNK_PAGES)
        def _(p):
            for copy in copies(r, p):
                copy.start()

    nk_ref[...] = k_ref[...]
    nv_ref[...] = v_ref[...]

    lane_head = lax.broadcasted_iota(jnp.int32, (rows, width), 1) // HEAD
    row_head = lax.broadcasted_iota(jnp.int32, (rows, width), 0) // fresh
    own_head = lane_head == row_head
    row_token = lax.broadcasted_iota(jnp.int32, (rows, fresh), 0) % fresh
    causal = row_token >= lax.broadcasted_iota(jnp.int32, (rows, fresh), 1)
    column = lax.broadcasted_iota(jnp.int32, (rows, span), 1)

    for r in range(req_count):
        mine = pl.ds(r * fresh, fresh)
        query = jnp.concatenate([q_ref[mine, :]] * heads, axis=0)
        query = jnp.where(own_head, query, jnp.zeros_like(query))
        scores = lax.dot_general(
            query, k_ref[mine, :], (((1,), (1,)), ((), ())), preferred_element_type=jnp.float32
        )
        scores = jnp.where(causal, scores, -1e30)
        peak = jnp.max(scores, axis=1, keepdims=True)
        weights = jnp.exp2((scores - peak) * factor)
        total = jnp.sum(weights, axis=1, keepdims=True)
        mixed = jnp.dot(
            weights.astype(jnp.bfloat16), v_ref[mine, :], preferred_element_type=jnp.float32
        )
        length = lengths[r]

        def step(n, carry):
            peak, total, mixed = carry
            for p in range(CHUNK_PAGES):
                for copy in copies(r, n * CHUNK_PAGES + p):
                    copy.wait()
            here = pl.ds(r * maxp + n * CHUNK_PAGES, CHUNK_PAGES)
            keys = kbuf[here].reshape(span, width)
            values = vbuf[here].reshape(span, width)
            scores = lax.dot_general(
                query, keys, (((1,), (1,)), ((), ())), preferred_element_type=jnp.float32
            )
            scores = jnp.where(column < length - n * span, scores, -1e30)
            higher = jnp.maximum(peak, jnp.max(scores, axis=1, keepdims=True))
            shrink = jnp.exp2((peak - higher) * factor)
            weights = jnp.exp2((scores - higher) * factor)
            total = total * shrink + jnp.sum(weights, axis=1, keepdims=True)
            mixed = mixed * shrink + jnp.dot(
                weights.astype(jnp.bfloat16), values, preferred_element_type=jnp.float32
            )
            return higher, total, mixed

        peak, total, mixed = lax.fori_loop(0, chunks_of(r), step, (peak, total, mixed))
        mixed = jnp.where(own_head, mixed / total, 0.0)
        summed = mixed[:fresh]
        for h in range(1, heads):
            summed = summed + mixed[h * fresh : (h + 1) * fresh]
        out_ref[mine, :] = summed.astype(out_ref.dtype)


def attention(lengths, table, q, k, v, key_pool, value_pool):
    rows, width = q.shape
    page = key_pool.shape[1]
    slots = table.shape[0] * table.shape[1]
    out = jax.ShapeDtypeStruct((rows, width), jnp.bfloat16)
    vmem = pl.BlockSpec(memory_space=pltpu.VMEM)
    smem = pl.BlockSpec(memory_space=pltpu.SMEM)
    anywhere = pl.BlockSpec(memory_space=pl.ANY)
    return pl.pallas_call(
        attention_kernel,
        out_shape=(out, out, out),
        in_specs=[smem, smem, vmem, vmem, vmem, anywhere, anywhere],
        out_specs=(vmem, vmem, vmem),
        scratch_shapes=[
            pltpu.VMEM((slots, page, width), jnp.bfloat16),
            pltpu.VMEM((slots, page, width), jnp.bfloat16),
            pltpu.SemaphoreType.DMA((2, slots)),
        ],
        compiler_params=pltpu.CompilerParams(vmem_limit_bytes=40 << 20),
    )(lengths, table, q, k, v, key_pool, value_pool)


def per_device(
    arrivals, group_of, lengths, page_table, ln_gain, ln_bias, w_qkv, qkv_bias, key_pool, value_pool
):
    req_count, fresh, part = arrivals.shape
    model_width = ln_gain.shape[0]
    local_cols = w_qkv.shape[1]
    local_heads = local_cols // (3 * HEAD)
    everyone = group_of.shape[0]
    devices = everyone // req_count
    groups = devices // 2
    half = part // 2
    each = fresh // groups
    order = jnp.argsort(group_of, stable=True).astype(jnp.int32)

    pieces = arrivals.reshape(req_count, each, groups, 2, half).transpose(2, 3, 0, 1, 4)
    pieces = pieces.reshape(devices, req_count, each * half)
    pieces = lax.all_to_all(pieces, "req", 0, 0, tiled=True)
    pieces = pieces.reshape(everyone, each * half)[order].reshape(devices, req_count, each * half)
    pieces = lax.all_to_all(pieces, "req", 0, 0, tiled=True)
    pieces = pieces.reshape(groups, 2, req_count, each, half).transpose(2, 3, 0, 1, 4)
    tokens = pieces.reshape(req_count * fresh, part)

    gathered = lax.all_gather(tokens, "wgt", axis=1, tiled=True)
    widened = gathered.astype(jnp.float32)
    center = jnp.mean(widened, axis=-1, keepdims=True)
    spread = jnp.mean(jnp.square(widened - center), axis=-1, keepdims=True)
    normed = (widened - center) * lax.rsqrt(spread + EPS) * ln_gain.astype(
        jnp.float32
    ) + ln_bias.astype(jnp.float32)
    summed = jnp.dot(
        normed.astype(jnp.bfloat16),
        lax.all_gather(w_qkv, "req", axis=0, tiled=True),
        preferred_element_type=jnp.float32,
    )
    summed = summed + qkv_bias.astype(jnp.float32)
    projected = summed.reshape(req_count, fresh, local_heads, 3, HEAD)
    positions = (
        lengths[:, None] + jnp.arange(fresh, dtype=jnp.int32)[None, :]
    ).astype(jnp.float32)
    flat = (req_count * fresh, local_heads * HEAD)
    q = rotary(projected[:, :, :, 0], positions).astype(jnp.bfloat16).reshape(flat)
    k = rotary(projected[:, :, :, 1], positions).astype(jnp.bfloat16).reshape(flat)
    v = projected[:, :, :, 2].astype(jnp.bfloat16).reshape(flat)
    outs = attention(lengths, page_table, q, k, v, key_pool, value_pool)
    return tuple(a.reshape(req_count, fresh, local_heads * HEAD) for a in outs)


def solution(mesh):
    in_specs = (
        P("req", None, "wgt"),
        P(),
        P("req"),
        P("req", None),
        P(),
        P(),
        P("req", "wgt"),
        P("wgt"),
        P("req", None, "wgt"),
        P("req", None, "wgt"),
    )
    out_specs = (P("req", None, "wgt"), P("req", None, "wgt"), P("req", None, "wgt"))
    return jax.shard_map(
        per_device, mesh=mesh, in_specs=in_specs, out_specs=out_specs, check_vma=False
    )
```

```python
import math

import jax
import jax.numpy as jnp
from jax import lax
from jax.experimental import pallas as pl
from jax.experimental.pallas import tpu as pltpu
from jax.sharding import PartitionSpec as P
import numpy as np

HEAD = 96
ROT = 24
EPS = 1e-05
CHUNK_PAGES = 4


def attention_kernel(
    lengths, table, q_ref, k_ref, v_ref, key_pool, value_pool, out_ref, nk_ref, nv_ref, kbuf, vbuf, sems
):
    req_count, maxp = table.shape
    page, width = kbuf.shape[1], kbuf.shape[2]
    fresh = q_ref.shape[0] // req_count
    heads = width // HEAD
    rows = heads * fresh
    span = CHUNK_PAGES * page
    factor = math.log2(math.e) / math.sqrt(HEAD)

    def chunks_of(r):
        return (lengths[r] + (span - 1)) // span

    def copies(r, p):
        slot = r * maxp + p
        number = table[r, p]
        return (
            pltpu.make_async_copy(key_pool.at[number], kbuf.at[slot], sems.at[0, slot]),
            pltpu.make_async_copy(value_pool.at[number], vbuf.at[slot], sems.at[1, slot]),
        )

    for r in range(req_count):

        @pl.loop(0, chunks_of(r) * CHUNK_PAGES)
        def _(p):
            for copy in copies(r, p):
                copy.start()

    nk_ref[...] = k_ref[...]
    nv_ref[...] = v_ref[...]

    lane_head = lax.broadcasted_iota(jnp.int32, (rows, width), 1) // HEAD
    row_head = lax.broadcasted_iota(jnp.int32, (rows, width), 0) // fresh
    own_head = lane_head == row_head
    row_token = lax.broadcasted_iota(jnp.int32, (rows, fresh), 0) % fresh
    causal = row_token >= lax.broadcasted_iota(jnp.int32, (rows, fresh), 1)
    column = lax.broadcasted_iota(jnp.int32, (rows, span), 1)

    for r in range(req_count):
        mine = pl.ds(r * fresh, fresh)
        query = jnp.concatenate([q_ref[mine, :]] * heads, axis=0)
        query = jnp.where(own_head, query, jnp.zeros_like(query))
        scores = lax.dot_general(
            query, k_ref[mine, :], (((1,), (1,)), ((), ())), preferred_element_type=jnp.float32
        )
        scores = jnp.where(causal, scores, -1e30)
        peak = jnp.max(scores, axis=1, keepdims=True)
        weights = jnp.exp2((scores - peak) * factor)
        total = jnp.sum(weights, axis=1, keepdims=True)
        mixed = jnp.dot(
            weights.astype(jnp.bfloat16), v_ref[mine, :], preferred_element_type=jnp.float32
        )
        length = lengths[r]

        def step(n, carry):
            peak, total, mixed = carry
            for p in range(CHUNK_PAGES):
                for copy in copies(r, n * CHUNK_PAGES + p):
                    copy.wait()
            here = pl.ds(r * maxp + n * CHUNK_PAGES, CHUNK_PAGES)
            keys = kbuf[here].reshape(span, width)
            values = vbuf[here].reshape(span, width)
            scores = lax.dot_general(
                query, keys, (((1,), (1,)), ((), ())), preferred_element_type=jnp.float32
            )
            scores = jnp.where(column < length - n * span, scores, -1e30)
            higher = jnp.maximum(peak, jnp.max(scores, axis=1, keepdims=True))
            shrink = jnp.exp2((peak - higher) * factor)
            weights = jnp.exp2((scores - higher) * factor)
            total = total * shrink + jnp.sum(weights, axis=1, keepdims=True)
            mixed = mixed * shrink + jnp.dot(
                weights.astype(jnp.bfloat16), values, preferred_element_type=jnp.float32
            )
            return higher, total, mixed

        peak, total, mixed = lax.fori_loop(0, chunks_of(r), step, (peak, total, mixed))
        mixed = jnp.where(own_head, mixed / total, 0.0)
        summed = mixed[:fresh]
        for h in range(1, heads):
            summed = summed + mixed[h * fresh : (h + 1) * fresh]
        out_ref[mine, :] = summed.astype(out_ref.dtype)


def attention(lengths, table, q, k, v, key_pool, value_pool):
    rows, width = q.shape
    page = key_pool.shape[1]
    slots = table.shape[0] * table.shape[1]
    out = jax.ShapeDtypeStruct((rows, width), jnp.bfloat16)
    vmem = pl.BlockSpec(memory_space=pltpu.VMEM)
    smem = pl.BlockSpec(memory_space=pltpu.SMEM)
    anywhere = pl.BlockSpec(memory_space=pltpu.HBM)
    return pl.pallas_call(
        attention_kernel,
        out_shape=(out, out, out),
        in_specs=[smem, smem, vmem, vmem, vmem, anywhere, anywhere],
        out_specs=(vmem, vmem, vmem),
        scratch_shapes=[
            pltpu.VMEM((slots, page, width), jnp.bfloat16),
            pltpu.VMEM((slots, page, width), jnp.bfloat16),
            pltpu.SemaphoreType.DMA((2, slots)),
        ],
        compiler_params=pltpu.CompilerParams(vmem_limit_bytes=40 << 20),
    )(lengths, table, q, k, v, key_pool, value_pool)


MESH = pl.DeviceIdType.MESH
SIDE = 4
CHIPS = SIDE * SIDE
DEPTH = 8
OFFSETS = (0, -1, 1, 2)


def copy_numbers():
    names = []
    for h in (0, 1):
        names += [("own", h, s) for s in (1, -1)]
        names += [("own on", h, s) for s in (1, -1)]
        names += [("row", h, du, s) for du in OFFSETS for s in (1, -1)]
        names += [("row on", h, du, s) for du in OFFSETS for s in (1, -1)]
        names += [("core", h, du, dv) for du in OFFSETS for dv in OFFSETS]
    names += [("z", k, s) for k in (1, 2, 3, 4) for s in (1, -1)]
    names.append(("swap",))
    return {name: number for number, name in enumerate(names)}


NUMBER = copy_numbers()


def project_kernel(
    lengths, x_ref, w_ref, group_ref, gain_ref, bias_ref, col_bias_ref, q_ref, k_ref, v_ref,
    weights, slabs, normed, acc, cosines, sines, means, squares, out1, in1, swapped, out2, in2,
    send, recv, send1, recv1, send2, recv2,
):
    f32, bf16, i32 = jnp.float32, jnp.bfloat16, jnp.int32
    tokens, part = x_ref.shape
    depth, cols = w_ref.shape
    req_count = lengths.shape[0]
    fresh = tokens // req_count
    half = part // 2
    each = fresh // CHIPS
    width = cols // 3
    rows_half, rows_sub = depth // 2, depth // 4
    me, z = lax.axis_index("req"), lax.axis_index("wgt")
    core = me % 2
    chip = me // 2
    y, x = chip // SIDE, chip % SIDE
    iota = lambda shape, axis: lax.broadcasted_iota(i32, shape, axis)

    def device(number, c=core):
        return (number * 2 + c, z)

    partner = device(chip, 1 - core)

    barrier = pltpu.get_barrier_semaphore()

    @pl.loop(1, CHIPS)
    def _(d):
        pl.semaphore_signal(barrier, 1, device_id=device((chip + d) % CHIPS), device_id_type=MESH)

    pl.semaphore_signal(barrier, 1, device_id=partner, device_id_type=MESH)
    for s in (1, DEPTH - 1):
        pl.semaphore_signal(barrier, 1, device_id=(me, (z + s) % DEPTH), device_id_type=MESH)

    def by_kind(value):
        heads = range(width // HEAD)
        return jnp.concatenate(
            [
                value[:, (h * 3 + kind) * HEAD : (h * 3 + kind + 1) * HEAD]
                for kind in range(3)
                for h in heads
            ],
            axis=1,
        )

    def place(number, c):
        return number // 2, (number % 2) * (2 * depth) + c * depth

    own_pair, own_row = place(chip, core)
    weights[own_pair, pl.ds(pl.multiple_of(own_row, 64), depth), :] = by_kind(w_ref[...])

    m, n = iota((CHIPS * 8, tokens), 0), iota((CHIPS * 8, tokens), 1)
    for t in range(each):
        take = (m % 8) // 2 * fresh + t * CHIPS + m // 8 == n
        piece = jnp.zeros((CHIPS * 8, half), f32)
        for h in (0, 1):
            chosen = jnp.where(take & (m % 2 == h), 1.0, 0.0).astype(bf16)
            piece += jnp.dot(chosen, x_ref[:, h * half : (h + 1) * half], preferred_element_type=f32)
        out1[:, :, t * half : (t + 1) * half] = piece.reshape(CHIPS, 8, half).astype(bf16)
    in1[chip] = out1[chip]

    pl.semaphore_wait(barrier, CHIPS - 1 + 3)

    def spread(source, target, send_sems, recv_sems):
        def copy(d):
            other = (chip + d) % CHIPS
            return pltpu.make_async_remote_copy(
                src_ref=source.at[other],
                dst_ref=target.at[chip],
                send_sem=send_sems.at[d],
                recv_sem=recv_sems.at[d],
                device_id=device(other),
                device_id_type=MESH,
            )

        return copy

    first, second = spread(out1, in1, send1, recv1), spread(out2, in2, send2, recv2)

    @pl.loop(1, CHIPS)
    def _(d):
        first(d).start()

    def remote(name, ref, target, dst=None):
        return pltpu.make_async_remote_copy(
            src_ref=ref,
            dst_ref=ref if dst is None else dst,
            send_sem=send.at[NUMBER[name]],
            recv_sem=recv.at[NUMBER[name]],
            device_id=target,
            device_id_type=MESH,
        )

    where = {0: (x, y), 1: (y, x)}

    def chip_at(h, du, dv):
        u, v = where[h]
        u, v = (u + du + SIDE) % SIDE, (v + dv + SIDE) % SIDE
        return v * SIDE + u if h == 0 else u * SIDE + v

    def block(h, du, dv, c=core, sub=None):
        pair, row = place(chip_at(h, du, dv), c)
        row = row + h * rows_half + (0 if sub in (None, 1) else rows_sub)
        return weights.at[pair, pl.ds(pl.multiple_of(row, 16), rows_half if sub is None else rows_sub), :]

    def weight_copy(name):
        kind, h = name[0], name[1]
        if kind == "own":
            return remote(name, block(h, 0, 0), device(chip_at(h, name[2], 0)))
        if kind == "own on":
            s = name[2]
            return remote(name, block(h, -s, 0, sub=s), device(chip_at(h, s, 0)))
        if kind == "row":
            du, s = name[2], name[3]
            return remote(name, block(h, du, 0), device(chip_at(h, 0, s)))
        if kind == "row on":
            du, s = name[2], name[3]
            return remote(name, block(h, du, -s, sub=s), device(chip_at(h, 0, s)))
        du, dv = name[2], name[3]
        return remote(name, block(h, du, dv), partner)

    started = []

    def start(*name):
        weight_copy(name).start()
        started.append(name)

    def arrive(*name):
        weight_copy(name).wait_recv()

    for h in (0, 1):
        for s in (1, -1):
            start("own", h, s)
    for h in (0, 1):
        start("core", h, 0, 0)

    a, b = iota((CHIPS * 8, CHIPS * 8), 0), iota((CHIPS * 8, CHIPS * 8), 1)
    group_row = jnp.broadcast_to(group_ref[...], a.shape)
    group_col = jnp.sum(jnp.where(a == b, group_row, 0), axis=1, keepdims=True)
    rank = jnp.sum(jnp.where((group_col == group_row) & (a < b), 1, 0), axis=0, keepdims=True)
    slot_row = group_ref[...] * req_count + rank
    slot_col = jnp.sum(jnp.where(a == b, jnp.broadcast_to(slot_row, a.shape), 0), axis=1, keepdims=True)

    def selector(c):
        arriving = (b // 8 * 2 + c) * req_count + b % 8 // 2
        slot = jnp.sum(jnp.where(a == arriving, slot_col, 0), axis=0, keepdims=True)
        wanted = (a // 8 * 2 + core) * req_count + a % 8 // 2
        return jnp.where((wanted == slot) & (a % 2 == b % 2), 1.0, 0.0).astype(bf16)

    pick_own, pick_other = selector(core), selector(1 - core)

    @pl.loop(1, CHIPS)
    def _(d):
        first(d).wait_recv()

    swap = remote(("swap",), in1, partner, swapped)
    swap.start()

    def flat(ref):
        return ref[...].astype(f32).reshape(CHIPS * 8, each * half).astype(bf16)

    mixed = jnp.dot(pick_own, flat(in1), preferred_element_type=f32)
    swap.wait_recv()
    mixed = mixed + jnp.dot(pick_other, flat(swapped), preferred_element_type=f32)
    out2[...] = mixed.reshape(CHIPS, 8, each * half).astype(bf16)
    in2[chip] = out2[chip]

    @pl.loop(1, CHIPS)
    def _(d):
        second(d).start()

    for h in (0, 1):
        for s in (1, -1):
            start("row", h, 0, s)

    lane = iota((1, width), 1) % HEAD
    inverse = jnp.zeros((1, width), f32)
    for i in range(ROT // 2):
        value = float(np.float32(10000.0) ** np.float32(-2.0 * i / ROT))
        inverse = jnp.where((lane == i) | (lane == i + ROT // 2), value, inverse)
    for r in range(req_count):
        mine = pl.ds(r * fresh, fresh)
        position = (iota((fresh, 1), 0) + lengths[r]).astype(f32)
        angle = position * inverse
        cosines[mine, :] = jnp.cos(angle)
        sines[mine, :] = jnp.where(lane < ROT // 2, -jnp.sin(angle), jnp.sin(angle))

    for h in (0, 1):
        for s in (1, -1):
            arrive("own", h, s)
            start("own on", h, s)
            start("row", h, -s, 1)
            start("row", h, -s, -1)
            start("core", h, -s, 0)

    @pl.loop(1, CHIPS)
    def _(d):
        second(d).wait_recv()

    m, n = iota((req_count * CHIPS, CHIPS * 8), 0), iota((req_count * CHIPS, CHIPS * 8), 1)
    pieces = flat(in2)
    for h in (0, 1):
        chosen = jnp.where(m % CHIPS * 8 + m // CHIPS * 2 + h == n, 1.0, 0.0).astype(bf16)
        for t in range(each):
            rows = jnp.dot(chosen, pieces[:, t * half : (t + 1) * half], preferred_element_type=f32)
            for r in range(req_count):
                slabs[z, pl.ds(r * fresh + t * CHIPS, CHIPS), h * half : (h + 1) * half] = rows[
                    r * CHIPS : (r + 1) * CHIPS
                ].astype(bf16)

    def slab(k, s):
        ref = slabs.at[(z - k * s + DEPTH) % DEPTH]
        if k < 4:
            return ref
        return ref.at[pl.ds(0 if s == 1 else tokens // 2, tokens // 2), :]

    def z_copy(k, s):
        ref = slab(k - 1, s)
        if k == 4:
            ref = ref.at[pl.ds(0 if s == 1 else tokens // 2, tokens // 2), :]
        return remote(("z", k, s), ref, (me, (z + s + DEPTH) % DEPTH))

    block_rows = 32

    def gather_stats(number):
        @pl.loop(0, tokens, step=block_rows)
        def _(row):
            mine = pl.ds(pl.multiple_of(row, block_rows), block_rows)
            value = slabs[number, mine, :].astype(f32)
            mean = jnp.sum(value, axis=1, keepdims=True) * (1.0 / part)
            rest = value - mean
            means[number, mine, :] = mean
            squares[number, mine, :] = jnp.sum(rest * rest, axis=1, keepdims=True)

    def z_step(k):
        for s in (1, -1):
            z_copy(k, s).wait_recv()
            if k < 4:
                z_copy(k + 1, s).start()
        if k < 4:
            gather_stats((z - k + DEPTH) % DEPTH)
            gather_stats((z + k) % DEPTH)
        else:
            gather_stats((z + k) % DEPTH)

    def rows_step(du):
        for h in (0, 1):
            for s in (1, -1):
                arrive("row", h, du, s)
                start("row on", h, du, s)
                start("core", h, du, -s)

    for s in (1, -1):
        z_copy(1, s).start()
    gather_stats(z)

    for h in (0, 1):
        for s in (1, -1):
            arrive("own on", h, s)
        start("row", h, 2, 1)
        start("row", h, 2, -1)
        start("core", h, 2, 0)

    rows_step(0)
    z_step(1)
    rows_step(-1)
    z_step(2)
    rows_step(1)
    z_step(3)
    rows_step(2)
    z_step(4)

    @pl.loop(0, tokens, step=block_rows)
    def _(row):
        mine = pl.ds(pl.multiple_of(row, block_rows), block_rows)
        mean = means[0, mine, :]
        for w in range(1, DEPTH):
            mean = mean + means[w, mine, :]
        mean = mean * (1.0 / DEPTH)
        spread_sum = jnp.zeros_like(mean)
        for w in range(DEPTH):
            apart = means[w, mine, :] - mean
            spread_sum = spread_sum + (squares[w, mine, :] + part * (apart * apart))
        inv = lax.rsqrt(spread_sum * (1.0 / (part * DEPTH)) + EPS)
        for w in range(DEPTH):
            here = slice(w * part, (w + 1) * part)
            value = (slabs[w, mine, :].astype(f32) - mean) * inv
            value = value * gain_ref[:, here].astype(f32) + bias_ref[:, here].astype(f32)
            normed[w, mine, :] = value.astype(bf16)

    acc[...] = jnp.broadcast_to(by_kind(col_bias_ref[...].astype(f32)), acc.shape)

    def far(h, du):
        for s in (1, -1):
            arrive("row on", h, du, s)
        start("core", h, du, 2)

    def from_core(h, du, dv):
        remote(("core", h, du, dv), block(h, du, dv, c=1 - core), partner).wait_recv()

    for dy in OFFSETS:
        far(1, dy)
        if dy == 2:
            for dx in OFFSETS:
                far(0, dx)
        for dx in OFFSETS:
            from_core(0, dx, dy)
            from_core(1, dy, dx)
        first_pair = (y + dy + SIDE) % SIDE * 2

        @pl.loop(first_pair, first_pair + 2)
        def _(pair):
            acc[...] += jnp.dot(normed[pair], weights[pair], preferred_element_type=f32)

    def turn(value):
        near = jnp.where(lane < ROT // 2, pltpu.roll(value, width - ROT // 2, 1), pltpu.roll(value, ROT // 2, 1))
        return value * cosines[...] + near * sines[...]

    q_ref[...] = turn(acc[:, :width]).astype(bf16)
    k_ref[...] = turn(acc[:, width : 2 * width]).astype(bf16)
    v_ref[...] = acc[:, 2 * width :].astype(bf16)

    for name in started:
        weight_copy(name).wait_send()
    for k in (1, 2, 3, 4):
        for s in (1, -1):
            z_copy(k, s).wait_send()
    swap.wait_send()

    @pl.loop(1, CHIPS)
    def _(d):
        first(d).wait_send()
        second(d).wait_send()


def project(lengths, x, w, group_of, gain, bias, col_bias):
    tokens, part = x.shape
    depth, cols = w.shape
    width = cols // 3
    lanes = tokens * part // (CHIPS * 8)
    out = jax.ShapeDtypeStruct((tokens, width), jnp.bfloat16)
    vmem = pl.BlockSpec(memory_space=pltpu.VMEM)
    message = pltpu.VMEM((CHIPS, 8, lanes), jnp.bfloat16)
    pairs = pltpu.SemaphoreType.DMA((CHIPS,))
    copies = pltpu.SemaphoreType.DMA((len(NUMBER),))
    return pl.pallas_call(
        project_kernel,
        out_shape=(out, out, out),
        in_specs=[pl.BlockSpec(memory_space=pltpu.SMEM)] + [vmem] * 6,
        out_specs=(vmem, vmem, vmem),
        scratch_shapes=[
            pltpu.VMEM((CHIPS // 2, 4 * depth, cols), jnp.bfloat16),
            pltpu.VMEM((DEPTH, tokens, part), jnp.bfloat16),
            pltpu.VMEM((DEPTH, tokens, part), jnp.bfloat16),
            pltpu.VMEM((tokens, cols), jnp.float32),
            pltpu.VMEM((tokens, width), jnp.float32),
            pltpu.VMEM((tokens, width), jnp.float32),
            pltpu.VMEM((DEPTH, tokens, 1), jnp.float32),
            pltpu.VMEM((DEPTH, tokens, 1), jnp.float32),
            message,
            message,
            message,
            message,
            message,
            copies,
            copies,
            pairs,
            pairs,
            pairs,
            pairs,
        ],
        compiler_params=pltpu.CompilerParams(
            collective_id=0, has_side_effects=True, vmem_limit_bytes=48 << 20
        ),
    )(lengths, x, w, group_of, gain, bias, col_bias)


def per_device(
    arrivals, group_of, lengths, page_table, ln_gain, ln_bias, w_qkv, qkv_bias, key_pool, value_pool
):
    req_count, fresh, part = arrivals.shape
    q, k, v = project(
        lengths,
        arrivals.reshape(req_count * fresh, part),
        w_qkv,
        group_of.reshape(1, -1),
        ln_gain.reshape(1, -1),
        ln_bias.reshape(1, -1),
        qkv_bias.reshape(1, -1),
    )
    outs = attention(lengths, page_table, q, k, v, key_pool, value_pool)
    return tuple(a.reshape(req_count, fresh, -1) for a in outs)


def solution(mesh):
    in_specs = (
        P("req", None, "wgt"),
        P(),
        P("req"),
        P("req", None),
        P(),
        P(),
        P("req", "wgt"),
        P("wgt"),
        P("req", None, "wgt"),
        P("req", None, "wgt"),
    )
    out_specs = (P("req", None, "wgt"), P("req", None, "wgt"), P("req", None, "wgt"))
    return jax.shard_map(
        per_device, mesh=mesh, in_specs=in_specs, out_specs=out_specs, check_vma=False
    )
```

```python
import math

import jax
import jax.numpy as jnp
from jax import lax
from jax.experimental import pallas as pl
from jax.experimental.pallas import tpu as pltpu
from jax.sharding import PartitionSpec as P
import numpy as np

HEAD = 96
ROT = 24
EPS = 1e-05
CHUNK_PAGES = 4
VMEM_BYTES = 67043328


def attention_kernel(
    lengths, table, q_ref, k_ref, v_ref, key_pool, value_pool, out_ref, nk_ref, nv_ref,
    kbuf, vbuf, scores, mixed, sems,
):
    f32, bf16 = jnp.float32, jnp.bfloat16
    req_count, maxp = table.shape
    page, width = kbuf.shape[1], kbuf.shape[2]
    fresh = q_ref.shape[0] // req_count
    heads = width // HEAD
    rows = heads * fresh
    span = CHUNK_PAGES * page
    factor = math.log2(math.e) / math.sqrt(HEAD)
    low = -1e30

    def chunks_of(r):
        return (lengths[r] + (span - 1)) // span

    def key_copy(r, p):
        slot = r * maxp + p
        return pltpu.make_async_copy(key_pool.at[table[r, p]], kbuf.at[slot], sems.at[0, slot])

    def value_copy(r, p):
        slot = r * maxp + p
        return pltpu.make_async_copy(value_pool.at[table[r, p]], vbuf.at[slot], sems.at[1, slot])

    for r in range(req_count):

        @pl.loop(0, chunks_of(r) * CHUNK_PAGES)
        def _(p):
            key_copy(r, p).start()
            value_copy(r, p).start()

    nk_ref[...] = k_ref[...]
    nv_ref[...] = v_ref[...]

    iota = lambda shape, axis: lax.broadcasted_iota(jnp.int32, shape, axis)
    own_head = iota((rows, width), 1) // HEAD == iota((rows, width), 0) // fresh
    causal = iota((rows, fresh), 0) % fresh >= iota((rows, fresh), 1)
    column = iota((1, span), 1)

    def fold(value, op):
        folded = value[:, :128]
        for n in range(1, value.shape[1] // 128):
            folded = op(folded, value[:, n * 128 : (n + 1) * 128])
        return folded

    across = (((1,), (1,)), ((), ()))
    queries, fresh_scores, fresh_peaks = [], [], []
    for r in range(req_count):
        mine = pl.ds(r * fresh, fresh)
        query = jnp.concatenate([q_ref[mine, :]] * heads, axis=0)
        query = jnp.where(own_head, query, jnp.zeros_like(query))
        own = lax.dot_general(query, k_ref[mine, :], across, preferred_element_type=f32)
        own = jnp.where(causal, own, low)
        queries.append(query)
        fresh_scores.append(own)
        fresh_peaks.append(jnp.max(own, axis=1, keepdims=True))

    for r in range(req_count):
        mine = pl.ds(r * fresh, fresh)
        query, length = queries[r], lengths[r]

        def first(n, peak):
            for p in range(CHUNK_PAGES):
                key_copy(r, n * CHUNK_PAGES + p).wait()
            keys = kbuf[pl.ds(r * maxp + n * CHUNK_PAGES, CHUNK_PAGES)].reshape(span, width)
            value = lax.dot_general(query, keys, across, preferred_element_type=f32)
            value = value + jnp.where(column < length - n * span, 0.0, low)
            scores[n] = value
            return jnp.maximum(peak, fold(value, jnp.maximum))

        peak = lax.fori_loop(0, chunks_of(r), first, jnp.full((rows, 128), low, f32))
        peak = jnp.maximum(jnp.max(peak, axis=1, keepdims=True), fresh_peaks[r])
        offset = peak * factor
        weights = jnp.exp2(fresh_scores[r] * factor - offset)
        mixed[...] = jnp.dot(weights.astype(bf16), v_ref[mine, :], preferred_element_type=f32)
        fresh_total = jnp.sum(weights, axis=1, keepdims=True)

        def second(n, total):
            for p in range(CHUNK_PAGES):
                value_copy(r, n * CHUNK_PAGES + p).wait()
            values = vbuf[pl.ds(r * maxp + n * CHUNK_PAGES, CHUNK_PAGES)].reshape(span, width)
            weights = jnp.exp2(scores[n] * factor - offset)
            mixed[...] += jnp.dot(weights.astype(bf16), values, preferred_element_type=f32)
            return total + fold(weights, jnp.add)

        total = lax.fori_loop(0, chunks_of(r), second, jnp.zeros((rows, 128), f32))
        total = jnp.sum(total, axis=1, keepdims=True) + fresh_total
        part = jnp.where(own_head, mixed[...] * (1.0 / total), 0.0)
        summed = part[:fresh]
        for h in range(1, heads):
            summed = summed + part[h * fresh : (h + 1) * fresh]
        out_ref[mine, :] = summed.astype(out_ref.dtype)


def attention(lengths, table, q, k, v, key_pool, value_pool):
    rows, width = q.shape
    page = key_pool.shape[1]
    req_count, maxp = table.shape
    slots = req_count * maxp
    wide = width // HEAD * (rows // req_count)
    out = jax.ShapeDtypeStruct((rows, width), jnp.bfloat16)
    vmem = pl.BlockSpec(memory_space=pltpu.VMEM)
    smem = pl.BlockSpec(memory_space=pltpu.SMEM)
    anywhere = pl.BlockSpec(memory_space=pl.ANY)
    return pl.pallas_call(
        attention_kernel,
        out_shape=(out, out, out),
        in_specs=[smem, smem, vmem, vmem, vmem, anywhere, anywhere],
        out_specs=(vmem, vmem, vmem),
        scratch_shapes=[
            pltpu.VMEM((slots, page, width), jnp.bfloat16),
            pltpu.VMEM((slots, page, width), jnp.bfloat16),
            pltpu.VMEM((maxp // CHUNK_PAGES, wide, CHUNK_PAGES * page), jnp.float32),
            pltpu.VMEM((wide, width), jnp.float32),
            pltpu.SemaphoreType.DMA((2, slots)),
        ],
        compiler_params=pltpu.CompilerParams(vmem_limit_bytes=VMEM_BYTES),
    )(lengths, table, q, k, v, key_pool, value_pool)


MESH = pl.DeviceIdType.MESH
SIDE = 4
CHIPS = SIDE * SIDE
DEPTH = 8
OFFSETS = (0, -1, 1, 2)
THIRDS = 3


def last_parts(s):
    return ((0, None), (1, 0)) if s == 1 else ((2, None), (1, 1))


def copy_numbers():
    names = []
    for h in (0, 1):
        names += [("own", h, s) for s in (1, -1)]
        names += [("own on", h, s) for s in (1, -1)]
        names += [("row", h, du, s) for du in OFFSETS for s in (1, -1)]
        names += [("row on", h, du, s) for du in OFFSETS for s in (1, -1)]
        names += [("core", h, du, dv) for du in OFFSETS for dv in OFFSETS]
    for s in (1, -1):
        names += [("z", k, s, t) for k in (1, 2, 3) for t in range(THIRDS)]
        names += [("z", 4, s, t) for t, _ in last_parts(s)]
    names.append(("swap",))
    return {name: number for number, name in enumerate(names)}


NUMBER = copy_numbers()


def project_kernel(
    lengths, x_hbm, w_hbm, group_ref, gain_ref, bias_ref, col_bias_ref, q_ref, k_ref, v_ref,
    x_ref, w_ref, weights, slabs, normed, acc, cosines, sines, pivot, sums, squares, gains, biases,
    out1, in1, swapped, out2, in2, load, send, recv, send1, recv1, send2, recv2,
):
    f32, bf16, i32 = jnp.float32, jnp.bfloat16, jnp.int32
    tokens, part = x_ref.shape
    depth, cols = w_ref.shape
    model_width = part * DEPTH
    req_count = lengths.shape[0]
    fresh = tokens // req_count
    half = part // 2
    third = tokens // THIRDS
    width = cols // 3
    rows_half, rows_sub = depth // 2, depth // 4
    me, z = lax.axis_index("req"), lax.axis_index("wgt")
    core = me % 2
    chip = me // 2
    y, x = chip // SIDE, chip % SIDE
    iota = lambda shape, axis: lax.broadcasted_iota(i32, shape, axis)

    def device(number, c=core):
        return (number * 2 + c, z)

    partner = device(chip, 1 - core)

    load_x = pltpu.make_async_copy(x_hbm, x_ref, load.at[0])
    load_w = pltpu.make_async_copy(w_hbm, w_ref, load.at[1])
    load_x.start()
    load_w.start()

    barrier = pltpu.get_barrier_semaphore()

    @pl.loop(1, CHIPS)
    def _(d):
        pl.semaphore_signal(barrier, 1, device_id=device((chip + d) % CHIPS), device_id_type=MESH)

    pl.semaphore_signal(barrier, 1, device_id=partner, device_id_type=MESH)
    for s in (1, DEPTH - 1):
        pl.semaphore_signal(barrier, 1, device_id=(me, (z + s) % DEPTH), device_id_type=MESH)

    load_x.wait()
    m, n = iota((CHIPS * 8, tokens), 0), iota((CHIPS * 8, tokens), 1)
    for t in range(THIRDS):
        take = (m % 8) // 2 * fresh + t * CHIPS + m // 8 == n
        piece = jnp.zeros((CHIPS * 8, half), f32)
        for h in (0, 1):
            chosen = jnp.where(take & (m % 2 == h), 1.0, 0.0).astype(bf16)
            piece += jnp.dot(chosen, x_ref[:, h * half : (h + 1) * half], preferred_element_type=f32)
        out1[:, :, t * half : (t + 1) * half] = piece.reshape(CHIPS, 8, half).astype(bf16)
    in1[chip] = out1[chip]

    pl.semaphore_wait(barrier, CHIPS - 1 + 3)

    def spread(source, target, send_sems, recv_sems):
        def copy(d):
            other = (chip + d) % CHIPS
            return pltpu.make_async_remote_copy(
                src_ref=source.at[other],
                dst_ref=target.at[chip],
                send_sem=send_sems.at[d],
                recv_sem=recv_sems.at[d],
                device_id=device(other),
                device_id_type=MESH,
            )

        return copy

    first, second = spread(out1, in1, send1, recv1), spread(out2, in2, send2, recv2)

    @pl.loop(1, CHIPS)
    def _(d):
        first(d).start()

    def by_kind(value):
        heads = range(width // HEAD)
        return jnp.concatenate(
            [
                value[:, (h * 3 + kind) * HEAD : (h * 3 + kind + 1) * HEAD]
                for kind in range(3)
                for h in heads
            ],
            axis=1,
        )

    def place(number, c):
        return number // 2, (number % 2) * (2 * depth) + c * depth

    load_w.wait()
    own_pair, own_row = place(chip, core)
    weights[own_pair, pl.ds(pl.multiple_of(own_row, 64), depth), :] = by_kind(w_ref[...])

    def remote(name, ref, target, dst=None):
        return pltpu.make_async_remote_copy(
            src_ref=ref,
            dst_ref=ref if dst is None else dst,
            send_sem=send.at[NUMBER[name]],
            recv_sem=recv.at[NUMBER[name]],
            device_id=target,
            device_id_type=MESH,
        )

    where = {0: (x, y), 1: (y, x)}

    def chip_at(h, du, dv):
        u, v = where[h]
        u, v = (u + du + SIDE) % SIDE, (v + dv + SIDE) % SIDE
        return v * SIDE + u if h == 0 else u * SIDE + v

    def block(h, du, dv, c=core, sub=None):
        pair, row = place(chip_at(h, du, dv), c)
        row = row + h * rows_half + (0 if sub in (None, 1) else rows_sub)
        return weights.at[pair, pl.ds(pl.multiple_of(row, 16), rows_half if sub is None else rows_sub), :]

    def weight_copy(name):
        kind, h = name[0], name[1]
        if kind == "own":
            return remote(name, block(h, 0, 0), device(chip_at(h, name[2], 0)))
        if kind == "own on":
            s = name[2]
            return remote(name, block(h, -s, 0, sub=s), device(chip_at(h, s, 0)))
        if kind == "row":
            du, s = name[2], name[3]
            return remote(name, block(h, du, 0), device(chip_at(h, 0, s)))
        if kind == "row on":
            du, s = name[2], name[3]
            return remote(name, block(h, du, -s, sub=s), device(chip_at(h, 0, s)))
        du, dv = name[2], name[3]
        return remote(name, block(h, du, dv), partner)

    started = []

    def start(*name):
        weight_copy(name).start()
        started.append(name)

    def arrive(*name):
        weight_copy(name).wait_recv()

    for h in (0, 1):
        for s in (1, -1):
            start("own", h, s)
    for h in (0, 1):
        start("core", h, 0, 0)

    a, b = iota((CHIPS * 8, CHIPS * 8), 0), iota((CHIPS * 8, CHIPS * 8), 1)
    groups = group_ref[...].reshape(1, -1)
    group_row = jnp.broadcast_to(groups, a.shape)
    group_col = jnp.sum(jnp.where(a == b, group_row, 0), axis=1, keepdims=True)
    rank = jnp.sum(jnp.where((group_col == group_row) & (a < b), 1, 0), axis=0, keepdims=True)
    slot_row = groups * req_count + rank
    slot_col = jnp.sum(jnp.where(a == b, jnp.broadcast_to(slot_row, a.shape), 0), axis=1, keepdims=True)

    def selector(c):
        arriving = (b // 8 * 2 + c) * req_count + b % 8 // 2
        slot = jnp.sum(jnp.where(a == arriving, slot_col, 0), axis=0, keepdims=True)
        wanted = (a // 8 * 2 + core) * req_count + a % 8 // 2
        return jnp.where((wanted == slot) & (a % 2 == b % 2), 1.0, 0.0).astype(bf16)

    pick_own, pick_other = selector(core), selector(1 - core)

    @pl.loop(1, CHIPS)
    def _(d):
        first(d).wait_recv()

    swap = remote(("swap",), in1, partner, swapped)
    swap.start()

    def flat(ref):
        return ref[...].astype(f32).reshape(CHIPS * 8, THIRDS * half).astype(bf16)

    mixed = jnp.dot(pick_own, flat(in1), preferred_element_type=f32)
    swap.wait_recv()
    mixed = mixed + jnp.dot(pick_other, flat(swapped), preferred_element_type=f32)
    out2[...] = mixed.reshape(CHIPS, 8, THIRDS * half).astype(bf16)
    in2[chip] = out2[chip]

    @pl.loop(1, CHIPS)
    def _(d):
        second(d).start()

    for h in (0, 1):
        for s in (1, -1):
            start("row", h, 0, s)

    gains[...] = jnp.broadcast_to(gain_ref[...].astype(f32).reshape(1, -1), gains.shape)
    biases[...] = jnp.broadcast_to(bias_ref[...].astype(f32).reshape(1, -1), biases.shape)
    acc[...] = jnp.broadcast_to(by_kind(col_bias_ref[...].astype(f32).reshape(1, -1)), acc.shape)

    lane = iota((1, 128), 1) % 32
    turning = ROT // 2
    inverse = jnp.zeros((1, 128), f32)
    for i in range(turning):
        value = float(np.float32(10000.0) ** np.float32(-2.0 * i / ROT))
        inverse = jnp.where((lane == i) | (lane == i + turning), value, inverse)
    row = iota((tokens, 1), 0)
    request = row % third // CHIPS
    position = row // third * CHIPS + row % CHIPS
    for r in range(req_count):
        position = position + jnp.where(request == r, lengths[r], 0)
    angle = position.astype(f32) * inverse
    cosines[...] = jnp.cos(angle)
    sine = jnp.sin(angle)
    sines[...] = jnp.where(lane < turning, -sine, sine)

    for h in (0, 1):
        for s in (1, -1):
            arrive("own", h, s)
            start("own on", h, s)
            start("row", h, -s, 1)
            start("row", h, -s, -1)
            start("core", h, -s, 0)

    @pl.loop(1, CHIPS)
    def _(d):
        second(d).wait_recv()

    m, n = iota((third, CHIPS * 8), 0), iota((third, CHIPS * 8), 1)
    pieces = flat(in2)
    for h in (0, 1):
        chosen = jnp.where(m % CHIPS * 8 + m // CHIPS * 2 + h == n, 1.0, 0.0).astype(bf16)
        rows = jnp.dot(chosen, pieces, preferred_element_type=f32).astype(bf16)
        for t in range(THIRDS):
            slabs[z, pl.ds(t * third, third), h * half : (h + 1) * half] = rows[:, t * half : (t + 1) * half]

    def slab(k, s, t, piece=None):
        ref = slabs.at[(z - k * s + DEPTH) % DEPTH]
        if piece is None:
            return ref.at[pl.ds(t * third, third), :]
        return ref.at[pl.ds(t * third + piece * (third // 2), third // 2), :]

    def z_copy(k, s, t):
        piece = dict(last_parts(s))[t] if k == 4 else None
        return remote(("z", k, s, t), slab(k - 1, s, t, piece), (me, (z + s + DEPTH) % DEPTH))

    for t in range(THIRDS):
        for s in (1, -1):
            z_copy(1, s, t).start()

    def folded(value):
        total = value[:, :128]
        for j in range(1, part // 128):
            total = total + value[:, j * 128 : (j + 1) * 128]
        return total

    for t in range(THIRDS):
        mine = pl.ds(t * third, third)
        own = jnp.sum(folded(slabs[z, mine, :].astype(f32)), axis=1, keepdims=True) * (1.0 / part)
        pivot[mine, :] = jnp.broadcast_to(own, (third, 128))
    sums[...] = jnp.zeros_like(sums)
    squares[...] = jnp.zeros_like(squares)

    def add_sums(number):
        @pl.loop(0, tokens, step=32)
        def _(start_row):
            mine = pl.ds(pl.multiple_of(start_row, 32), 32)
            origin, total, square = pivot[mine, :], sums[mine, :], squares[mine, :]
            for j in range(part // 128):
                apart = slabs[number, mine, j * 128 : (j + 1) * 128].astype(f32) - origin
                total = total + apart
                square = square + apart * apart
            sums[mine, :] = total
            squares[mine, :] = square

    def z_step(k):
        if k < 4:
            for t in range(THIRDS):
                for s in (1, -1):
                    z_copy(k, s, t).wait_recv()
                    if k < 3 or t in dict(last_parts(s)):
                        z_copy(k + 1, s, t).start()
            add_sums((z - k + DEPTH) % DEPTH)
            add_sums((z + k) % DEPTH)
        else:
            for s in (1, -1):
                for t, _ in last_parts(s):
                    z_copy(4, s, t).wait_recv()
            add_sums((z + 4) % DEPTH)

    def rows_step(du):
        for h in (0, 1):
            for s in (1, -1):
                arrive("row", h, du, s)
                start("row on", h, du, s)
                start("core", h, du, -s)

    for h in (0, 1):
        for s in (1, -1):
            arrive("own on", h, s)
        start("row", h, 2, 1)
        start("row", h, 2, -1)
        start("core", h, 2, 0)

    add_sums(z)
    z_step(1)
    rows_step(0)
    z_step(2)
    rows_step(-1)
    z_step(3)
    rows_step(1)
    z_step(4)

    def normalise(start_row):
        mine = pl.ds(pl.multiple_of(start_row, 32), 32)
        shift = jnp.sum(sums[mine, :], axis=1, keepdims=True) * (1.0 / model_width)
        square = jnp.sum(squares[mine, :], axis=1, keepdims=True) * (1.0 / model_width)
        inv = jnp.broadcast_to(lax.rsqrt(jnp.maximum(square - shift * shift, 0.0) + EPS), (32, 128))
        mean = pivot[mine, :] + shift
        for j in range(model_width // 128):
            w, lanes = j * 128 // part, slice(j * 128 % part, j * 128 % part + 128)
            value = (slabs[w, mine, lanes].astype(f32) - mean) * inv
            value = value.reshape(4, 8, 128) * gains[:, j * 128 : (j + 1) * 128][None]
            value = value + biases[:, j * 128 : (j + 1) * 128][None]
            normed[w, mine, lanes] = value.reshape(32, 128).astype(bf16)

    pl.loop(0, tokens, step=32)(normalise)

    rows_step(2)

    def far(h, du):
        for s in (1, -1):
            arrive("row on", h, du, s)
        start("core", h, du, 2)

    def from_core(h, du, dv):
        remote(("core", h, du, dv), block(h, du, dv, c=1 - core), partner).wait_recv()

    for dy in OFFSETS:
        far(1, dy)
        if dy == 2:
            for dx in OFFSETS:
                far(0, dx)
        for dx in OFFSETS:
            from_core(0, dx, dy)
            from_core(1, dy, dx)
        first_pair = (y + dy + SIDE) % SIDE * 2

        @pl.loop(first_pair, first_pair + 2)
        def _(pair):
            acc[...] += jnp.dot(normed[pair], weights[pair], preferred_element_type=f32)

    def turn(value):
        lanes = iota((1, width), 1) % HEAD
        forward, backward = pltpu.roll(value, width - turning, 1), pltpu.roll(value, turning, 1)
        near = jnp.where(lanes < turning, forward, backward)
        cosine = jnp.concatenate([cosines[...]] * (width // 128), axis=1)
        sine = jnp.concatenate([sines[...]] * (width // 128), axis=1)
        return jnp.where(lanes < ROT, value * cosine + near * sine, value)

    def put(ref, value):
        value = value.astype(bf16)
        for t in range(THIRDS):
            for r in range(req_count):
                row = t * third + r * CHIPS
                ref[pl.ds(r * fresh + t * CHIPS, CHIPS), :] = value[row : row + CHIPS]

    put(q_ref, turn(acc[:, :width]))
    put(k_ref, turn(acc[:, width : 2 * width]))
    put(v_ref, acc[:, 2 * width :])

    for name in started:
        weight_copy(name).wait_send()
    for s in (1, -1):
        for k in (1, 2, 3, 4):
            for t in range(THIRDS):
                if k < 4 or t in dict(last_parts(s)):
                    z_copy(k, s, t).wait_send()
    swap.wait_send()

    @pl.loop(1, CHIPS)
    def _(d):
        first(d).wait_send()
        second(d).wait_send()


def project(lengths, x, w, group_of, gain, bias, col_bias):
    tokens, part = x.shape
    depth, cols = w.shape
    width = cols // 3
    lanes = tokens * part // (CHIPS * 8)
    f32, bf16 = jnp.float32, jnp.bfloat16
    out = jax.ShapeDtypeStruct((tokens, width), bf16)
    vmem = pl.BlockSpec(memory_space=pltpu.VMEM)
    smem = pl.BlockSpec(memory_space=pltpu.SMEM)
    anywhere = pl.BlockSpec(memory_space=pl.ANY)
    message = pltpu.VMEM((CHIPS, 8, lanes), bf16)
    wide = pltpu.VMEM((tokens, 128), f32)
    pairs = pltpu.SemaphoreType.DMA((CHIPS,))
    copies = pltpu.SemaphoreType.DMA((len(NUMBER),))
    return pl.pallas_call(
        project_kernel,
        out_shape=(out, out, out),
        in_specs=[smem, anywhere, anywhere, vmem, vmem, vmem, vmem],
        out_specs=(vmem, vmem, vmem),
        scratch_shapes=[
            pltpu.VMEM((tokens, part), bf16),
            pltpu.VMEM((depth, cols), bf16),
            pltpu.VMEM((CHIPS // 2, 4 * depth, cols), bf16),
            pltpu.VMEM((DEPTH, tokens, part), bf16),
            pltpu.VMEM((DEPTH, tokens, part), bf16),
            pltpu.VMEM((tokens, cols), f32),
            wide,
            wide,
            wide,
            wide,
            wide,
            pltpu.VMEM((8, part * DEPTH), f32),
            pltpu.VMEM((8, part * DEPTH), f32),
            message,
            message,
            message,
            message,
            message,
            pltpu.SemaphoreType.DMA((2,)),
            copies,
            copies,
            pairs,
            pairs,
            pairs,
            pairs,
        ],
        compiler_params=pltpu.CompilerParams(
            collective_id=0, has_side_effects=True, vmem_limit_bytes=VMEM_BYTES
        ),
    )(lengths, x, w, group_of, gain, bias, col_bias)


def per_device(
    arrivals, group_of, lengths, page_table, ln_gain, ln_bias, w_qkv, qkv_bias, key_pool, value_pool
):
    req_count, fresh, part = arrivals.shape
    x = arrivals.reshape(req_count * fresh, part)
    q, k, v = project(lengths, x, w_qkv, group_of, ln_gain, ln_bias, qkv_bias)
    outs = attention(lengths, page_table, q, k, v, key_pool, value_pool)
    return tuple(a.reshape(req_count, fresh, -1) for a in outs)


def solution(mesh):
    in_specs = (
        P("req", None, "wgt"),
        P(),
        P("req"),
        P("req", None),
        P(),
        P(),
        P("req", "wgt"),
        P("wgt"),
        P("req", None, "wgt"),
        P("req", None, "wgt"),
    )
    out_specs = (P("req", None, "wgt"), P("req", None, "wgt"), P("req", None, "wgt"))
    return jax.shard_map(
        per_device, mesh=mesh, in_specs=in_specs, out_specs=out_specs, check_vma=False
    )
```

```python
import math

import jax
import jax.numpy as jnp
from jax import lax
from jax.experimental import pallas as pl
from jax.experimental.pallas import tpu as pltpu
from jax.sharding import PartitionSpec as P
import numpy as np

HEAD = 96
ROT = 24
EPS = 1e-05
CHUNK_PAGES = 4
VMEM_BYTES = 67043328


def attention_kernel(
    lengths, table, q_ref, k_ref, v_ref, key_pool, value_pool, out_ref, nk_ref, nv_ref,
    kbuf, vbuf, scores, mixed, sems,
):
    f32, bf16 = jnp.float32, jnp.bfloat16
    req_count, maxp = table.shape
    page, width = kbuf.shape[1], kbuf.shape[2]
    fresh = q_ref.shape[0] // req_count
    heads = width // HEAD
    rows = heads * fresh
    span = CHUNK_PAGES * page
    factor = math.log2(math.e) / math.sqrt(HEAD)
    low = -1e30

    def chunks_of(r):
        return (lengths[r] + (span - 1)) // span

    def key_copy(r, p):
        slot = r * maxp + p
        return pltpu.make_async_copy(key_pool.at[table[r, p]], kbuf.at[slot], sems.at[0, slot])

    def value_copy(r, p):
        slot = r * maxp + p
        return pltpu.make_async_copy(value_pool.at[table[r, p]], vbuf.at[slot], sems.at[1, slot])

    for r in range(req_count):

        @pl.loop(0, chunks_of(r) * CHUNK_PAGES)
        def _(p):
            key_copy(r, p).start()
            value_copy(r, p).start()

    nk_ref[...] = k_ref[...]
    nv_ref[...] = v_ref[...]

    iota = lambda shape, axis: lax.broadcasted_iota(jnp.int32, shape, axis)
    own_head = iota((rows, width), 1) // HEAD == iota((rows, width), 0) // fresh
    causal = iota((rows, fresh), 0) % fresh >= iota((rows, fresh), 1)
    column = iota((1, span), 1)

    def fold(value, op):
        folded = value[:, :128]
        for n in range(1, value.shape[1] // 128):
            folded = op(folded, value[:, n * 128 : (n + 1) * 128])
        return folded

    across = (((1,), (1,)), ((), ()))
    queries, fresh_scores, fresh_peaks = [], [], []
    for r in range(req_count):
        mine = pl.ds(r * fresh, fresh)
        query = jnp.concatenate([q_ref[mine, :]] * heads, axis=0)
        query = jnp.where(own_head, query, jnp.zeros_like(query))
        own = lax.dot_general(query, k_ref[mine, :], across, preferred_element_type=f32)
        own = jnp.where(causal, own, low)
        queries.append(query)
        fresh_scores.append(own)
        fresh_peaks.append(jnp.max(own, axis=1, keepdims=True))

    for r in range(req_count):
        mine = pl.ds(r * fresh, fresh)
        query, length = queries[r], lengths[r]

        def first(n, peak):
            for p in range(CHUNK_PAGES):
                key_copy(r, n * CHUNK_PAGES + p).wait()
            keys = kbuf[pl.ds(r * maxp + n * CHUNK_PAGES, CHUNK_PAGES)].reshape(span, width)
            value = lax.dot_general(query, keys, across, preferred_element_type=f32)
            value = value + jnp.where(column < length - n * span, 0.0, low)
            scores[n] = value
            return jnp.maximum(peak, fold(value, jnp.maximum))

        peak = lax.fori_loop(0, chunks_of(r), first, jnp.full((rows, 128), low, f32))
        peak = jnp.maximum(jnp.max(peak, axis=1, keepdims=True), fresh_peaks[r])
        offset = peak * factor
        weights = jnp.exp2(fresh_scores[r] * factor - offset)
        mixed[...] = jnp.dot(weights.astype(bf16), v_ref[mine, :], preferred_element_type=f32)
        fresh_total = jnp.sum(weights, axis=1, keepdims=True)

        def second(n, total):
            for p in range(CHUNK_PAGES):
                value_copy(r, n * CHUNK_PAGES + p).wait()
            values = vbuf[pl.ds(r * maxp + n * CHUNK_PAGES, CHUNK_PAGES)].reshape(span, width)
            weights = jnp.exp2(scores[n] * factor - offset)
            mixed[...] += jnp.dot(weights.astype(bf16), values, preferred_element_type=f32)
            return total + fold(weights, jnp.add)

        total = lax.fori_loop(0, chunks_of(r), second, jnp.zeros((rows, 128), f32))
        total = jnp.sum(total, axis=1, keepdims=True) + fresh_total
        part = jnp.where(own_head, mixed[...] * (1.0 / total), 0.0)
        summed = part[:fresh]
        for h in range(1, heads):
            summed = summed + part[h * fresh : (h + 1) * fresh]
        out_ref[mine, :] = summed.astype(out_ref.dtype)


def attention(lengths, table, q, k, v, key_pool, value_pool):
    rows, width = q.shape
    page = key_pool.shape[1]
    req_count, maxp = table.shape
    slots = req_count * maxp
    wide = width // HEAD * (rows // req_count)
    out = jax.ShapeDtypeStruct((rows, width), jnp.bfloat16)
    vmem = pl.BlockSpec(memory_space=pltpu.VMEM)
    smem = pl.BlockSpec(memory_space=pltpu.SMEM)
    anywhere = pl.BlockSpec(memory_space=pl.ANY)
    return pl.pallas_call(
        attention_kernel,
        out_shape=(out, out, out),
        in_specs=[smem, smem, vmem, vmem, vmem, anywhere, anywhere],
        out_specs=(vmem, vmem, vmem),
        scratch_shapes=[
            pltpu.VMEM((slots, page, width), jnp.bfloat16),
            pltpu.VMEM((slots, page, width), jnp.bfloat16),
            pltpu.VMEM((maxp // CHUNK_PAGES, wide, CHUNK_PAGES * page), jnp.float32),
            pltpu.VMEM((wide, width), jnp.float32),
            pltpu.SemaphoreType.DMA((2, slots)),
        ],
        compiler_params=pltpu.CompilerParams(vmem_limit_bytes=VMEM_BYTES),
    )(lengths, table, q, k, v, key_pool, value_pool)


MESH = pl.DeviceIdType.MESH
SIDE = 4
CHIPS = SIDE * SIDE
DEPTH = 8
OFFSETS = (0, -1, 1, 2)
THIRDS = 3


def last_parts(s):
    return ((0, None), (1, 0)) if s == 1 else ((2, None), (1, 1))


def copy_numbers():
    names = []
    for h in (0, 1):
        names += [("own", h, s) for s in (1, -1)]
        names += [("own on", h, s) for s in (1, -1)]
        names += [("row", h, du, s) for du in OFFSETS for s in (1, -1)]
        names += [("row on", h, du, s) for du in OFFSETS for s in (1, -1)]
        names += [("core", h, du, dv) for du in OFFSETS for dv in OFFSETS]
    for s in (1, -1):
        names += [("z", k, s, t) for k in (1, 2, 3) for t in range(THIRDS)]
        names += [("z", 4, s, t) for t, _ in last_parts(s)]
    names.append(("swap",))
    return {name: number for number, name in enumerate(names)}


NUMBER = copy_numbers()


def arrivals_in_order():
    rows = lambda du: [("row", h, du, s) for h in (1, 0) for s in (1, -1)]
    rows_on = lambda du: [("row on", 1, du), ("row on", 0, du)]
    thirds = lambda k, *ts: [("z", k, s, t) for t in ts for s in (1, -1)]
    order = rows(0) + thirds(1, 0) + [("own on", 0), ("own on", 1)] + thirds(1, 1, 2)
    order += rows(-1) + thirds(2, 0, 1, 2) + rows(1) + thirds(3, 0) + rows_on(0) + thirds(3, 1, 2)
    order += rows(2) + [("z", 4, -1, 1), ("z", 4, 1, 0), ("z", 4, 1, 1), ("z", 4, -1, 2)]
    order += rows_on(-1) + ["row 0"] + rows_on(1) + ["row -1"] + rows_on(2) + ["row 1", "row 2"]
    return order


def project_kernel(
    lengths, x_hbm, w_hbm, group_ref, gain_ref, bias_ref, col_bias_ref, q_ref, k_ref, v_ref,
    x_ref, w_ref, weights, slabs, normed, acc, cosines, sines, pivot, sums, squares, gains, biases,
    out1, in1, swapped, out2, in2, load, send, recv, send1, recv1, send2, recv2,
):
    f32, bf16, i32 = jnp.float32, jnp.bfloat16, jnp.int32
    tokens, part = x_ref.shape
    depth, cols = w_ref.shape
    model_width = part * DEPTH
    req_count = lengths.shape[0]
    fresh = tokens // req_count
    half = part // 2
    third = tokens // THIRDS
    width = cols // 3
    rows_half, rows_sub = depth // 2, depth // 4
    me, z = lax.axis_index("req"), lax.axis_index("wgt")
    core = me % 2
    chip = me // 2
    y, x = chip // SIDE, chip % SIDE
    iota = lambda shape, axis: lax.broadcasted_iota(i32, shape, axis)

    def device(number, c=core):
        return (number * 2 + c, z)

    partner = device(chip, 1 - core)

    load_x = pltpu.make_async_copy(x_hbm, x_ref, load.at[0])
    load_w = pltpu.make_async_copy(w_hbm, w_ref, load.at[1])
    load_x.start()
    load_w.start()

    barrier = pltpu.get_barrier_semaphore()

    @pl.loop(1, CHIPS)
    def _(d):
        pl.semaphore_signal(barrier, 1, device_id=device((chip + d) % CHIPS), device_id_type=MESH)

    pl.semaphore_signal(barrier, 1, device_id=partner, device_id_type=MESH)
    for s in (1, DEPTH - 1):
        pl.semaphore_signal(barrier, 1, device_id=(me, (z + s) % DEPTH), device_id_type=MESH)

    load_x.wait()
    m, n = iota((CHIPS * 8, tokens), 0), iota((CHIPS * 8, tokens), 1)
    for t in range(THIRDS):
        take = (m % 8) // 2 * fresh + t * CHIPS + m // 8 == n
        piece = jnp.zeros((CHIPS * 8, half), f32)
        for h in (0, 1):
            chosen = jnp.where(take & (m % 2 == h), 1.0, 0.0).astype(bf16)
            piece += jnp.dot(chosen, x_ref[:, h * half : (h + 1) * half], preferred_element_type=f32)
        out1[:, :, t * half : (t + 1) * half] = piece.reshape(CHIPS, 8, half).astype(bf16)
    in1[chip] = out1[chip]

    pl.semaphore_wait(barrier, CHIPS - 1 + 3)

    def spread(source, target, send_sems, recv_sems):
        def copy(d):
            other = (chip + d) % CHIPS
            return pltpu.make_async_remote_copy(
                src_ref=source.at[other],
                dst_ref=target.at[chip],
                send_sem=send_sems.at[d],
                recv_sem=recv_sems.at[d],
                device_id=device(other),
                device_id_type=MESH,
            )

        return copy

    first, second = spread(out1, in1, send1, recv1), spread(out2, in2, send2, recv2)

    @pl.loop(1, CHIPS)
    def _(d):
        first(d).start()

    def by_kind(value):
        heads = range(width // HEAD)
        return jnp.concatenate(
            [
                value[:, (h * 3 + kind) * HEAD : (h * 3 + kind + 1) * HEAD]
                for kind in range(3)
                for h in heads
            ],
            axis=1,
        )

    def place(number, c):
        return number // 2, (number % 2) * (2 * depth) + c * depth

    load_w.wait()
    own_pair, own_row = place(chip, core)
    weights[own_pair, pl.ds(pl.multiple_of(own_row, 64), depth), :] = by_kind(w_ref[...])

    def remote(name, ref, target, dst=None):
        return pltpu.make_async_remote_copy(
            src_ref=ref,
            dst_ref=ref if dst is None else dst,
            send_sem=send.at[NUMBER[name]],
            recv_sem=recv.at[NUMBER[name]],
            device_id=target,
            device_id_type=MESH,
        )

    where = {0: (x, y), 1: (y, x)}

    def chip_at(h, du, dv):
        u, v = where[h]
        u, v = (u + du + SIDE) % SIDE, (v + dv + SIDE) % SIDE
        return v * SIDE + u if h == 0 else u * SIDE + v

    def block(h, du, dv, c=core, sub=None):
        pair, row = place(chip_at(h, du, dv), c)
        row = row + h * rows_half + (0 if sub in (None, 1) else rows_sub)
        return weights.at[pair, pl.ds(pl.multiple_of(row, 16), rows_half if sub is None else rows_sub), :]

    def weight_copy(name):
        kind, h = name[0], name[1]
        if kind == "own":
            return remote(name, block(h, 0, 0), device(chip_at(h, name[2], 0)))
        if kind == "own on":
            s = name[2]
            return remote(name, block(h, -s, 0, sub=s), device(chip_at(h, s, 0)))
        if kind == "row":
            du, s = name[2], name[3]
            return remote(name, block(h, du, 0), device(chip_at(h, 0, s)))
        if kind == "row on":
            du, s = name[2], name[3]
            return remote(name, block(h, du, -s, sub=s), device(chip_at(h, 0, s)))
        du, dv = name[2], name[3]
        return remote(name, block(h, du, dv), partner)

    started = []

    def start(*name):
        weight_copy(name).start()
        started.append(name)

    def arrive(*name):
        weight_copy(name).wait_recv()

    for h in (0, 1):
        for s in (1, -1):
            start("own", h, s)
    for h in (0, 1):
        start("core", h, 0, 0)

    a, b = iota((CHIPS * 8, CHIPS * 8), 0), iota((CHIPS * 8, CHIPS * 8), 1)
    groups = group_ref[...].reshape(1, -1)
    group_row = jnp.broadcast_to(groups, a.shape)
    group_col = jnp.sum(jnp.where(a == b, group_row, 0), axis=1, keepdims=True)
    rank = jnp.sum(jnp.where((group_col == group_row) & (a < b), 1, 0), axis=0, keepdims=True)
    slot_row = groups * req_count + rank
    slot_col = jnp.sum(jnp.where(a == b, jnp.broadcast_to(slot_row, a.shape), 0), axis=1, keepdims=True)

    def selector(c):
        arriving = (b // 8 * 2 + c) * req_count + b % 8 // 2
        slot = jnp.sum(jnp.where(a == arriving, slot_col, 0), axis=0, keepdims=True)
        wanted = (a // 8 * 2 + core) * req_count + a % 8 // 2
        return jnp.where((wanted == slot) & (a % 2 == b % 2), 1.0, 0.0).astype(bf16)

    pick_own, pick_other = selector(core), selector(1 - core)

    @pl.loop(1, CHIPS)
    def _(d):
        first(d).wait_recv()

    swap = remote(("swap",), in1, partner, swapped)
    swap.start()

    def flat(ref):
        return ref[...].astype(f32).reshape(CHIPS * 8, THIRDS * half).astype(bf16)

    mixed = jnp.dot(pick_own, flat(in1), preferred_element_type=f32)
    swap.wait_recv()
    mixed = mixed + jnp.dot(pick_other, flat(swapped), preferred_element_type=f32)
    out2[...] = mixed.reshape(CHIPS, 8, THIRDS * half).astype(bf16)
    in2[chip] = out2[chip]

    @pl.loop(1, CHIPS)
    def _(d):
        second(d).start()

    for h in (0, 1):
        for s in (1, -1):
            start("row", h, 0, s)

    gains[...] = jnp.broadcast_to(gain_ref[...].astype(f32).reshape(1, -1), gains.shape)
    biases[...] = jnp.broadcast_to(bias_ref[...].astype(f32).reshape(1, -1), biases.shape)
    acc[...] = jnp.broadcast_to(by_kind(col_bias_ref[...].astype(f32).reshape(1, -1)), acc.shape)

    lane = iota((1, 128), 1) % 32
    turning = ROT // 2
    inverse = jnp.zeros((1, 128), f32)
    for i in range(turning):
        value = float(np.float32(10000.0) ** np.float32(-2.0 * i / ROT))
        inverse = jnp.where((lane == i) | (lane == i + turning), value, inverse)
    row = iota((tokens, 1), 0)
    request = row % third // CHIPS
    position = row // third * CHIPS + row % CHIPS
    for r in range(req_count):
        position = position + jnp.where(request == r, lengths[r], 0)
    angle = position.astype(f32) * inverse
    cosines[...] = jnp.cos(angle)
    sine = jnp.sin(angle)
    sines[...] = jnp.where(lane < turning, -sine, sine)

    for h in (0, 1):
        for s in (1, -1):
            arrive("own", h, s)
    for h in (0, 1):
        for s in (1, -1):
            start("own on", h, s)
    for h in (0, 1):
        for s in (1, -1):
            start("core", h, -s, 0)
    for s in (1, -1):
        for h in (0, 1):
            start("row", h, -s, 1)
            start("row", h, -s, -1)

    @pl.loop(1, CHIPS)
    def _(d):
        second(d).wait_recv()

    m, n = iota((third, CHIPS * 8), 0), iota((third, CHIPS * 8), 1)
    pieces = flat(in2)
    for h in (0, 1):
        chosen = jnp.where(m % CHIPS * 8 + m // CHIPS * 2 + h == n, 1.0, 0.0).astype(bf16)
        rows = jnp.dot(chosen, pieces, preferred_element_type=f32).astype(bf16)
        for t in range(THIRDS):
            slabs[z, pl.ds(t * third, third), h * half : (h + 1) * half] = rows[:, t * half : (t + 1) * half]

    def slab(k, s, t, piece=None):
        ref = slabs.at[(z - k * s + DEPTH) % DEPTH]
        if piece is None:
            return ref.at[pl.ds(t * third, third), :]
        return ref.at[pl.ds(t * third + piece * (third // 2), third // 2), :]

    def z_copy(k, s, t):
        piece = dict(last_parts(s))[t] if k == 4 else None
        return remote(("z", k, s, t), slab(k - 1, s, t, piece), (me, (z + s + DEPTH) % DEPTH))

    for t in range(THIRDS):
        for s in (1, -1):
            z_copy(1, s, t).start()

    def folded(value):
        total = value[:, :128]
        for j in range(1, part // 128):
            total = total + value[:, j * 128 : (j + 1) * 128]
        return total

    for t in range(THIRDS):
        mine = pl.ds(t * third, third)
        own = jnp.sum(folded(slabs[z, mine, :].astype(f32)), axis=1, keepdims=True) * (1.0 / part)
        pivot[mine, :] = jnp.broadcast_to(own, (third, 128))
    sums[...] = jnp.zeros_like(sums)
    squares[...] = jnp.zeros_like(squares)

    def add_sums(number, t):
        @pl.loop(t * third, (t + 1) * third, step=32)
        def _(start_row):
            mine = pl.ds(pl.multiple_of(start_row, 32), 32)
            origin, total, square = pivot[mine, :], sums[mine, :], squares[mine, :]
            for j in range(part // 128):
                apart = slabs[number, mine, j * 128 : (j + 1) * 128].astype(f32) - origin
                total = total + apart
                square = square + apart * apart
            sums[mine, :] = total
            squares[mine, :] = square

    def normalise(t):
        @pl.loop(t * third, (t + 1) * third, step=32)
        def _(start_row):
            mine = pl.ds(pl.multiple_of(start_row, 32), 32)
            shift = jnp.sum(sums[mine, :], axis=1, keepdims=True) * (1.0 / model_width)
            square = jnp.sum(squares[mine, :], axis=1, keepdims=True) * (1.0 / model_width)
            inv = lax.rsqrt(jnp.maximum(square - shift * shift, 0.0) + EPS)
            inv = jnp.broadcast_to(inv, (32, 128))
            mean = pivot[mine, :] + shift
            for j in range(model_width // 128):
                w, lanes = j * 128 // part, slice(j * 128 % part, j * 128 % part + 128)
                value = (slabs[w, mine, lanes].astype(f32) - mean) * inv
                value = value.reshape(4, 8, 128) * gains[:, j * 128 : (j + 1) * 128][None]
                value = value + biases[:, j * 128 : (j + 1) * 128][None]
                normed[w, mine, lanes] = value.reshape(32, 128).astype(bf16)

    def from_core(h, du, dv):
        remote(("core", h, du, dv), block(h, du, dv, c=1 - core), partner).wait_recv()

    def multiply(dy):
        for dx in OFFSETS:
            from_core(0, dx, dy)
            from_core(1, dy, dx)
        first_pair = (y + dy + SIDE) % SIDE * 2

        @pl.loop(first_pair, first_pair + 2)
        def _(pair):
            acc[...] += jnp.dot(normed[pair], weights[pair], preferred_element_type=f32)

    for t in range(THIRDS):
        add_sums(z, t)

    seen = set()
    for event in arrivals_in_order():
        seen.add(event)
        if event[0] == "own on":
            h = event[1]
            arrive("own on", h, 1)
            arrive("own on", h, -1)
            start("row", h, 2, 1)
            start("row", h, 2, -1)
            start("core", h, 2, 0)
        elif event[0] == "row":
            arrive(*event)
            _, h, du, s = event
            start("row on", h, du, s)
            start("core", h, du, -s)
        elif event[0] == "row on":
            _, h, du = event
            arrive("row on", h, du, 1)
            arrive("row on", h, du, -1)
            start("core", h, du, 2)
        elif event[0] == "z":
            _, k, s, t = event
            z_copy(k, s, t).wait_recv()
            if k < 3 or (k == 3 and t in dict(last_parts(s))):
                z_copy(k + 1, s, t).start()
            if k < 4:
                add_sums((z - k * s + DEPTH) % DEPTH, t)
            elif all(("z", 4, d, t) in seen for d in (1, -1) if t in dict(last_parts(d))):
                add_sums((z + 4) % DEPTH, t)
                normalise(t)
        else:
            multiply(int(event.split()[1]))

    def turn(value):
        lanes = iota((1, width), 1) % HEAD
        forward, backward = pltpu.roll(value, width - turning, 1), pltpu.roll(value, turning, 1)
        near = jnp.where(lanes < turning, forward, backward)
        cosine = jnp.concatenate([cosines[...]] * (width // 128), axis=1)
        sine = jnp.concatenate([sines[...]] * (width // 128), axis=1)
        return jnp.where(lanes < ROT, value * cosine + near * sine, value)

    def put(ref, value):
        value = value.astype(bf16)
        for t in range(THIRDS):
            for r in range(req_count):
                row = t * third + r * CHIPS
                ref[pl.ds(r * fresh + t * CHIPS, CHIPS), :] = value[row : row + CHIPS]

    put(q_ref, turn(acc[:, :width]))
    put(k_ref, turn(acc[:, width : 2 * width]))
    put(v_ref, acc[:, 2 * width :])

    for name in started:
        weight_copy(name).wait_send()
    for s in (1, -1):
        for k in (1, 2, 3, 4):
            for t in range(THIRDS):
                if k < 4 or t in dict(last_parts(s)):
                    z_copy(k, s, t).wait_send()
    swap.wait_send()

    @pl.loop(1, CHIPS)
    def _(d):
        first(d).wait_send()
        second(d).wait_send()


def project(lengths, x, w, group_of, gain, bias, col_bias):
    tokens, part = x.shape
    depth, cols = w.shape
    width = cols // 3
    lanes = tokens * part // (CHIPS * 8)
    f32, bf16 = jnp.float32, jnp.bfloat16
    out = jax.ShapeDtypeStruct((tokens, width), bf16)
    vmem = pl.BlockSpec(memory_space=pltpu.VMEM)
    smem = pl.BlockSpec(memory_space=pltpu.SMEM)
    anywhere = pl.BlockSpec(memory_space=pl.ANY)
    message = pltpu.VMEM((CHIPS, 8, lanes), bf16)
    wide = pltpu.VMEM((tokens, 128), f32)
    pairs = pltpu.SemaphoreType.DMA((CHIPS,))
    copies = pltpu.SemaphoreType.DMA((len(NUMBER),))
    return pl.pallas_call(
        project_kernel,
        out_shape=(out, out, out),
        in_specs=[smem, anywhere, anywhere, vmem, vmem, vmem, vmem],
        out_specs=(vmem, vmem, vmem),
        scratch_shapes=[
            pltpu.VMEM((tokens, part), bf16),
            pltpu.VMEM((depth, cols), bf16),
            pltpu.VMEM((CHIPS // 2, 4 * depth, cols), bf16),
            pltpu.VMEM((DEPTH, tokens, part), bf16),
            pltpu.VMEM((DEPTH, tokens, part), bf16),
            pltpu.VMEM((tokens, cols), f32),
            wide,
            wide,
            wide,
            wide,
            wide,
            pltpu.VMEM((8, part * DEPTH), f32),
            pltpu.VMEM((8, part * DEPTH), f32),
            message,
            message,
            message,
            message,
            message,
            pltpu.SemaphoreType.DMA((2,)),
            copies,
            copies,
            pairs,
            pairs,
            pairs,
            pairs,
        ],
        compiler_params=pltpu.CompilerParams(
            collective_id=0, has_side_effects=True, vmem_limit_bytes=VMEM_BYTES
        ),
    )(lengths, x, w, group_of, gain, bias, col_bias)


def per_device(
    arrivals, group_of, lengths, page_table, ln_gain, ln_bias, w_qkv, qkv_bias, key_pool, value_pool
):
    req_count, fresh, part = arrivals.shape
    x = arrivals.reshape(req_count * fresh, part)
    q, k, v = project(lengths, x, w_qkv, group_of, ln_gain, ln_bias, qkv_bias)
    outs = attention(lengths, page_table, q, k, v, key_pool, value_pool)
    return tuple(a.reshape(req_count, fresh, -1) for a in outs)


def solution(mesh):
    in_specs = (
        P("req", None, "wgt"),
        P(),
        P("req"),
        P("req", None),
        P(),
        P(),
        P("req", "wgt"),
        P("wgt"),
        P("req", None, "wgt"),
        P("req", None, "wgt"),
    )
    out_specs = (P("req", None, "wgt"), P("req", None, "wgt"), P("req", None, "wgt"))
    return jax.shard_map(
        per_device, mesh=mesh, in_specs=in_specs, out_specs=out_specs, check_vma=False
    )
```

```python
import math

import jax
import jax.numpy as jnp
from jax import lax
from jax.experimental import pallas as pl
from jax.experimental.pallas import tpu as pltpu
from jax.sharding import PartitionSpec as P
import numpy as np

HEAD = 96
ROT = 24
EPS = 1e-05
CHUNK_PAGES = 4
VMEM_BYTES = 67043328


def attention_kernel(
    lengths, table, q_ref, k_ref, v_ref, key_pool, value_pool, out_ref, nk_ref, nv_ref,
    kbuf, vbuf, queries, scores, peaks, offsets, totals, mixed, work, sems,
):
    f32, bf16 = jnp.float32, jnp.bfloat16
    req_count, maxp = table.shape
    page, width = kbuf.shape[1], kbuf.shape[2]
    fresh = q_ref.shape[0] // req_count
    heads = width // HEAD
    rows = heads * fresh
    span = CHUNK_PAGES * page
    factor = math.log2(math.e) / math.sqrt(HEAD)
    low = -1e30

    count = 0
    for r in range(req_count):
        chunks = (lengths[r] + (span - 1)) // span

        @pl.loop(0, chunks)
        def _(n):
            i = count + n
            work[0, i] = r
            work[1, i] = n
            for p in range(CHUNK_PAGES):
                number, slot = table[r, n * CHUNK_PAGES + p], i * CHUNK_PAGES + p
                pltpu.make_async_copy(key_pool.at[number], kbuf.at[slot], sems.at[0, i]).start()
                pltpu.make_async_copy(value_pool.at[number], vbuf.at[slot], sems.at[1, i]).start()

        count = count + chunks

    def pages(i):
        return pl.ds(i * CHUNK_PAGES, CHUNK_PAGES)

    def wait(pool, buffer, kind, i):
        pltpu.make_async_copy(pool.at[pl.ds(0, CHUNK_PAGES)], buffer.at[pages(i)], sems.at[kind, i]).wait()

    nk_ref[...] = k_ref[...]
    nv_ref[...] = v_ref[...]

    iota = lambda shape, axis: lax.broadcasted_iota(jnp.int32, shape, axis)
    own_head = iota((rows, width), 1) // HEAD == iota((rows, width), 0) // fresh
    causal = iota((rows, fresh), 0) % fresh >= iota((rows, fresh), 1)
    column = iota((1, span), 1)

    def fold(value, op):
        folded = value[:, :128]
        for n in range(1, value.shape[1] // 128):
            folded = op(folded, value[:, n * 128 : (n + 1) * 128])
        return folded

    across = (((1,), (1,)), ((), ()))
    fresh_scores = []
    for r in range(req_count):
        mine = pl.ds(r * fresh, fresh)
        query = jnp.concatenate([q_ref[mine, :]] * heads, axis=0)
        query = jnp.where(own_head, query, jnp.zeros_like(query))
        queries[r] = query
        own = lax.dot_general(query, k_ref[mine, :], across, preferred_element_type=f32)
        own = jnp.where(causal, own, low)
        fresh_scores.append(own)
        peaks[r] = jnp.broadcast_to(jnp.max(own, axis=1, keepdims=True), (rows, 128))
        totals[r] = jnp.zeros((rows, 128), f32)

    def over_chunks(step):
        @pl.loop(0, count // 2)
        def _(j):
            step((2 * j, 2 * j + 1))

        @pl.when(count % 2 == 1)
        def _():
            step((count - 1,))

    def first(chunks):
        for i in chunks:
            wait(key_pool, kbuf, 0, i)
        values = []
        for i in chunks:
            r, n = work[0, i], work[1, i]
            keys = kbuf[pages(i)].reshape(span, width)
            value = lax.dot_general(queries[r], keys, across, preferred_element_type=f32)
            values.append(value + jnp.where(column < lengths[r] - n * span, 0.0, low))
        for i, value in zip(chunks, values):
            r = work[0, i]
            scores[i] = value
            peaks[r] = jnp.maximum(peaks[r], fold(value, jnp.maximum))

    over_chunks(first)

    fresh_totals = []
    for r in range(req_count):
        mine = pl.ds(r * fresh, fresh)
        offset = jnp.max(peaks[r], axis=1, keepdims=True) * factor
        offsets[r] = jnp.broadcast_to(offset, (rows, 128))
        weights = jnp.exp2(fresh_scores[r] * factor - offset)
        mixed[r] = jnp.dot(weights.astype(bf16), v_ref[mine, :], preferred_element_type=f32)
        fresh_totals.append(jnp.sum(weights, axis=1, keepdims=True))

    def second(chunks):
        for i in chunks:
            wait(value_pool, vbuf, 1, i)
        parts = []
        for i in chunks:
            r = work[0, i]
            values = vbuf[pages(i)].reshape(span, width)
            offset = jnp.concatenate([offsets[r]] * (span // 128), axis=1)
            weights = jnp.exp2(scores[i] * factor - offset)
            part = jnp.dot(weights.astype(bf16), values, preferred_element_type=f32)
            parts.append((part, fold(weights, jnp.add)))
        for i, (part, total) in zip(chunks, parts):
            r = work[0, i]
            mixed[r] += part
            totals[r] += total

    over_chunks(second)

    for r in range(req_count):
        total = jnp.sum(totals[r], axis=1, keepdims=True) + fresh_totals[r]
        part = jnp.where(own_head, mixed[r] * (1.0 / total), 0.0)
        summed = part[:fresh]
        for h in range(1, heads):
            summed = summed + part[h * fresh : (h + 1) * fresh]
        out_ref[pl.ds(r * fresh, fresh), :] = summed.astype(out_ref.dtype)


def attention(lengths, table, q, k, v, key_pool, value_pool):
    rows, width = q.shape
    page = key_pool.shape[1]
    req_count, maxp = table.shape
    slots = req_count * maxp
    chunks = slots // CHUNK_PAGES
    wide = width // HEAD * (rows // req_count)
    f32, bf16 = jnp.float32, jnp.bfloat16
    out = jax.ShapeDtypeStruct((rows, width), bf16)
    vmem = pl.BlockSpec(memory_space=pltpu.VMEM)
    smem = pl.BlockSpec(memory_space=pltpu.SMEM)
    anywhere = pl.BlockSpec(memory_space=pl.ANY)
    return pl.pallas_call(
        attention_kernel,
        out_shape=(out, out, out),
        in_specs=[smem, smem, vmem, vmem, vmem, anywhere, anywhere],
        out_specs=(vmem, vmem, vmem),
        scratch_shapes=[
            pltpu.VMEM((slots, page, width), bf16),
            pltpu.VMEM((slots, page, width), bf16),
            pltpu.VMEM((req_count, wide, width), bf16),
            pltpu.VMEM((chunks, wide, CHUNK_PAGES * page), f32),
            pltpu.VMEM((req_count, wide, 128), f32),
            pltpu.VMEM((req_count, wide, 128), f32),
            pltpu.VMEM((req_count, wide, 128), f32),
            pltpu.VMEM((req_count, wide, width), f32),
            pltpu.SMEM((2, chunks), jnp.int32),
            pltpu.SemaphoreType.DMA((2, chunks)),
        ],
        compiler_params=pltpu.CompilerParams(vmem_limit_bytes=VMEM_BYTES),
    )(lengths, table, q, k, v, key_pool, value_pool)


MESH = pl.DeviceIdType.MESH
SIDE = 4
CHIPS = SIDE * SIDE
DEPTH = 8
OFFSETS = (0, -1, 1, 2)
THIRDS = 3


def last_parts(s):
    return ((0, None), (1, 0)) if s == 1 else ((2, None), (1, 1))


def copy_numbers():
    names = []
    for h in (0, 1):
        names += [("own", h, s) for s in (1, -1)]
        names += [("own on", h, s) for s in (1, -1)]
        names += [("row", h, du, s) for du in OFFSETS for s in (1, -1)]
        names += [("row on", h, du, s) for du in OFFSETS for s in (1, -1)]
        names += [("core", h, du, dv) for du in OFFSETS for dv in OFFSETS]
    for s in (1, -1):
        names += [("z", k, s, t) for k in (1, 2, 3) for t in range(THIRDS)]
        names += [("z", 4, s, t) for t, _ in last_parts(s)]
    names += [("swap",), ("first",), ("second",)]
    return {name: number for number, name in enumerate(names)}


NUMBER = copy_numbers()
SENDS = ("own", "own on", "row", "row on", "core", "z", "z last", "swap", "first", "second")


def send_number(name):
    return SENDS.index("z last" if name[:2] == ("z", 4) else name[0])


def arrivals_in_order():
    rows = lambda du: [("row", h, du, s) for h in (1, 0) for s in (1, -1)]
    rows_on = lambda du: [("row on", 1, du), ("row on", 0, du)]
    thirds = lambda k, *ts: [("z", k, s, t) for t in ts for s in (1, -1)]
    order = rows(0) + thirds(1, 0) + [("own on", 0), ("own on", 1)] + thirds(1, 1, 2)
    order += rows(-1) + thirds(2, 0, 1, 2) + rows(1) + thirds(3, 0) + rows_on(0) + thirds(3, 1, 2)
    order += rows(2) + [("z", 4, -1, 1), ("z", 4, 1, 0), ("z", 4, 1, 1), ("z", 4, -1, 2)]
    order += rows_on(-1) + ["row 0"] + rows_on(1) + ["row -1"] + rows_on(2) + ["row 1", "near 2", "far 2"]
    return order


def project_kernel(
    lengths, x_hbm, w_hbm, group_ref, gain_ref, bias_ref, col_bias_ref, q_ref, k_ref, v_ref,
    x_ref, w_ref, weights, slabs, normed, acc, cosines, sines, pivot, sums, squares, gains, biases,
    out1, in1, swapped, out2, in2, load, send, recv,
):
    f32, bf16, i32 = jnp.float32, jnp.bfloat16, jnp.int32
    tokens, part = x_ref.shape
    depth, cols = w_ref.shape
    model_width = part * DEPTH
    req_count = lengths.shape[0]
    fresh = tokens // req_count
    half = part // 2
    third = tokens // THIRDS
    width = cols // 3
    rows_half, rows_sub = depth // 2, depth // 4
    me, z = lax.axis_index("req"), lax.axis_index("wgt")
    core = me % 2
    chip = me // 2
    y, x = chip // SIDE, chip % SIDE
    iota = lambda shape, axis: lax.broadcasted_iota(i32, shape, axis)

    def device(number, c=core):
        return (number * 2 + c, z)

    partner = device(chip, 1 - core)

    load_x = pltpu.make_async_copy(x_hbm, x_ref, load.at[0])
    load_w = pltpu.make_async_copy(w_hbm, w_ref, load.at[1])
    load_x.start()
    load_w.start()

    barrier = pltpu.get_barrier_semaphore()

    for d in range(1, CHIPS):
        pl.semaphore_signal(barrier, 1, device_id=device((chip + d) % CHIPS), device_id_type=MESH)

    pl.semaphore_signal(barrier, 1, device_id=partner, device_id_type=MESH)
    for s in (1, DEPTH - 1):
        pl.semaphore_signal(barrier, 1, device_id=(me, (z + s) % DEPTH), device_id_type=MESH)

    load_x.wait()
    m, n = iota((CHIPS * 8, tokens), 0), iota((CHIPS * 8, tokens), 1)
    for t in range(THIRDS):
        take = (m % 8) // 2 * fresh + t * CHIPS + m // 8 == n
        piece = jnp.zeros((CHIPS * 8, half), f32)
        for h in (0, 1):
            chosen = jnp.where(take & (m % 2 == h), 1.0, 0.0).astype(bf16)
            piece += jnp.dot(chosen, x_ref[:, h * half : (h + 1) * half], preferred_element_type=f32)
        out1[:, :, t * half : (t + 1) * half] = piece.reshape(CHIPS, 8, half).astype(bf16)
    in1[chip] = out1[chip]

    pl.semaphore_wait(barrier, CHIPS - 1 + 3)

    def spread(name, source, target):
        for d in range(1, CHIPS):
            other = (chip + d) % CHIPS
            remote((name,), source.at[other], device(other), target.at[chip]).start()

    def gathered(name, target):
        ref = target.at[pl.ds(0, CHIPS - 1)]
        remote((name,), ref, partner).wait_recv()

    def remote(name, ref, target, dst=None):
        return pltpu.make_async_remote_copy(
            src_ref=ref,
            dst_ref=ref if dst is None else dst,
            send_sem=send.at[send_number(name)],
            recv_sem=recv.at[NUMBER[name]],
            device_id=target,
            device_id_type=MESH,
        )

    spread("first", out1, in1)

    def by_kind(value):
        heads = range(width // HEAD)
        return jnp.concatenate(
            [
                value[:, (h * 3 + kind) * HEAD : (h * 3 + kind + 1) * HEAD]
                for kind in range(3)
                for h in heads
            ],
            axis=1,
        )

    def place(number, c):
        return number // 2, (number % 2) * (2 * depth) + c * depth

    load_w.wait()
    own_pair, own_row = place(chip, core)
    weights[own_pair, pl.ds(pl.multiple_of(own_row, 64), depth), :] = by_kind(w_ref[...])

    where = {0: (x, y), 1: (y, x)}

    def chip_at(h, du, dv):
        u, v = where[h]
        u, v = (u + du + SIDE) % SIDE, (v + dv + SIDE) % SIDE
        return v * SIDE + u if h == 0 else u * SIDE + v

    def block(h, du, dv, c=core, sub=None):
        pair, row = place(chip_at(h, du, dv), c)
        row = row + h * rows_half + (0 if sub in (None, 1) else rows_sub)
        return weights.at[pair, pl.ds(pl.multiple_of(row, 16), rows_half if sub is None else rows_sub), :]

    def weight_copy(name):
        kind, h = name[0], name[1]
        if kind == "own":
            return remote(name, block(h, 0, 0), device(chip_at(h, name[2], 0)))
        if kind == "own on":
            s = name[2]
            return remote(name, block(h, -s, 0, sub=s), device(chip_at(h, s, 0)))
        if kind == "row":
            du, s = name[2], name[3]
            return remote(name, block(h, du, 0), device(chip_at(h, 0, s)))
        if kind == "row on":
            du, s = name[2], name[3]
            return remote(name, block(h, du, -s, sub=s), device(chip_at(h, 0, s)))
        du, dv = name[2], name[3]
        return remote(name, block(h, du, dv), partner)

    def start(*name):
        weight_copy(name).start()

    def arrive(*name):
        weight_copy(name).wait_recv()

    for h in (0, 1):
        for s in (1, -1):
            start("own", h, s)
    for h in (0, 1):
        start("core", h, 0, 0)

    a, b = iota((CHIPS * 8, CHIPS * 8), 0), iota((CHIPS * 8, CHIPS * 8), 1)
    groups = group_ref[...].reshape(1, -1)
    group_row = jnp.broadcast_to(groups, a.shape)
    group_col = jnp.sum(jnp.where(a == b, group_row, 0), axis=1, keepdims=True)
    rank = jnp.sum(jnp.where((group_col == group_row) & (a < b), 1, 0), axis=0, keepdims=True)
    slot_row = groups * req_count + rank
    slot_col = jnp.sum(jnp.where(a == b, jnp.broadcast_to(slot_row, a.shape), 0), axis=1, keepdims=True)

    def selector(c):
        arriving = (b // 8 * 2 + c) * req_count + b % 8 // 2
        slot = jnp.sum(jnp.where(a == arriving, slot_col, 0), axis=0, keepdims=True)
        wanted = (a // 8 * 2 + core) * req_count + a % 8 // 2
        return jnp.where((wanted == slot) & (a % 2 == b % 2), 1.0, 0.0).astype(bf16)

    pick_own, pick_other = selector(core), selector(1 - core)

    gathered("first", in1)

    swap = remote(("swap",), in1, partner, swapped)
    swap.start()

    def flat(ref):
        return ref[...].astype(f32).reshape(CHIPS * 8, THIRDS * half).astype(bf16)

    mixed = jnp.dot(pick_own, flat(in1), preferred_element_type=f32)
    swap.wait_recv()
    mixed = mixed + jnp.dot(pick_other, flat(swapped), preferred_element_type=f32)
    out2[...] = mixed.reshape(CHIPS, 8, THIRDS * half).astype(bf16)
    in2[chip] = out2[chip]

    spread("second", out2, in2)

    for h in (0, 1):
        for s in (1, -1):
            start("row", h, 0, s)

    gains[...] = jnp.broadcast_to(gain_ref[...].astype(f32).reshape(1, -1), gains.shape)
    biases[...] = jnp.broadcast_to(bias_ref[...].astype(f32).reshape(1, -1), biases.shape)
    acc[...] = jnp.broadcast_to(by_kind(col_bias_ref[...].astype(f32).reshape(1, -1)), acc.shape)

    lane = iota((1, 128), 1) % 32
    turning = ROT // 2
    inverse = jnp.zeros((1, 128), f32)
    for i in range(turning):
        value = float(np.float32(10000.0) ** np.float32(-2.0 * i / ROT))
        inverse = jnp.where((lane == i) | (lane == i + turning), value, inverse)
    row = iota((tokens, 1), 0)
    request = row % third // CHIPS
    position = row // third * CHIPS + row % CHIPS
    for r in range(req_count):
        position = position + jnp.where(request == r, lengths[r], 0)
    angle = position.astype(f32) * inverse
    cosines[...] = jnp.cos(angle)
    sine = jnp.sin(angle)
    sines[...] = jnp.where(lane < turning, -sine, sine)

    for h in (0, 1):
        for s in (1, -1):
            arrive("own", h, s)
    for h in (0, 1):
        for s in (1, -1):
            start("own on", h, s)
    for h in (0, 1):
        for s in (1, -1):
            start("core", h, -s, 0)
    for s in (1, -1):
        for h in (0, 1):
            start("row", h, -s, 1)
            start("row", h, -s, -1)

    gathered("second", in2)

    m, n = iota((third, CHIPS * 8), 0), iota((third, CHIPS * 8), 1)
    pieces = flat(in2)
    for h in (0, 1):
        chosen = jnp.where(m % CHIPS * 8 + m // CHIPS * 2 + h == n, 1.0, 0.0).astype(bf16)
        rows = jnp.dot(chosen, pieces, preferred_element_type=f32).astype(bf16)
        for t in range(THIRDS):
            slabs[z, pl.ds(t * third, third), h * half : (h + 1) * half] = rows[:, t * half : (t + 1) * half]

    def slab(k, s, t, piece=None):
        ref = slabs.at[(z - k * s + DEPTH) % DEPTH]
        if piece is None:
            return ref.at[pl.ds(t * third, third), :]
        return ref.at[pl.ds(t * third + piece * (third // 2), third // 2), :]

    def z_copy(k, s, t):
        piece = dict(last_parts(s))[t] if k == 4 else None
        return remote(("z", k, s, t), slab(k - 1, s, t, piece), (me, (z + s + DEPTH) % DEPTH))

    for t in range(THIRDS):
        for s in (1, -1):
            z_copy(1, s, t).start()

    def folded(value):
        total = value[:, :128]
        for j in range(1, part // 128):
            total = total + value[:, j * 128 : (j + 1) * 128]
        return total

    for t in range(THIRDS):
        mine = pl.ds(t * third, third)
        own = jnp.sum(folded(slabs[z, mine, :].astype(f32)), axis=1, keepdims=True) * (1.0 / part)
        pivot[mine, :] = jnp.broadcast_to(own, (third, 128))
    sums[...] = jnp.zeros_like(sums)
    squares[...] = jnp.zeros_like(squares)

    def add_sums(number, t):
        @pl.loop(t * third, (t + 1) * third, step=32)
        def _(start_row):
            mine = pl.ds(pl.multiple_of(start_row, 32), 32)
            origin, total, square = pivot[mine, :], sums[mine, :], squares[mine, :]
            for j in range(part // 128):
                apart = slabs[number, mine, j * 128 : (j + 1) * 128].astype(f32) - origin
                total = total + apart
                square = square + apart * apart
            sums[mine, :] = total
            squares[mine, :] = square

    def normalise(t):
        @pl.loop(t * third, (t + 1) * third, step=32)
        def _(start_row):
            mine = pl.ds(pl.multiple_of(start_row, 32), 32)
            shift = jnp.sum(sums[mine, :], axis=1, keepdims=True) * (1.0 / model_width)
            square = jnp.sum(squares[mine, :], axis=1, keepdims=True) * (1.0 / model_width)
            inv = lax.rsqrt(jnp.maximum(square - shift * shift, 0.0) + EPS)
            inv = jnp.broadcast_to(inv, (32, 128))
            mean = pivot[mine, :] + shift
            for j in range(model_width // 128):
                w, lanes = j * 128 // part, slice(j * 128 % part, j * 128 % part + 128)
                value = (slabs[w, mine, lanes].astype(f32) - mean) * inv
                value = value.reshape(4, 8, 128) * gains[:, j * 128 : (j + 1) * 128][None]
                value = value + biases[:, j * 128 : (j + 1) * 128][None]
                normed[w, mine, lanes] = value.reshape(32, 128).astype(bf16)

    def from_core(h, du, dv):
        remote(("core", h, du, dv), block(h, du, dv, c=1 - core), partner).wait_recv()

    def multiply_pair(pair):
        acc[...] += jnp.dot(normed[pair], weights[pair], preferred_element_type=f32)

    def multiply(dy, what):
        for dx in OFFSETS:
            if (dx == 2 and what != "near") or (dx != 2 and what != "far"):
                from_core(0, dx, dy)
                from_core(1, dy, dx)
        first_pair = (y + dy + SIDE) % SIDE * 2
        if what == "row":
            pl.loop(first_pair, first_pair + 2)(multiply_pair)
        elif what == "near":
            multiply_pair(first_pair + x // 2)
        else:
            multiply_pair(first_pair + 1 - x // 2)

    for t in range(THIRDS):
        add_sums(z, t)

    seen = set()
    for event in arrivals_in_order():
        seen.add(event)
        if event[0] == "own on":
            h = event[1]
            arrive("own on", h, 1)
            arrive("own on", h, -1)
            start("row", h, 2, 1)
            start("row", h, 2, -1)
            start("core", h, 2, 0)
        elif event[0] == "row":
            arrive(*event)
            _, h, du, s = event
            start("row on", h, du, s)
            start("core", h, du, -s)
        elif event[0] == "row on":
            _, h, du = event
            arrive("row on", h, du, 1)
            arrive("row on", h, du, -1)
            start("core", h, du, 2)
        elif event[0] == "z":
            _, k, s, t = event
            z_copy(k, s, t).wait_recv()
            if k < 3 or (k == 3 and t in dict(last_parts(s))):
                z_copy(k + 1, s, t).start()
            if k < 4:
                add_sums((z - k * s + DEPTH) % DEPTH, t)
            elif all(("z", 4, d, t) in seen for d in (1, -1) if t in dict(last_parts(d))):
                add_sums((z + 4) % DEPTH, t)
                normalise(t)
        else:
            what, dy = event.split()
            multiply(int(dy), what)

    lanes = iota((1, width), 1) % HEAD
    rotated = [lanes[:, j * 128 : (j + 1) * 128] for j in range(width // 128)]
    for t in range(THIRDS):
        for r in range(req_count):
            here = pl.ds(t * third + r * CHIPS, CHIPS)
            there = pl.ds(r * fresh + t * CHIPS, CHIPS)
            cosine, sine = cosines[here, :], sines[here, :]
            for kind, ref in enumerate((q_ref, k_ref, v_ref)):
                for j in range(width // 128):
                    column = kind * width + j * 128
                    value = acc[here, column : column + 128]
                    if kind < 2:
                        near = jnp.where(
                            rotated[j] < turning,
                            pltpu.roll(value, 128 - turning, 1),
                            pltpu.roll(value, turning, 1),
                        )
                        value = jnp.where(rotated[j] < ROT, value * cosine + near * sine, value)
                    ref[there, j * 128 : (j + 1) * 128] = value.astype(bf16)

    def sent(kind, ref):
        name = ("z", 4, 1, 0) if kind == "z last" else next(n for n in NUMBER if n[0] == kind)
        remote(name, ref, partner).wait_send()

    sent("own", weights.at[0, pl.ds(0, 2 * depth), :])
    sent("own on", weights.at[0, pl.ds(0, depth), :])
    sent("row", weights.at[pl.ds(0, 2)])
    sent("row on", weights.at[0])
    sent("core", weights.at[pl.ds(0, 4)])
    sent("z", slabs.at[pl.ds(0, 6)])
    sent("z last", slabs.at[0])
    sent("swap", in1)
    sent("first", in1.at[pl.ds(0, CHIPS - 1)])
    sent("second", in1.at[pl.ds(0, CHIPS - 1)])


def project(lengths, x, w, group_of, gain, bias, col_bias):
    tokens, part = x.shape
    depth, cols = w.shape
    width = cols // 3
    lanes = tokens * part // (CHIPS * 8)
    f32, bf16 = jnp.float32, jnp.bfloat16
    out = jax.ShapeDtypeStruct((tokens, width), bf16)
    vmem = pl.BlockSpec(memory_space=pltpu.VMEM)
    smem = pl.BlockSpec(memory_space=pltpu.SMEM)
    anywhere = pl.BlockSpec(memory_space=pl.ANY)
    message = pltpu.VMEM((CHIPS, 8, lanes), bf16)
    wide = pltpu.VMEM((tokens, 128), f32)
    copies = pltpu.SemaphoreType.DMA((len(NUMBER),))
    return pl.pallas_call(
        project_kernel,
        out_shape=(out, out, out),
        in_specs=[smem, anywhere, anywhere, vmem, vmem, vmem, vmem],
        out_specs=(vmem, vmem, vmem),
        scratch_shapes=[
            pltpu.VMEM((tokens, part), bf16),
            pltpu.VMEM((depth, cols), bf16),
            pltpu.VMEM((CHIPS // 2, 4 * depth, cols), bf16),
            pltpu.VMEM((DEPTH, tokens, part), bf16),
            pltpu.VMEM((DEPTH, tokens, part), bf16),
            pltpu.VMEM((tokens, cols), f32),
            wide,
            wide,
            wide,
            wide,
            wide,
            pltpu.VMEM((8, part * DEPTH), f32),
            pltpu.VMEM((8, part * DEPTH), f32),
            message,
            message,
            message,
            message,
            message,
            pltpu.SemaphoreType.DMA((2,)),
            pltpu.SemaphoreType.DMA((len(SENDS),)),
            copies,
        ],
        compiler_params=pltpu.CompilerParams(
            collective_id=0, has_side_effects=True, vmem_limit_bytes=VMEM_BYTES
        ),
    )(lengths, x, w, group_of, gain, bias, col_bias)


def per_device(
    arrivals, group_of, lengths, page_table, ln_gain, ln_bias, w_qkv, qkv_bias, key_pool, value_pool
):
    req_count, fresh, part = arrivals.shape
    x = arrivals.reshape(req_count * fresh, part)
    q, k, v = project(lengths, x, w_qkv, group_of, ln_gain, ln_bias, qkv_bias)
    outs = attention(lengths, page_table, q, k, v, key_pool, value_pool)
    return tuple(a.reshape(req_count, fresh, -1) for a in outs)


def solution(mesh):
    in_specs = (
        P("req", None, "wgt"),
        P(),
        P("req"),
        P("req", None),
        P(),
        P(),
        P("req", "wgt"),
        P("wgt"),
        P("req", None, "wgt"),
        P("req", None, "wgt"),
    )
    out_specs = (P("req", None, "wgt"), P("req", None, "wgt"), P("req", None, "wgt"))
    return jax.shard_map(
        per_device, mesh=mesh, in_specs=in_specs, out_specs=out_specs, check_vma=False
    )
```

```python
import math

import jax
import jax.numpy as jnp
from jax import lax
from jax.experimental import pallas as pl
from jax.experimental.pallas import tpu as pltpu
from jax.sharding import PartitionSpec as P
import numpy as np

HEAD = 96
ROT = 24
EPS = 1e-05
CHUNK_PAGES = 4
VMEM_BYTES = 67043328


def attention_kernel(
    lengths, table, q_hbm, k_hbm, v_hbm, key_pool, value_pool, out_hbm, nk_hbm, nv_hbm,
    q_ref, k_ref, v_ref, out_ref, kbuf, vbuf, queries, scores, peaks, offsets, totals, mixed, work, sems, io,
):
    f32, bf16 = jnp.float32, jnp.bfloat16
    req_count, maxp = table.shape
    page, width = kbuf.shape[1], kbuf.shape[2]
    fresh = q_ref.shape[0] // req_count
    heads = width // HEAD
    rows = heads * fresh
    span = CHUNK_PAGES * page
    factor = math.log2(math.e) / math.sqrt(HEAD)
    low = -1e30

    loads = [
        pltpu.make_async_copy(source, target, io.at[n])
        for n, (source, target) in enumerate(((q_hbm, q_ref), (k_hbm, k_ref), (v_hbm, v_ref)))
    ]
    for copy in loads:
        copy.start()

    count = 0
    for r in range(req_count):
        chunks = (lengths[r] + (span - 1)) // span

        @pl.loop(0, chunks)
        def _(n):
            i = count + n
            work[0, i] = r
            work[1, i] = n
            for p in range(CHUNK_PAGES):
                number, slot = table[r, n * CHUNK_PAGES + p], i * CHUNK_PAGES + p
                pltpu.make_async_copy(key_pool.at[number], kbuf.at[slot], sems.at[0, i]).start()
                pltpu.make_async_copy(value_pool.at[number], vbuf.at[slot], sems.at[1, i]).start()

        count = count + chunks

    def pages(i):
        return pl.ds(i * CHUNK_PAGES, CHUNK_PAGES)

    def wait(pool, buffer, kind, i):
        pltpu.make_async_copy(pool.at[pl.ds(0, CHUNK_PAGES)], buffer.at[pages(i)], sems.at[kind, i]).wait()

    for copy in loads:
        copy.wait()
    stores = [
        pltpu.make_async_copy(k_ref, nk_hbm, io.at[3]),
        pltpu.make_async_copy(v_ref, nv_hbm, io.at[4]),
        pltpu.make_async_copy(out_ref, out_hbm, io.at[5]),
    ]
    stores[0].start()
    stores[1].start()

    iota = lambda shape, axis: lax.broadcasted_iota(jnp.int32, shape, axis)
    row_head = iota((rows, 256), 0) // fresh
    own_head = (iota((rows, 256), 1) + row_head // 2 * 128) // HEAD == row_head
    half_rows = rows // 2
    halves = ((slice(0, half_rows), slice(0, 256)), (slice(half_rows, rows), slice(128, 384)))
    causal = iota((rows, fresh), 0) % fresh >= iota((rows, fresh), 1)
    column = iota((1, span), 1)

    def fold(value, op):
        folded = value[:, :128]
        for n in range(1, value.shape[1] // 128):
            folded = op(folded, value[:, n * 128 : (n + 1) * 128])
        return folded

    across = (((1,), (1,)), ((), ()))

    def times_keys(query, keys):
        products = [
            lax.dot_general(query[group], keys[:, lanes], across, preferred_element_type=f32)
            for group, lanes in halves
        ]
        return jnp.concatenate(products, axis=0)

    def times_values(weights, values):
        weights = weights.astype(bf16)
        products = [
            jnp.dot(weights[group], values[:, lanes], preferred_element_type=f32)
            for group, lanes in halves
        ]
        return jnp.concatenate(products, axis=0)

    fresh_scores = []
    for r in range(req_count):
        mine = pl.ds(r * fresh, fresh)
        query = jnp.concatenate([q_ref[mine, lanes] for _, lanes in halves for _ in (0, 1)], axis=0)
        query = jnp.where(own_head, query, jnp.zeros_like(query))
        queries[r] = query
        own = times_keys(query, k_ref[mine, :])
        own = jnp.where(causal, own, low)
        fresh_scores.append(own)
        peaks[r] = jnp.broadcast_to(jnp.max(own, axis=1, keepdims=True), (rows, 128))
        totals[r] = jnp.zeros((rows, 128), f32)

    def over_chunks(step):
        @pl.loop(0, count // 2)
        def _(j):
            step((2 * j, 2 * j + 1))

        @pl.when(count % 2 == 1)
        def _():
            step((count - 1,))

    def first(chunks):
        for i in chunks:
            wait(key_pool, kbuf, 0, i)
        values = []
        for i in chunks:
            r, n = work[0, i], work[1, i]
            keys = kbuf[pages(i)].reshape(span, width)
            value = times_keys(queries[r], keys)
            values.append(value + jnp.where(column < lengths[r] - n * span, 0.0, low))
        for i, value in zip(chunks, values):
            r = work[0, i]
            scores[i] = value
            peaks[r] = jnp.maximum(peaks[r], fold(value, jnp.maximum))

    over_chunks(first)

    fresh_totals = []
    for r in range(req_count):
        mine = pl.ds(r * fresh, fresh)
        offset = jnp.max(peaks[r], axis=1, keepdims=True) * factor
        offsets[r] = jnp.broadcast_to(offset, (rows, 128))
        weights = jnp.exp2(fresh_scores[r] * factor - offset)
        mixed[r] = times_values(weights, v_ref[mine, :])
        fresh_totals.append(jnp.sum(weights, axis=1, keepdims=True))

    def second(chunks):
        for i in chunks:
            wait(value_pool, vbuf, 1, i)
        parts = []
        for i in chunks:
            r = work[0, i]
            values = vbuf[pages(i)].reshape(span, width)
            offset = jnp.concatenate([offsets[r]] * (span // 128), axis=1)
            weights = jnp.exp2(scores[i] * factor - offset)
            part = times_values(weights, values)
            parts.append((part, fold(weights, jnp.add)))
        for i, (part, total) in zip(chunks, parts):
            r = work[0, i]
            mixed[r] += part
            totals[r] += total

    over_chunks(second)

    for r in range(req_count):
        total = jnp.sum(totals[r], axis=1, keepdims=True) + fresh_totals[r]
        part = jnp.where(own_head, mixed[r] * (1.0 / total), 0.0)
        low_pair = part[:fresh] + part[fresh : 2 * fresh]
        high_pair = part[2 * fresh : 3 * fresh] + part[3 * fresh :]
        middle = low_pair[:, 128:] + high_pair[:, :128]
        value = jnp.concatenate([low_pair[:, :128], middle, high_pair[:, 128:]], axis=1)
        out_ref[pl.ds(r * fresh, fresh), :] = value.astype(out_ref.dtype)

    stores[2].start()
    for copy in stores:
        copy.wait()


def attention(lengths, table, q, k, v, key_pool, value_pool):
    rows, width = q.shape
    page = key_pool.shape[1]
    req_count, maxp = table.shape
    slots = req_count * maxp
    chunks = slots // CHUNK_PAGES
    wide = width // HEAD * (rows // req_count)
    f32, bf16 = jnp.float32, jnp.bfloat16
    out = jax.ShapeDtypeStruct((rows, width), bf16)
    smem = pl.BlockSpec(memory_space=pltpu.SMEM)
    anywhere = pl.BlockSpec(memory_space=pl.ANY)
    return pl.pallas_call(
        attention_kernel,
        out_shape=(out, out, out),
        in_specs=[smem, smem] + [anywhere] * 5,
        out_specs=(anywhere, anywhere, anywhere),
        scratch_shapes=[
            pltpu.VMEM((rows, width), bf16),
            pltpu.VMEM((rows, width), bf16),
            pltpu.VMEM((rows, width), bf16),
            pltpu.VMEM((rows, width), bf16),
            pltpu.VMEM((slots, page, width), bf16),
            pltpu.VMEM((slots, page, width), bf16),
            pltpu.VMEM((req_count, wide, 256), bf16),
            pltpu.VMEM((chunks, wide, CHUNK_PAGES * page), f32),
            pltpu.VMEM((req_count, wide, 128), f32),
            pltpu.VMEM((req_count, wide, 128), f32),
            pltpu.VMEM((req_count, wide, 128), f32),
            pltpu.VMEM((req_count, wide, 256), f32),
            pltpu.SMEM((2, chunks), jnp.int32),
            pltpu.SemaphoreType.DMA((2, chunks)),
            pltpu.SemaphoreType.DMA((6,)),
        ],
        compiler_params=pltpu.CompilerParams(vmem_limit_bytes=VMEM_BYTES),
    )(lengths, table, q, k, v, key_pool, value_pool)


MESH = pl.DeviceIdType.MESH
SIDE = 4
CHIPS = SIDE * SIDE
DEPTH = 8
OFFSETS = (0, -1, 1, 2)
THIRDS = 3


def last_parts(s):
    return ((0, None), (1, 0)) if s == 1 else ((2, None), (1, 1))


def copy_numbers():
    names = []
    for h in (0, 1):
        names += [("own", h, s) for s in (1, -1)]
        names += [("own on", h, s) for s in (1, -1)]
        names += [("row", h, du, s) for du in OFFSETS for s in (1, -1)]
        names += [("row on", h, du, s) for du in OFFSETS for s in (1, -1)]
        names += [("core", h, du, dv) for du in OFFSETS for dv in OFFSETS]
    for s in (1, -1):
        names += [("z", k, s, t) for k in (1, 2, 3) for t in range(THIRDS)]
        names += [("z", 4, s, t) for t, _ in last_parts(s)]
    names += [("swap",), ("first",), ("second",)]
    return {name: number for number, name in enumerate(names)}


NUMBER = copy_numbers()
SENDS = ("own", "own on", "row", "row on", "core", "z", "z last", "swap", "first", "second")


def send_number(name):
    return SENDS.index("z last" if name[:2] == ("z", 4) else name[0])


def arrivals_in_order():
    rows = lambda du: [("row", h, du, s) for h in (1, 0) for s in (1, -1)]
    rows_on = lambda du: [("row on", 1, du), ("row on", 0, du)]
    thirds = lambda k, *ts: [("z", k, s, t) for t in ts for s in (1, -1)]
    order = rows(0) + thirds(1, 0) + [("own on", 0), ("own on", 1)] + thirds(1, 1, 2)
    order += rows(-1) + thirds(2, 0, 1, 2) + rows(1) + thirds(3, 0) + rows_on(0) + thirds(3, 1, 2)
    order += rows(2) + [("z", 4, -1, 1), ("z", 4, 1, 0), ("z", 4, 1, 1), ("z", 4, -1, 2)]
    order += rows_on(-1) + ["row 0"] + rows_on(1) + ["row -1"] + rows_on(2) + ["row 1", "near 2", "far 2"]
    return order


def project_kernel(
    lengths_hbm, x_hbm, w_hbm, group_hbm, gain_hbm, bias_hbm, col_bias_hbm, q_hbm, k_hbm, v_hbm,
    lengths, x_ref, w_ref, group_ref, gain_ref, bias_ref, col_bias_ref, q_ref, k_ref, v_ref, weights, slabs, normed, acc, cosines, sines, pivot, sums, squares, gains, biases,
    out1, in1, swapped, out2, in2, load, send, recv,
):
    f32, bf16, i32 = jnp.float32, jnp.bfloat16, jnp.int32
    tokens, part = x_ref.shape
    depth, cols = w_ref.shape
    model_width = part * DEPTH
    req_count = lengths.shape[0]
    fresh = tokens // req_count
    half = part // 2
    third = tokens // THIRDS
    width = cols // 3
    rows_half, rows_sub = depth // 2, depth // 4
    me, z = lax.axis_index("req"), lax.axis_index("wgt")
    core = me % 2
    chip = me // 2
    y, x = chip // SIDE, chip % SIDE
    iota = lambda shape, axis: lax.broadcasted_iota(i32, shape, axis)

    def device(number, c=core):
        return (number * 2 + c, z)

    partner = device(chip, 1 - core)

    pairs = (
        (x_hbm, x_ref), (w_hbm, w_ref), (group_hbm, group_ref), (lengths_hbm, lengths),
        (gain_hbm, gain_ref), (bias_hbm, bias_ref), (col_bias_hbm, col_bias_ref),
    )
    loads = [pltpu.make_async_copy(a, b, load.at[n]) for n, (a, b) in enumerate(pairs)]
    loads[0].start()

    barrier = pltpu.get_barrier_semaphore()

    for d in range(1, CHIPS):
        pl.semaphore_signal(barrier, 1, device_id=device((chip + d) % CHIPS), device_id_type=MESH)

    pl.semaphore_signal(barrier, 1, device_id=partner, device_id_type=MESH)
    for s in (1, DEPTH - 1):
        pl.semaphore_signal(barrier, 1, device_id=(me, (z + s) % DEPTH), device_id_type=MESH)

    for copy in loads[1:]:
        copy.start()

    loads[0].wait()
    m, n = iota((CHIPS * 8, tokens), 0), iota((CHIPS * 8, tokens), 1)
    for t in range(THIRDS):
        take = (m % 8) // 2 * fresh + t * CHIPS + m // 8 == n
        piece = jnp.zeros((CHIPS * 8, half), f32)
        for h in (0, 1):
            chosen = jnp.where(take & (m % 2 == h), 1.0, 0.0).astype(bf16)
            piece += jnp.dot(chosen, x_ref[:, h * half : (h + 1) * half], preferred_element_type=f32)
        out1[:, :, t * half : (t + 1) * half] = piece.reshape(CHIPS, 8, half).astype(bf16)
    in1[chip] = out1[chip]

    pl.semaphore_wait(barrier, CHIPS - 1 + 3)

    def spread(name, source, target):
        for d in range(1, CHIPS):
            other = (chip + d) % CHIPS
            remote((name,), source.at[other], device(other), target.at[chip]).start()

    def gathered(name, target):
        ref = target.at[pl.ds(0, CHIPS - 1)]
        remote((name,), ref, partner).wait_recv()

    def remote(name, ref, target, dst=None):
        return pltpu.make_async_remote_copy(
            src_ref=ref,
            dst_ref=ref if dst is None else dst,
            send_sem=send.at[send_number(name)],
            recv_sem=recv.at[NUMBER[name]],
            device_id=target,
            device_id_type=MESH,
        )

    spread("first", out1, in1)

    def by_kind(value):
        heads = range(width // HEAD)
        return jnp.concatenate(
            [
                value[:, (h * 3 + kind) * HEAD : (h * 3 + kind + 1) * HEAD]
                for kind in range(3)
                for h in heads
            ],
            axis=1,
        )

    def place(number, c):
        return number // 2, (number % 2) * (2 * depth) + c * depth

    loads[1].wait()
    own_pair, own_row = place(chip, core)
    weights[own_pair, pl.ds(pl.multiple_of(own_row, 64), depth), :] = by_kind(w_ref[...])

    where = {0: (x, y), 1: (y, x)}

    def chip_at(h, du, dv):
        u, v = where[h]
        u, v = (u + du + SIDE) % SIDE, (v + dv + SIDE) % SIDE
        return v * SIDE + u if h == 0 else u * SIDE + v

    def block(h, du, dv, c=core, sub=None):
        pair, row = place(chip_at(h, du, dv), c)
        row = row + h * rows_half + (0 if sub in (None, 1) else rows_sub)
        return weights.at[pair, pl.ds(pl.multiple_of(row, 16), rows_half if sub is None else rows_sub), :]

    def weight_copy(name):
        kind, h = name[0], name[1]
        if kind == "own":
            return remote(name, block(h, 0, 0), device(chip_at(h, name[2], 0)))
        if kind == "own on":
            s = name[2]
            return remote(name, block(h, -s, 0, sub=s), device(chip_at(h, s, 0)))
        if kind == "row":
            du, s = name[2], name[3]
            return remote(name, block(h, du, 0), device(chip_at(h, 0, s)))
        if kind == "row on":
            du, s = name[2], name[3]
            return remote(name, block(h, du, -s, sub=s), device(chip_at(h, 0, s)))
        du, dv = name[2], name[3]
        return remote(name, block(h, du, dv), partner)

    def start(*name):
        weight_copy(name).start()

    def arrive(*name):
        weight_copy(name).wait_recv()

    for h in (0, 1):
        for s in (1, -1):
            start("own", h, s)
    for h in (0, 1):
        start("core", h, 0, 0)

    a, b = iota((CHIPS * 8, CHIPS * 8), 0), iota((CHIPS * 8, CHIPS * 8), 1)
    loads[2].wait()
    groups = group_ref[...].reshape(1, -1)
    group_row = jnp.broadcast_to(groups, a.shape)
    group_col = jnp.sum(jnp.where(a == b, group_row, 0), axis=1, keepdims=True)
    rank = jnp.sum(jnp.where((group_col == group_row) & (a < b), 1, 0), axis=0, keepdims=True)
    slot_row = groups * req_count + rank
    slot_col = jnp.sum(jnp.where(a == b, jnp.broadcast_to(slot_row, a.shape), 0), axis=1, keepdims=True)

    def selector(c):
        arriving = (b // 8 * 2 + c) * req_count + b % 8 // 2
        slot = jnp.sum(jnp.where(a == arriving, slot_col, 0), axis=0, keepdims=True)
        wanted = (a // 8 * 2 + core) * req_count + a % 8 // 2
        return jnp.where((wanted == slot) & (a % 2 == b % 2), 1.0, 0.0).astype(bf16)

    pick_own, pick_other = selector(core), selector(1 - core)

    gathered("first", in1)

    swap = remote(("swap",), in1, partner, swapped)
    swap.start()

    def flat(ref):
        return ref[...].astype(f32).reshape(CHIPS * 8, THIRDS * half).astype(bf16)

    mixed = jnp.dot(pick_own, flat(in1), preferred_element_type=f32)
    swap.wait_recv()
    mixed = mixed + jnp.dot(pick_other, flat(swapped), preferred_element_type=f32)
    out2[...] = mixed.reshape(CHIPS, 8, THIRDS * half).astype(bf16)
    in2[chip] = out2[chip]

    spread("second", out2, in2)

    for h in (0, 1):
        for s in (1, -1):
            start("row", h, 0, s)

    for copy in loads[3:]:
        copy.wait()
    gains[...] = jnp.broadcast_to(gain_ref[...].astype(f32).reshape(1, -1), gains.shape)
    biases[...] = jnp.broadcast_to(bias_ref[...].astype(f32).reshape(1, -1), biases.shape)
    acc[...] = jnp.broadcast_to(by_kind(col_bias_ref[...].astype(f32).reshape(1, -1)), acc.shape)

    lane = iota((1, 128), 1) % 32
    turning = ROT // 2
    inverse = jnp.zeros((1, 128), f32)
    for i in range(turning):
        value = float(np.float32(10000.0) ** np.float32(-2.0 * i / ROT))
        inverse = jnp.where((lane == i) | (lane == i + turning), value, inverse)
    row = iota((tokens, 1), 0)
    request = row % third // CHIPS
    position = row // third * CHIPS + row % CHIPS
    for r in range(req_count):
        position = position + jnp.where(request == r, lengths[r], 0)
    angle = position.astype(f32) * inverse
    cosines[...] = jnp.cos(angle)
    sine = jnp.sin(angle)
    sines[...] = jnp.where(lane < turning, -sine, sine)

    for h in (0, 1):
        for s in (1, -1):
            arrive("own", h, s)
    for h in (0, 1):
        for s in (1, -1):
            start("own on", h, s)
    for h in (0, 1):
        for s in (1, -1):
            start("core", h, -s, 0)
    for s in (1, -1):
        for h in (0, 1):
            start("row", h, -s, 1)
            start("row", h, -s, -1)

    gathered("second", in2)

    m, n = iota((third, CHIPS * 8), 0), iota((third, CHIPS * 8), 1)
    pieces = flat(in2)
    for h in (0, 1):
        chosen = jnp.where(m % CHIPS * 8 + m // CHIPS * 2 + h == n, 1.0, 0.0).astype(bf16)
        rows = jnp.dot(chosen, pieces, preferred_element_type=f32).astype(bf16)
        for t in range(THIRDS):
            slabs[z, pl.ds(t * third, third), h * half : (h + 1) * half] = rows[:, t * half : (t + 1) * half]

    def slab(k, s, t, piece=None):
        ref = slabs.at[(z - k * s + DEPTH) % DEPTH]
        if piece is None:
            return ref.at[pl.ds(t * third, third), :]
        return ref.at[pl.ds(t * third + piece * (third // 2), third // 2), :]

    def z_copy(k, s, t):
        piece = dict(last_parts(s))[t] if k == 4 else None
        return remote(("z", k, s, t), slab(k - 1, s, t, piece), (me, (z + s + DEPTH) % DEPTH))

    for t in range(THIRDS):
        for s in (1, -1):
            z_copy(1, s, t).start()

    def folded(value):
        total = value[:, :128]
        for j in range(1, part // 128):
            total = total + value[:, j * 128 : (j + 1) * 128]
        return total

    for t in range(THIRDS):
        mine = pl.ds(t * third, third)
        own = jnp.sum(folded(slabs[z, mine, :].astype(f32)), axis=1, keepdims=True) * (1.0 / part)
        pivot[mine, :] = jnp.broadcast_to(own, (third, 128))
    sums[...] = jnp.zeros_like(sums)
    squares[...] = jnp.zeros_like(squares)

    def add_sums(number, t):
        @pl.loop(t * third, (t + 1) * third, step=32)
        def _(start_row):
            mine = pl.ds(pl.multiple_of(start_row, 32), 32)
            origin, total, square = pivot[mine, :], sums[mine, :], squares[mine, :]
            for j in range(part // 128):
                apart = slabs[number, mine, j * 128 : (j + 1) * 128].astype(f32) - origin
                total = total + apart
                square = square + apart * apart
            sums[mine, :] = total
            squares[mine, :] = square

    def normalise(t):
        @pl.loop(t * third, (t + 1) * third, step=32)
        def _(start_row):
            mine = pl.ds(pl.multiple_of(start_row, 32), 32)
            shift = jnp.sum(sums[mine, :], axis=1, keepdims=True) * (1.0 / model_width)
            square = jnp.sum(squares[mine, :], axis=1, keepdims=True) * (1.0 / model_width)
            inv = lax.rsqrt(jnp.maximum(square - shift * shift, 0.0) + EPS)
            inv = jnp.broadcast_to(inv, (32, 128))
            mean = pivot[mine, :] + shift
            for j in range(model_width // 128):
                w, lanes = j * 128 // part, slice(j * 128 % part, j * 128 % part + 128)
                value = (slabs[w, mine, lanes].astype(f32) - mean) * inv
                value = value.reshape(4, 8, 128) * gains[:, j * 128 : (j + 1) * 128][None]
                value = value + biases[:, j * 128 : (j + 1) * 128][None]
                normed[w, mine, lanes] = value.reshape(32, 128).astype(bf16)

    def from_core(h, du, dv):
        remote(("core", h, du, dv), block(h, du, dv, c=1 - core), partner).wait_recv()

    def multiply_pair(pair):
        acc[...] += jnp.dot(normed[pair], weights[pair], preferred_element_type=f32)

    def multiply(dy, what):
        for dx in OFFSETS:
            if (dx == 2 and what != "near") or (dx != 2 and what != "far"):
                from_core(0, dx, dy)
                from_core(1, dy, dx)
        first_pair = (y + dy + SIDE) % SIDE * 2
        if what == "row":
            pl.loop(first_pair, first_pair + 2)(multiply_pair)
        elif what == "near":
            multiply_pair(first_pair + x // 2)
        else:
            multiply_pair(first_pair + 1 - x // 2)

    for t in range(THIRDS):
        add_sums(z, t)

    seen = set()
    for event in arrivals_in_order():
        seen.add(event)
        if event[0] == "own on":
            h = event[1]
            arrive("own on", h, 1)
            arrive("own on", h, -1)
            start("row", h, 2, 1)
            start("row", h, 2, -1)
            start("core", h, 2, 0)
        elif event[0] == "row":
            arrive(*event)
            _, h, du, s = event
            start("row on", h, du, s)
            start("core", h, du, -s)
        elif event[0] == "row on":
            _, h, du = event
            arrive("row on", h, du, 1)
            arrive("row on", h, du, -1)
            start("core", h, du, 2)
        elif event[0] == "z":
            _, k, s, t = event
            z_copy(k, s, t).wait_recv()
            if k < 3 or (k == 3 and t in dict(last_parts(s))):
                z_copy(k + 1, s, t).start()
            if k < 4:
                add_sums((z - k * s + DEPTH) % DEPTH, t)
            elif all(("z", 4, d, t) in seen for d in (1, -1) if t in dict(last_parts(d))):
                add_sums((z + 4) % DEPTH, t)
                normalise(t)
        else:
            what, dy = event.split()
            multiply(int(dy), what)

    lanes = iota((1, width), 1) % HEAD
    rotated = [lanes[:, j * 128 : (j + 1) * 128] for j in range(width // 128)]
    for t in range(THIRDS):
        for r in range(req_count):
            here = pl.ds(t * third + r * CHIPS, CHIPS)
            there = pl.ds(r * fresh + t * CHIPS, CHIPS)
            cosine, sine = cosines[here, :], sines[here, :]
            for kind, ref in enumerate((q_ref, k_ref, v_ref)):
                for j in range(width // 128):
                    column = kind * width + j * 128
                    value = acc[here, column : column + 128]
                    if kind < 2:
                        near = jnp.where(
                            rotated[j] < turning,
                            pltpu.roll(value, 128 - turning, 1),
                            pltpu.roll(value, turning, 1),
                        )
                        value = jnp.where(rotated[j] < ROT, value * cosine + near * sine, value)
                    ref[there, j * 128 : (j + 1) * 128] = value.astype(bf16)

    results = [
        pltpu.make_async_copy(a, b, load.at[n])
        for n, (a, b) in enumerate(((q_ref, q_hbm), (k_ref, k_hbm), (v_ref, v_hbm)))
    ]
    for copy in results:
        copy.start()

    def sent(kind, ref):
        name = ("z", 4, 1, 0) if kind == "z last" else next(n for n in NUMBER if n[0] == kind)
        remote(name, ref, partner).wait_send()

    sent("own", weights.at[0, pl.ds(0, 2 * depth), :])
    sent("own on", weights.at[0, pl.ds(0, depth), :])
    sent("row", weights.at[pl.ds(0, 2)])
    sent("row on", weights.at[0])
    sent("core", weights.at[pl.ds(0, 4)])
    sent("z", slabs.at[pl.ds(0, 6)])
    sent("z last", slabs.at[0])
    sent("swap", in1)
    sent("first", in1.at[pl.ds(0, CHIPS - 1)])
    sent("second", in1.at[pl.ds(0, CHIPS - 1)])
    for copy in results:
        copy.wait()


def project(lengths, x, w, group_of, gain, bias, col_bias):
    tokens, part = x.shape
    depth, cols = w.shape
    width = cols // 3
    lanes = tokens * part // (CHIPS * 8)
    f32, bf16 = jnp.float32, jnp.bfloat16
    out = jax.ShapeDtypeStruct((tokens, width), bf16)
    anywhere = pl.BlockSpec(memory_space=pl.ANY)
    message = pltpu.VMEM((CHIPS, 8, lanes), bf16)
    wide = pltpu.VMEM((tokens, 128), f32)
    copies = pltpu.SemaphoreType.DMA((len(NUMBER),))
    return pl.pallas_call(
        project_kernel,
        out_shape=(out, out, out),
        in_specs=[anywhere] * 7,
        out_specs=(anywhere, anywhere, anywhere),
        scratch_shapes=[
            pltpu.SMEM(lengths.shape, jnp.int32),
            pltpu.VMEM((tokens, part), bf16),
            pltpu.VMEM((depth, cols), bf16),
            pltpu.VMEM(group_of.shape, jnp.int32),
            pltpu.VMEM(gain.shape, bf16),
            pltpu.VMEM(bias.shape, bf16),
            pltpu.VMEM(col_bias.shape, bf16),
            pltpu.VMEM((tokens, width), bf16),
            pltpu.VMEM((tokens, width), bf16),
            pltpu.VMEM((tokens, width), bf16),
            pltpu.VMEM((CHIPS // 2, 4 * depth, cols), bf16),
            pltpu.VMEM((DEPTH, tokens, part), bf16),
            pltpu.VMEM((DEPTH, tokens, part), bf16),
            pltpu.VMEM((tokens, cols), f32),
            wide,
            wide,
            wide,
            wide,
            wide,
            pltpu.VMEM((8, part * DEPTH), f32),
            pltpu.VMEM((8, part * DEPTH), f32),
            message,
            message,
            message,
            message,
            message,
            pltpu.SemaphoreType.DMA((7,)),
            pltpu.SemaphoreType.DMA((len(SENDS),)),
            copies,
        ],
        compiler_params=pltpu.CompilerParams(
            collective_id=0, has_side_effects=True, vmem_limit_bytes=VMEM_BYTES
        ),
    )(lengths, x, w, group_of, gain, bias, col_bias)


def per_device(
    arrivals, group_of, lengths, page_table, ln_gain, ln_bias, w_qkv, qkv_bias, key_pool, value_pool
):
    req_count, fresh, part = arrivals.shape
    x = arrivals.reshape(req_count * fresh, part)
    q, k, v = project(lengths, x, w_qkv, group_of, ln_gain, ln_bias, qkv_bias)
    outs = attention(lengths, page_table, q, k, v, key_pool, value_pool)
    return tuple(a.reshape(req_count, fresh, -1) for a in outs)


def solution(mesh):
    in_specs = (
        P("req", None, "wgt"),
        P(),
        P("req"),
        P("req", None),
        P(),
        P(),
        P("req", "wgt"),
        P("wgt"),
        P("req", None, "wgt"),
        P("req", None, "wgt"),
    )
    out_specs = (P("req", None, "wgt"), P("req", None, "wgt"), P("req", None, "wgt"))
    return jax.shard_map(
        per_device, mesh=mesh, in_specs=in_specs, out_specs=out_specs, check_vma=False
    )
```

```python
import math

import jax
import jax.numpy as jnp
from jax import lax
from jax.experimental import pallas as pl
from jax.experimental.pallas import tpu as pltpu
from jax.sharding import PartitionSpec as P
import numpy as np

HEAD = 96
ROT = 24
EPS = 1e-05
CHUNK_PAGES = 4
VMEM_BYTES = 67043328


def attention_kernel(
    lengths, table, q_ref, k_ref, v_ref, key_pool, value_pool, out_hbm, nk_hbm, nv_hbm,
    out_ref, queries, scores, peaks, offsets, totals, mixed, work, io,
):
    f32, bf16 = jnp.float32, jnp.bfloat16
    req_count, maxp = table.shape
    page, width = key_pool.shape[1], key_pool.shape[2]
    fresh = q_ref.shape[0] // req_count
    heads = width // HEAD
    rows = heads * fresh
    span = CHUNK_PAGES * page
    factor = math.log2(math.e) / math.sqrt(HEAD)
    low = -1e30

    count = 0
    for r in range(req_count):
        chunks = (lengths[r] + (span - 1)) // span

        @pl.loop(0, chunks)
        def _(n):
            i = count + n
            work[0, i] = r
            work[1, i] = n

        count = count + chunks

    def chunk(pool, i):
        r, n = work[0, i], work[1, i]
        pages = [pool[table[r, n * CHUNK_PAGES + p]] for p in range(CHUNK_PAGES)]
        return jnp.concatenate(pages, axis=0)

    stores = [
        pltpu.make_async_copy(k_ref, nk_hbm, io.at[0]),
        pltpu.make_async_copy(v_ref, nv_hbm, io.at[1]),
        pltpu.make_async_copy(out_ref, out_hbm, io.at[2]),
    ]
    stores[0].start()
    stores[1].start()

    iota = lambda shape, axis: lax.broadcasted_iota(jnp.int32, shape, axis)
    row_head = iota((rows, 256), 0) // fresh
    own_head = (iota((rows, 256), 1) + row_head // 2 * 128) // HEAD == row_head
    half_rows = rows // 2
    halves = ((slice(0, half_rows), slice(0, 256)), (slice(half_rows, rows), slice(128, 384)))
    causal = iota((rows, fresh), 0) % fresh >= iota((rows, fresh), 1)
    column = iota((1, span), 1)

    def fold(value, op):
        folded = value[:, :128]
        for n in range(1, value.shape[1] // 128):
            folded = op(folded, value[:, n * 128 : (n + 1) * 128])
        return folded

    across = (((1,), (1,)), ((), ()))

    def times_keys(query, keys):
        products = [
            lax.dot_general(query[group], keys[:, lanes], across, preferred_element_type=f32)
            for group, lanes in halves
        ]
        return jnp.concatenate(products, axis=0)

    def times_values(weights, values):
        weights = weights.astype(bf16)
        products = [
            jnp.dot(weights[group], values[:, lanes], preferred_element_type=f32)
            for group, lanes in halves
        ]
        return jnp.concatenate(products, axis=0)

    fresh_scores = []
    for r in range(req_count):
        mine = pl.ds(r * fresh, fresh)
        query = jnp.concatenate([q_ref[mine, lanes] for _, lanes in halves for _ in (0, 1)], axis=0)
        query = jnp.where(own_head, query, jnp.zeros_like(query))
        queries[r] = query
        own = times_keys(query, k_ref[mine, :])
        own = jnp.where(causal, own, low)
        fresh_scores.append(own)
        peaks[r] = jnp.broadcast_to(jnp.max(own, axis=1, keepdims=True), (rows, 128))
        totals[r] = jnp.zeros((rows, 128), f32)

    def over_chunks(step):
        @pl.loop(0, count // 2)
        def _(j):
            step((2 * j, 2 * j + 1))

        @pl.when(count % 2 == 1)
        def _():
            step((count - 1,))

    def first(chunks):
        values = []
        for i in chunks:
            r, n = work[0, i], work[1, i]
            keys = chunk(key_pool, i)
            value = times_keys(queries[r], keys)
            values.append(value + jnp.where(column < lengths[r] - n * span, 0.0, low))
        for i, value in zip(chunks, values):
            r = work[0, i]
            scores[i] = value
            peaks[r] = jnp.maximum(peaks[r], fold(value, jnp.maximum))

    over_chunks(first)

    fresh_totals = []
    for r in range(req_count):
        mine = pl.ds(r * fresh, fresh)
        offset = jnp.max(peaks[r], axis=1, keepdims=True) * factor
        offsets[r] = jnp.broadcast_to(offset, (rows, 128))
        weights = jnp.exp2(fresh_scores[r] * factor - offset)
        mixed[r] = times_values(weights, v_ref[mine, :])
        fresh_totals.append(jnp.sum(weights, axis=1, keepdims=True))

    def second(chunks):
        parts = []
        for i in chunks:
            r = work[0, i]
            values = chunk(value_pool, i)
            offset = jnp.concatenate([offsets[r]] * (span // 128), axis=1)
            weights = jnp.exp2(scores[i] * factor - offset)
            part = times_values(weights, values)
            parts.append((part, fold(weights, jnp.add)))
        for i, (part, total) in zip(chunks, parts):
            r = work[0, i]
            mixed[r] += part
            totals[r] += total

    over_chunks(second)

    for r in range(req_count):
        total = jnp.sum(totals[r], axis=1, keepdims=True) + fresh_totals[r]
        part = jnp.where(own_head, mixed[r] * (1.0 / total), 0.0)
        low_pair = part[:fresh] + part[fresh : 2 * fresh]
        high_pair = part[2 * fresh : 3 * fresh] + part[3 * fresh :]
        middle = low_pair[:, 128:] + high_pair[:, :128]
        value = jnp.concatenate([low_pair[:, :128], middle, high_pair[:, 128:]], axis=1)
        out_ref[pl.ds(r * fresh, fresh), :] = value.astype(out_ref.dtype)

    stores[2].start()
    for copy in stores:
        copy.wait()


def attention(lengths, table, q, k, v, key_pool, value_pool):
    rows, width = q.shape
    page = key_pool.shape[1]
    req_count, maxp = table.shape
    chunks = req_count * maxp // CHUNK_PAGES
    wide = width // HEAD * (rows // req_count)
    f32, bf16 = jnp.float32, jnp.bfloat16
    out = jax.ShapeDtypeStruct((rows, width), bf16)
    smem = pl.BlockSpec(memory_space=pltpu.SMEM)
    vmem = pl.BlockSpec(memory_space=pltpu.VMEM)
    anywhere = pl.BlockSpec(memory_space=pl.ANY)
    return pl.pallas_call(
        attention_kernel,
        out_shape=(out, out, out),
        in_specs=[smem, smem] + [vmem] * 5,
        out_specs=(anywhere, anywhere, anywhere),
        scratch_shapes=[
            pltpu.VMEM((rows, width), bf16),
            pltpu.VMEM((req_count, wide, 256), bf16),
            pltpu.VMEM((chunks, wide, CHUNK_PAGES * page), f32),
            pltpu.VMEM((req_count, wide, 128), f32),
            pltpu.VMEM((req_count, wide, 128), f32),
            pltpu.VMEM((req_count, wide, 128), f32),
            pltpu.VMEM((req_count, wide, 256), f32),
            pltpu.SMEM((2, chunks), jnp.int32),
            pltpu.SemaphoreType.DMA((3,)),
        ],
        compiler_params=pltpu.CompilerParams(vmem_limit_bytes=30 << 20),
    )(lengths, table, q, k, v, key_pool, value_pool)


MESH = pl.DeviceIdType.MESH
SIDE = 4
CHIPS = SIDE * SIDE
DEPTH = 8
OFFSETS = (0, -1, 1, 2)
THIRDS = 3


def last_parts(s):
    return ((0, None), (1, 0)) if s == 1 else ((2, None), (1, 1))


def copy_numbers():
    names = []
    for h in (0, 1):
        names += [("own", h, s) for s in (1, -1)]
        names += [("own on", h, s) for s in (1, -1)]
        names += [("row", h, du, s) for du in OFFSETS for s in (1, -1)]
        names += [("row on", h, du, s) for du in OFFSETS for s in (1, -1)]
        names += [("core", h, du, dv) for du in OFFSETS for dv in OFFSETS]
    for s in (1, -1):
        names += [("z", k, s, t) for k in (1, 2, 3) for t in range(THIRDS)]
        names += [("z", 4, s, t) for t, _ in last_parts(s)]
    names += [("swap",), ("first",), ("second",)]
    return {name: number for number, name in enumerate(names)}


NUMBER = copy_numbers()
SENDS = ("own", "own on", "row", "row on", "core", "z", "z last", "swap", "first", "second")


def send_number(name):
    return SENDS.index("z last" if name[:2] == ("z", 4) else name[0])


def arrivals_in_order():
    rows = lambda du: [("row", h, du, s) for h in (1, 0) for s in (1, -1)]
    rows_on = lambda du: [("row on", 1, du), ("row on", 0, du)]
    thirds = lambda k, *ts: [("z", k, s, t) for t in ts for s in (1, -1)]
    order = rows(0) + thirds(1, 0) + [("own on", 0), ("own on", 1)] + thirds(1, 1, 2)
    order += rows(-1) + thirds(2, 0, 1, 2) + rows(1) + thirds(3, 0) + rows_on(0) + thirds(3, 1, 2)
    order += rows(2) + [("z", 4, -1, 1), ("z", 4, 1, 0), ("z", 4, 1, 1), ("z", 4, -1, 2)]
    order += rows_on(-1) + ["row 0"] + rows_on(1) + ["row -1"] + rows_on(2) + ["row 1", "near 2", "far 2"]
    return order


def project_kernel(
    lengths_hbm, x_hbm, w_hbm, group_hbm, gain_hbm, bias_hbm, col_bias_hbm, q_ref, k_ref, v_ref,
    lengths, x_ref, w_ref, group_ref, gain_ref, bias_ref, col_bias_ref, weights, slabs, normed, acc, cosines, sines, pivot, sums, squares, gains, biases,
    out1, in1, swapped, out2, in2, load, send, recv,
):
    f32, bf16, i32 = jnp.float32, jnp.bfloat16, jnp.int32
    tokens, part = x_ref.shape
    depth, cols = w_ref.shape
    model_width = part * DEPTH
    req_count = lengths.shape[0]
    fresh = tokens // req_count
    half = part // 2
    third = tokens // THIRDS
    width = cols // 3
    rows_half, rows_sub = depth // 2, depth // 4
    me, z = lax.axis_index("req"), lax.axis_index("wgt")
    core = me % 2
    chip = me // 2
    y, x = chip // SIDE, chip % SIDE
    iota = lambda shape, axis: lax.broadcasted_iota(i32, shape, axis)

    def device(number, c=core):
        return (number * 2 + c, z)

    partner = device(chip, 1 - core)

    pairs = (
        (x_hbm, x_ref), (w_hbm, w_ref), (group_hbm, group_ref), (lengths_hbm, lengths),
        (gain_hbm, gain_ref), (bias_hbm, bias_ref), (col_bias_hbm, col_bias_ref),
    )
    loads = [pltpu.make_async_copy(a, b, load.at[n]) for n, (a, b) in enumerate(pairs)]
    loads[0].start()

    barrier = pltpu.get_barrier_semaphore()

    for d in range(1, CHIPS):
        pl.semaphore_signal(barrier, 1, device_id=device((chip + d) % CHIPS), device_id_type=MESH)

    pl.semaphore_signal(barrier, 1, device_id=partner, device_id_type=MESH)
    for s in (1, DEPTH - 1):
        pl.semaphore_signal(barrier, 1, device_id=(me, (z + s) % DEPTH), device_id_type=MESH)

    for copy in loads[1:]:
        copy.start()

    loads[0].wait()
    m, n = iota((CHIPS * 8, tokens), 0), iota((CHIPS * 8, tokens), 1)
    for t in range(THIRDS):
        take = (m % 8) // 2 * fresh + t * CHIPS + m // 8 == n
        piece = jnp.zeros((CHIPS * 8, half), f32)
        for h in (0, 1):
            chosen = jnp.where(take & (m % 2 == h), 1.0, 0.0).astype(bf16)
            piece += jnp.dot(chosen, x_ref[:, h * half : (h + 1) * half], preferred_element_type=f32)
        out1[:, :, t * half : (t + 1) * half] = piece.reshape(CHIPS, 8, half).astype(bf16)
    in1[chip] = out1[chip]

    pl.semaphore_wait(barrier, CHIPS - 1 + 3)

    def spread(name, source, target):
        for d in range(1, CHIPS):
            other = (chip + d) % CHIPS
            remote((name,), source.at[other], device(other), target.at[chip]).start()

    def gathered(name, target):
        ref = target.at[pl.ds(0, CHIPS - 1)]
        remote((name,), ref, partner).wait_recv()

    def remote(name, ref, target, dst=None):
        return pltpu.make_async_remote_copy(
            src_ref=ref,
            dst_ref=ref if dst is None else dst,
            send_sem=send.at[send_number(name)],
            recv_sem=recv.at[NUMBER[name]],
            device_id=target,
            device_id_type=MESH,
        )

    spread("first", out1, in1)

    def by_kind(value):
        heads = range(width // HEAD)
        return jnp.concatenate(
            [
                value[:, (h * 3 + kind) * HEAD : (h * 3 + kind + 1) * HEAD]
                for kind in range(3)
                for h in heads
            ],
            axis=1,
        )

    def place(number, c):
        return number // 2, (number % 2) * (2 * depth) + c * depth

    loads[1].wait()
    own_pair, own_row = place(chip, core)
    weights[own_pair, pl.ds(pl.multiple_of(own_row, 64), depth), :] = by_kind(w_ref[...])

    where = {0: (x, y), 1: (y, x)}

    def chip_at(h, du, dv):
        u, v = where[h]
        u, v = (u + du + SIDE) % SIDE, (v + dv + SIDE) % SIDE
        return v * SIDE + u if h == 0 else u * SIDE + v

    def block(h, du, dv, c=core, sub=None):
        pair, row = place(chip_at(h, du, dv), c)
        row = row + h * rows_half + (0 if sub in (None, 1) else rows_sub)
        return weights.at[pair, pl.ds(pl.multiple_of(row, 16), rows_half if sub is None else rows_sub), :]

    def weight_copy(name):
        kind, h = name[0], name[1]
        if kind == "own":
            return remote(name, block(h, 0, 0), device(chip_at(h, name[2], 0)))
        if kind == "own on":
            s = name[2]
            return remote(name, block(h, -s, 0, sub=s), device(chip_at(h, s, 0)))
        if kind == "row":
            du, s = name[2], name[3]
            return remote(name, block(h, du, 0), device(chip_at(h, 0, s)))
        if kind == "row on":
            du, s = name[2], name[3]
            return remote(name, block(h, du, -s, sub=s), device(chip_at(h, 0, s)))
        du, dv = name[2], name[3]
        return remote(name, block(h, du, dv), partner)

    def start(*name):
        weight_copy(name).start()

    def arrive(*name):
        weight_copy(name).wait_recv()

    for h in (0, 1):
        for s in (1, -1):
            start("own", h, s)
    for h in (0, 1):
        start("core", h, 0, 0)

    a, b = iota((CHIPS * 8, CHIPS * 8), 0), iota((CHIPS * 8, CHIPS * 8), 1)
    loads[2].wait()
    groups = group_ref[...].reshape(1, -1)
    group_row = jnp.broadcast_to(groups, a.shape)
    group_col = jnp.sum(jnp.where(a == b, group_row, 0), axis=1, keepdims=True)
    rank = jnp.sum(jnp.where((group_col == group_row) & (a < b), 1, 0), axis=0, keepdims=True)
    slot_row = groups * req_count + rank
    slot_col = jnp.sum(jnp.where(a == b, jnp.broadcast_to(slot_row, a.shape), 0), axis=1, keepdims=True)

    def selector(c):
        arriving = (b // 8 * 2 + c) * req_count + b % 8 // 2
        slot = jnp.sum(jnp.where(a == arriving, slot_col, 0), axis=0, keepdims=True)
        wanted = (a // 8 * 2 + core) * req_count + a % 8 // 2
        return jnp.where((wanted == slot) & (a % 2 == b % 2), 1.0, 0.0).astype(bf16)

    pick_own, pick_other = selector(core), selector(1 - core)

    gathered("first", in1)

    swap = remote(("swap",), in1, partner, swapped)
    swap.start()

    def flat(ref):
        return ref[...].astype(f32).reshape(CHIPS * 8, THIRDS * half).astype(bf16)

    mixed = jnp.dot(pick_own, flat(in1), preferred_element_type=f32)
    swap.wait_recv()
    mixed = mixed + jnp.dot(pick_other, flat(swapped), preferred_element_type=f32)
    out2[...] = mixed.reshape(CHIPS, 8, THIRDS * half).astype(bf16)
    in2[chip] = out2[chip]

    spread("second", out2, in2)

    for h in (0, 1):
        for s in (1, -1):
            start("row", h, 0, s)

    for copy in loads[3:]:
        copy.wait()
    gains[...] = jnp.broadcast_to(gain_ref[...].astype(f32).reshape(1, -1), gains.shape)
    biases[...] = jnp.broadcast_to(bias_ref[...].astype(f32).reshape(1, -1), biases.shape)
    acc[...] = jnp.broadcast_to(by_kind(col_bias_ref[...].astype(f32).reshape(1, -1)), acc.shape)

    lane = iota((1, 128), 1) % 32
    turning = ROT // 2
    inverse = jnp.zeros((1, 128), f32)
    for i in range(turning):
        value = float(np.float32(10000.0) ** np.float32(-2.0 * i / ROT))
        inverse = jnp.where((lane == i) | (lane == i + turning), value, inverse)
    row = iota((tokens, 1), 0)
    request = row % third // CHIPS
    position = row // third * CHIPS + row % CHIPS
    for r in range(req_count):
        position = position + jnp.where(request == r, lengths[r], 0)
    angle = position.astype(f32) * inverse
    cosines[...] = jnp.cos(angle)
    sine = jnp.sin(angle)
    sines[...] = jnp.where(lane < turning, -sine, sine)

    for h in (0, 1):
        for s in (1, -1):
            arrive("own", h, s)
    for h in (0, 1):
        for s in (1, -1):
            start("own on", h, s)
    for h in (0, 1):
        for s in (1, -1):
            start("core", h, -s, 0)
    for s in (1, -1):
        for h in (0, 1):
            start("row", h, -s, 1)
            start("row", h, -s, -1)

    gathered("second", in2)

    m, n = iota((third, CHIPS * 8), 0), iota((third, CHIPS * 8), 1)
    pieces = flat(in2)
    for h in (0, 1):
        chosen = jnp.where(m % CHIPS * 8 + m // CHIPS * 2 + h == n, 1.0, 0.0).astype(bf16)
        rows = jnp.dot(chosen, pieces, preferred_element_type=f32).astype(bf16)
        for t in range(THIRDS):
            slabs[z, pl.ds(t * third, third), h * half : (h + 1) * half] = rows[:, t * half : (t + 1) * half]

    def slab(k, s, t, piece=None):
        ref = slabs.at[(z - k * s + DEPTH) % DEPTH]
        if piece is None:
            return ref.at[pl.ds(t * third, third), :]
        return ref.at[pl.ds(t * third + piece * (third // 2), third // 2), :]

    def z_copy(k, s, t):
        piece = dict(last_parts(s))[t] if k == 4 else None
        return remote(("z", k, s, t), slab(k - 1, s, t, piece), (me, (z + s + DEPTH) % DEPTH))

    for t in range(THIRDS):
        for s in (1, -1):
            z_copy(1, s, t).start()

    def folded(value):
        total = value[:, :128]
        for j in range(1, part // 128):
            total = total + value[:, j * 128 : (j + 1) * 128]
        return total

    for t in range(THIRDS):
        mine = pl.ds(t * third, third)
        own = jnp.sum(folded(slabs[z, mine, :].astype(f32)), axis=1, keepdims=True) * (1.0 / part)
        pivot[mine, :] = jnp.broadcast_to(own, (third, 128))
    sums[...] = jnp.zeros_like(sums)
    squares[...] = jnp.zeros_like(squares)

    def add_sums(number, t):
        @pl.loop(t * third, (t + 1) * third, step=32)
        def _(start_row):
            mine = pl.ds(pl.multiple_of(start_row, 32), 32)
            origin, total, square = pivot[mine, :], sums[mine, :], squares[mine, :]
            for j in range(part // 128):
                apart = slabs[number, mine, j * 128 : (j + 1) * 128].astype(f32) - origin
                total = total + apart
                square = square + apart * apart
            sums[mine, :] = total
            squares[mine, :] = square

    def normalise(t):
        @pl.loop(t * third, (t + 1) * third, step=32)
        def _(start_row):
            mine = pl.ds(pl.multiple_of(start_row, 32), 32)
            shift = jnp.sum(sums[mine, :], axis=1, keepdims=True) * (1.0 / model_width)
            square = jnp.sum(squares[mine, :], axis=1, keepdims=True) * (1.0 / model_width)
            inv = lax.rsqrt(jnp.maximum(square - shift * shift, 0.0) + EPS)
            inv = jnp.broadcast_to(inv, (32, 128))
            mean = pivot[mine, :] + shift
            for j in range(model_width // 128):
                w, lanes = j * 128 // part, slice(j * 128 % part, j * 128 % part + 128)
                value = (slabs[w, mine, lanes].astype(f32) - mean) * inv
                value = value.reshape(4, 8, 128) * gains[:, j * 128 : (j + 1) * 128][None]
                value = value + biases[:, j * 128 : (j + 1) * 128][None]
                normed[w, mine, lanes] = value.reshape(32, 128).astype(bf16)

    def from_core(h, du, dv):
        remote(("core", h, du, dv), block(h, du, dv, c=1 - core), partner).wait_recv()

    def multiply_pair(pair):
        acc[...] += jnp.dot(normed[pair], weights[pair], preferred_element_type=f32)

    def multiply(dy, what):
        for dx in OFFSETS:
            if (dx == 2 and what != "near") or (dx != 2 and what != "far"):
                from_core(0, dx, dy)
                from_core(1, dy, dx)
        first_pair = (y + dy + SIDE) % SIDE * 2
        if what == "row":
            pl.loop(first_pair, first_pair + 2)(multiply_pair)
        elif what == "near":
            multiply_pair(first_pair + x // 2)
        else:
            multiply_pair(first_pair + 1 - x // 2)

    for t in range(THIRDS):
        add_sums(z, t)

    seen = set()
    for event in arrivals_in_order():
        seen.add(event)
        if event[0] == "own on":
            h = event[1]
            arrive("own on", h, 1)
            arrive("own on", h, -1)
            start("row", h, 2, 1)
            start("row", h, 2, -1)
            start("core", h, 2, 0)
        elif event[0] == "row":
            arrive(*event)
            _, h, du, s = event
            start("row on", h, du, s)
            start("core", h, du, -s)
        elif event[0] == "row on":
            _, h, du = event
            arrive("row on", h, du, 1)
            arrive("row on", h, du, -1)
            start("core", h, du, 2)
        elif event[0] == "z":
            _, k, s, t = event
            z_copy(k, s, t).wait_recv()
            if k < 3 or (k == 3 and t in dict(last_parts(s))):
                z_copy(k + 1, s, t).start()
            if k < 4:
                add_sums((z - k * s + DEPTH) % DEPTH, t)
            elif all(("z", 4, d, t) in seen for d in (1, -1) if t in dict(last_parts(d))):
                add_sums((z + 4) % DEPTH, t)
                normalise(t)
        else:
            what, dy = event.split()
            multiply(int(dy), what)

    lanes = iota((1, width), 1) % HEAD
    rotated = [lanes[:, j * 128 : (j + 1) * 128] for j in range(width // 128)]
    for t in range(THIRDS):
        for r in range(req_count):
            here = pl.ds(t * third + r * CHIPS, CHIPS)
            there = pl.ds(r * fresh + t * CHIPS, CHIPS)
            cosine, sine = cosines[here, :], sines[here, :]
            for kind, ref in enumerate((q_ref, k_ref, v_ref)):
                for j in range(width // 128):
                    column = kind * width + j * 128
                    value = acc[here, column : column + 128]
                    if kind < 2:
                        near = jnp.where(
                            rotated[j] < turning,
                            pltpu.roll(value, 128 - turning, 1),
                            pltpu.roll(value, turning, 1),
                        )
                        value = jnp.where(rotated[j] < ROT, value * cosine + near * sine, value)
                    ref[there, j * 128 : (j + 1) * 128] = value.astype(bf16)

    def sent(kind, ref):
        name = ("z", 4, 1, 0) if kind == "z last" else next(n for n in NUMBER if n[0] == kind)
        remote(name, ref, partner).wait_send()

    sent("own", weights.at[0, pl.ds(0, 2 * depth), :])
    sent("own on", weights.at[0, pl.ds(0, depth), :])
    sent("row", weights.at[pl.ds(0, 2)])
    sent("row on", weights.at[0])
    sent("core", weights.at[pl.ds(0, 4)])
    sent("z", slabs.at[pl.ds(0, 6)])
    sent("z last", slabs.at[0])
    sent("swap", in1)
    sent("first", in1.at[pl.ds(0, CHIPS - 1)])
    sent("second", in1.at[pl.ds(0, CHIPS - 1)])


def project(lengths, x, w, group_of, gain, bias, col_bias):
    tokens, part = x.shape
    depth, cols = w.shape
    width = cols // 3
    lanes = tokens * part // (CHIPS * 8)
    f32, bf16 = jnp.float32, jnp.bfloat16
    out = jax.ShapeDtypeStruct((tokens, width), bf16)
    anywhere = pl.BlockSpec(memory_space=pl.ANY)
    vmem = pl.BlockSpec(memory_space=pltpu.VMEM)
    message = pltpu.VMEM((CHIPS, 8, lanes), bf16)
    wide = pltpu.VMEM((tokens, 128), f32)
    copies = pltpu.SemaphoreType.DMA((len(NUMBER),))
    return pl.pallas_call(
        project_kernel,
        out_shape=(out, out, out),
        in_specs=[anywhere] * 7,
        out_specs=(vmem, vmem, vmem),
        scratch_shapes=[
            pltpu.SMEM(lengths.shape, jnp.int32),
            pltpu.VMEM((tokens, part), bf16),
            pltpu.VMEM((depth, cols), bf16),
            pltpu.VMEM(group_of.shape, jnp.int32),
            pltpu.VMEM(gain.shape, bf16),
            pltpu.VMEM(bias.shape, bf16),
            pltpu.VMEM(col_bias.shape, bf16),
            pltpu.VMEM((CHIPS // 2, 4 * depth, cols), bf16),
            pltpu.VMEM((DEPTH, tokens, part), bf16),
            pltpu.VMEM((DEPTH, tokens, part), bf16),
            pltpu.VMEM((tokens, cols), f32),
            wide,
            wide,
            wide,
            wide,
            wide,
            pltpu.VMEM((8, part * DEPTH), f32),
            pltpu.VMEM((8, part * DEPTH), f32),
            message,
            message,
            message,
            message,
            message,
            pltpu.SemaphoreType.DMA((7,)),
            pltpu.SemaphoreType.DMA((len(SENDS),)),
            copies,
        ],
        compiler_params=pltpu.CompilerParams(
            collective_id=0, has_side_effects=True, vmem_limit_bytes=40 << 20
        ),
        cost_estimate=pl.CostEstimate(flops=10**11, bytes_accessed=10**8, transcendentals=0),
    )(lengths, x, w, group_of, gain, bias, col_bias)


def per_device(
    arrivals, group_of, lengths, page_table, ln_gain, ln_bias, w_qkv, qkv_bias, key_pool, value_pool
):
    req_count, fresh, part = arrivals.shape
    x = arrivals.reshape(req_count * fresh, part)
    operands = (lengths, x, w_qkv, group_of, ln_gain, ln_bias, qkv_bias)
    q, k, v = project(*(pltpu.with_memory_space_constraint(a, pltpu.HBM) for a in operands))
    outs = attention(lengths, page_table, q, k, v, key_pool, value_pool)
    return tuple(a.reshape(req_count, fresh, -1) for a in outs)


def solution(mesh):
    in_specs = (
        P("req", None, "wgt"),
        P(),
        P("req"),
        P("req", None),
        P(),
        P(),
        P("req", "wgt"),
        P("wgt"),
        P("req", None, "wgt"),
        P("req", None, "wgt"),
    )
    out_specs = (P("req", None, "wgt"), P("req", None, "wgt"), P("req", None, "wgt"))
    return jax.shard_map(
        per_device, mesh=mesh, in_specs=in_specs, out_specs=out_specs, check_vma=False
    )
```

```python
import math

import jax
import jax.numpy as jnp
from jax import lax
from jax.experimental import pallas as pl
from jax.experimental.pallas import tpu as pltpu
from jax.sharding import PartitionSpec as P
import numpy as np

HEAD = 96
ROT = 24
EPS = 1e-05
CHUNK_PAGES = 4
VMEM_BYTES = 67043328


def attention_kernel(
    lengths, table, q_ref, k_ref, v_ref, key_pool, value_pool, out_hbm, nk_hbm, nv_hbm,
    out_ref, queries, scores, peaks, offsets, totals, mixed, work, io,
):
    f32, bf16 = jnp.float32, jnp.bfloat16
    req_count, maxp = table.shape
    page, width = key_pool.shape[1], key_pool.shape[2]
    fresh = q_ref.shape[0] // req_count
    heads = width // HEAD
    rows = heads * fresh
    span = CHUNK_PAGES * page
    factor = math.log2(math.e) / math.sqrt(HEAD)
    low = -1e30

    count = 0
    for r in range(req_count):
        chunks = (lengths[r] + (span - 1)) // span

        @pl.loop(0, chunks)
        def _(n):
            i = count + n
            work[0, i] = r
            work[1, i] = n

        count = count + chunks

    def chunk(pool, i):
        r, n = work[0, i], work[1, i]
        pages = [pool[table[r, n * CHUNK_PAGES + p]] for p in range(CHUNK_PAGES)]
        return jnp.concatenate(pages, axis=0)

    stores = [
        pltpu.make_async_copy(k_ref, nk_hbm, io.at[0]),
        pltpu.make_async_copy(v_ref, nv_hbm, io.at[1]),
        pltpu.make_async_copy(out_ref, out_hbm, io.at[2]),
    ]
    stores[0].start()
    stores[1].start()

    iota = lambda shape, axis: lax.broadcasted_iota(jnp.int32, shape, axis)
    row_head = iota((rows, 256), 0) // fresh
    own_head = (iota((rows, 256), 1) + row_head // 2 * 128) // HEAD == row_head
    half_rows = rows // 2
    halves = ((slice(0, half_rows), slice(0, 256)), (slice(half_rows, rows), slice(128, 384)))
    causal = iota((rows, fresh), 0) % fresh >= iota((rows, fresh), 1)
    column = iota((1, span), 1)

    def fold(value, op):
        folded = value[:, :128]
        for n in range(1, value.shape[1] // 128):
            folded = op(folded, value[:, n * 128 : (n + 1) * 128])
        return folded

    across = (((1,), (1,)), ((), ()))

    def times_keys(query, keys):
        products = [
            lax.dot_general(query[group], keys[:, lanes], across, preferred_element_type=f32)
            for group, lanes in halves
        ]
        return jnp.concatenate(products, axis=0)

    def times_values(weights, values):
        weights = weights.astype(bf16)
        products = [
            jnp.dot(weights[group], values[:, lanes], preferred_element_type=f32)
            for group, lanes in halves
        ]
        return jnp.concatenate(products, axis=0)

    fresh_scores = []
    for r in range(req_count):
        mine = pl.ds(r * fresh, fresh)
        query = jnp.concatenate([q_ref[mine, lanes] for _, lanes in halves for _ in (0, 1)], axis=0)
        query = jnp.where(own_head, query, jnp.zeros_like(query))
        queries[r] = query
        own = times_keys(query, k_ref[mine, :])
        own = jnp.where(causal, own, low)
        fresh_scores.append(own)
        peaks[r] = jnp.broadcast_to(jnp.max(own, axis=1, keepdims=True), (rows, 128))
        totals[r] = jnp.zeros((rows, 128), f32)

    def over_chunks(step):
        @pl.loop(0, count // 2)
        def _(j):
            step((2 * j, 2 * j + 1))

        @pl.when(count % 2 == 1)
        def _():
            step((count - 1,))

    def first(chunks):
        values = []
        for i in chunks:
            r, n = work[0, i], work[1, i]
            keys = chunk(key_pool, i)
            value = times_keys(queries[r], keys)
            values.append(value + jnp.where(column < lengths[r] - n * span, 0.0, low))
        for i, value in zip(chunks, values):
            r = work[0, i]
            scores[i] = value
            peaks[r] = jnp.maximum(peaks[r], fold(value, jnp.maximum))

    over_chunks(first)

    fresh_totals = []
    for r in range(req_count):
        mine = pl.ds(r * fresh, fresh)
        offset = jnp.max(peaks[r], axis=1, keepdims=True) * factor
        offsets[r] = jnp.broadcast_to(offset, (rows, 128))
        weights = jnp.exp2(fresh_scores[r] * factor - offset)
        mixed[r] = times_values(weights, v_ref[mine, :])
        fresh_totals.append(jnp.sum(weights, axis=1, keepdims=True))

    def second(chunks):
        parts = []
        for i in chunks:
            r = work[0, i]
            values = chunk(value_pool, i)
            offset = jnp.concatenate([offsets[r]] * (span // 128), axis=1)
            weights = jnp.exp2(scores[i] * factor - offset)
            part = times_values(weights, values)
            parts.append((part, fold(weights, jnp.add)))
        for i, (part, total) in zip(chunks, parts):
            r = work[0, i]
            mixed[r] += part
            totals[r] += total

    over_chunks(second)

    for r in range(req_count):
        total = jnp.sum(totals[r], axis=1, keepdims=True) + fresh_totals[r]
        part = jnp.where(own_head, mixed[r] * (1.0 / total), 0.0)
        low_pair = part[:fresh] + part[fresh : 2 * fresh]
        high_pair = part[2 * fresh : 3 * fresh] + part[3 * fresh :]
        middle = low_pair[:, 128:] + high_pair[:, :128]
        value = jnp.concatenate([low_pair[:, :128], middle, high_pair[:, 128:]], axis=1)
        out_ref[pl.ds(r * fresh, fresh), :] = value.astype(out_ref.dtype)

    stores[2].start()
    for copy in stores:
        copy.wait()


def attention(lengths, table, q, k, v, key_pool, value_pool):
    rows, width = q.shape
    page = key_pool.shape[1]
    req_count, maxp = table.shape
    chunks = req_count * maxp // CHUNK_PAGES
    wide = width // HEAD * (rows // req_count)
    f32, bf16 = jnp.float32, jnp.bfloat16
    out = jax.ShapeDtypeStruct((rows, width), bf16)
    smem = pl.BlockSpec(memory_space=pltpu.SMEM)
    vmem = pl.BlockSpec(memory_space=pltpu.VMEM)
    anywhere = pl.BlockSpec(memory_space=pl.ANY)
    return pl.pallas_call(
        attention_kernel,
        out_shape=(out, out, out),
        in_specs=[smem, smem] + [vmem] * 5,
        out_specs=(anywhere, anywhere, anywhere),
        scratch_shapes=[
            pltpu.VMEM((rows, width), bf16),
            pltpu.VMEM((req_count, wide, 256), bf16),
            pltpu.VMEM((chunks, wide, CHUNK_PAGES * page), f32),
            pltpu.VMEM((req_count, wide, 128), f32),
            pltpu.VMEM((req_count, wide, 128), f32),
            pltpu.VMEM((req_count, wide, 128), f32),
            pltpu.VMEM((req_count, wide, 256), f32),
            pltpu.SMEM((2, chunks), jnp.int32),
            pltpu.SemaphoreType.DMA((3,)),
        ],
        compiler_params=pltpu.CompilerParams(vmem_limit_bytes=30 << 20),
    )(lengths, table, q, k, v, key_pool, value_pool)


MESH = pl.DeviceIdType.MESH
SIDE = 4
CHIPS = SIDE * SIDE
DEPTH = 8
OFFSETS = (0, -1, 1, 2)
THIRDS = 3


def last_parts(s):
    return ((0, None), (1, 0)) if s == 1 else ((2, None), (1, 1))


def copy_numbers():
    names = []
    for h in (0, 1):
        names += [("own", h, s) for s in (1, -1)]
        names += [("own on", h, s) for s in (1, -1)]
        names += [("row", h, du, s) for du in OFFSETS for s in (1, -1)]
        names += [("early", h, s) for s in (1, -1)]
        names += [("row on", h, du, s) for du in OFFSETS[:-1] for s in (1, -1)]
        names += [("row on", h, 2, s, p) for s in (1, -1) for p in (0, 1)]
        names += [("core", h, du, dv) for du in OFFSETS for dv in OFFSETS if (du, dv) != (2, 2)]
        names += [("core", h, 2, 2, s, p) for s in (1, -1) for p in (0, 1)]
    for s in (1, -1):
        names += [("z", k, s, t) for k in (1, 2, 3) for t in range(THIRDS)]
        names += [("z", 4, s, t) for t, _ in last_parts(s)]
    names += [("swap",), ("first",), ("second",)]
    return {name: number for number, name in enumerate(names)}


NUMBER = copy_numbers()
SENDS = ("own", "own on", "row", "row on", "core", "z", "z last", "swap", "first", "second")


def send_number(name):
    if name[:2] == ("z", 4):
        return SENDS.index("z last")
    return SENDS.index("row" if name[0] == "early" else name[0])


def arrivals_in_order():
    rows = lambda du: [("row", h, du, s) for h in (1, 0) for s in (1, -1)]
    rows_on = lambda du: [("row on", 1, du), ("row on", 0, du)]
    thirds = lambda k, *ts: [("z", k, s, t) for t in ts for s in (1, -1)]
    order = rows(0) + thirds(1, 0) + [("own on", 0), ("own on", 1)] + thirds(1, 1, 2)
    order += rows(-1) + thirds(2, 0, 1, 2) + rows(1) + thirds(3, 0) + rows_on(0) + thirds(3, 1, 2)
    order += rows(2) + [("z", 4, -1, 1), ("z", 4, 1, 0), ("z", 4, 1, 1), ("z", 4, -1, 2)]
    order += rows_on(-1) + ["row 0"] + rows_on(1) + ["row -1"]
    order += [("last", 0), ("last", 1), "row 1", "near 2", "far 2"]
    return order


def project_kernel(
    lengths_hbm, x_hbm, w_hbm, group_hbm, gain_hbm, bias_hbm, col_bias_hbm, q_ref, k_ref, v_ref,
    lengths, x_ref, w_ref, group_ref, gain_ref, bias_ref, col_bias_ref, weights, slabs, normed, acc, cosines, sines, pivot, sums, squares, gains, biases,
    out1, in1, swapped, out2, in2, load, send, recv,
):
    f32, bf16, i32 = jnp.float32, jnp.bfloat16, jnp.int32
    tokens, part = x_ref.shape
    depth, cols = w_ref.shape
    model_width = part * DEPTH
    req_count = lengths.shape[0]
    fresh = tokens // req_count
    half = part // 2
    third = tokens // THIRDS
    width = cols // 3
    rows_half, rows_sub = depth // 2, depth // 4
    me, z = lax.axis_index("req"), lax.axis_index("wgt")
    core = me % 2
    chip = me // 2
    y, x = chip // SIDE, chip % SIDE
    iota = lambda shape, axis: lax.broadcasted_iota(i32, shape, axis)

    def device(number, c=core):
        return (number * 2 + c, z)

    partner = device(chip, 1 - core)

    pairs = (
        (x_hbm, x_ref), (w_hbm, w_ref), (group_hbm, group_ref), (lengths_hbm, lengths),
        (gain_hbm, gain_ref), (bias_hbm, bias_ref), (col_bias_hbm, col_bias_ref),
    )
    loads = [pltpu.make_async_copy(a, b, load.at[n]) for n, (a, b) in enumerate(pairs)]
    loads[0].start()

    barrier = pltpu.get_barrier_semaphore()

    for d in range(1, CHIPS):
        pl.semaphore_signal(barrier, 1, device_id=device((chip + d) % CHIPS), device_id_type=MESH)

    pl.semaphore_signal(barrier, 1, device_id=partner, device_id_type=MESH)
    for s in (1, DEPTH - 1):
        pl.semaphore_signal(barrier, 1, device_id=(me, (z + s) % DEPTH), device_id_type=MESH)

    for copy in loads[1:]:
        copy.start()

    loads[0].wait()
    m, n = iota((CHIPS * 8, tokens), 0), iota((CHIPS * 8, tokens), 1)
    for t in range(THIRDS):
        take = (m % 8) // 2 * fresh + t * CHIPS + m // 8 == n
        piece = jnp.zeros((CHIPS * 8, half), f32)
        for h in (0, 1):
            chosen = jnp.where(take & (m % 2 == h), 1.0, 0.0).astype(bf16)
            piece += jnp.dot(chosen, x_ref[:, h * half : (h + 1) * half], preferred_element_type=f32)
        out1[:, :, t * half : (t + 1) * half] = piece.reshape(CHIPS, 8, half).astype(bf16)
    in1[chip] = out1[chip]

    pl.semaphore_wait(barrier, CHIPS - 1 + 3)

    def spread(name, source, target):
        for d in range(1, CHIPS):
            other = (chip + d) % CHIPS
            remote((name,), source.at[other], device(other), target.at[chip]).start()

    def gathered(name, target):
        ref = target.at[pl.ds(0, CHIPS - 1)]
        remote((name,), ref, partner).wait_recv()

    def remote(name, ref, target, dst=None):
        return pltpu.make_async_remote_copy(
            src_ref=ref,
            dst_ref=ref if dst is None else dst,
            send_sem=send.at[send_number(name)],
            recv_sem=recv.at[NUMBER[name]],
            device_id=target,
            device_id_type=MESH,
        )

    spread("first", out1, in1)

    def by_kind(value):
        heads = range(width // HEAD)
        return jnp.concatenate(
            [
                value[:, (h * 3 + kind) * HEAD : (h * 3 + kind + 1) * HEAD]
                for kind in range(3)
                for h in heads
            ],
            axis=1,
        )

    def place(number, c):
        return number // 2, (number % 2) * (2 * depth) + c * depth

    loads[1].wait()
    own_pair, own_row = place(chip, core)
    weights[own_pair, pl.ds(pl.multiple_of(own_row, 64), depth), :] = by_kind(w_ref[...])

    where = {0: (x, y), 1: (y, x)}

    def chip_at(h, du, dv):
        u, v = where[h]
        u, v = (u + du + SIDE) % SIDE, (v + dv + SIDE) % SIDE
        return v * SIDE + u if h == 0 else u * SIDE + v

    def block(h, du, dv, c=core, start_row=0, count=rows_half):
        pair, row = place(chip_at(h, du, dv), c)
        row = row + h * rows_half + start_row
        return weights.at[pair, pl.ds(pl.multiple_of(row, 16), count), :]

    def sub_rows(s, p=None):
        start_row = 0 if s == 1 else rows_sub
        if p is None:
            return start_row, rows_sub
        return (start_row, rows_sub - 16) if p == 0 else (start_row + rows_sub - 16, 16)

    def weight_copy(name):
        kind, h = name[0], name[1]
        if kind == "own":
            return remote(name, block(h, 0, 0), device(chip_at(h, name[2], 0)))
        if kind == "own on":
            s = name[2]
            return remote(name, block(h, -s, 0, core, *sub_rows(s)), device(chip_at(h, s, 0)))
        if kind == "early":
            return remote(name, block(h, 0, 0, core, 0, 16), device(chip_at(h, 0, name[2])))
        if kind == "row":
            du, s = name[2], name[3]
            ref = block(h, 0, 0, core, 16, rows_half - 16) if du == 0 else block(h, du, 0)
            return remote(name, ref, device(chip_at(h, 0, s)))
        if kind == "row on":
            du, s = name[2], name[3]
            return remote(name, block(h, du, -s, core, *sub_rows(*name[3:])), device(chip_at(h, 0, s)))
        du, dv = name[2], name[3]
        rows = sub_rows(*name[4:]) if len(name) > 4 else ()
        return remote(name, block(h, du, dv, core, *rows), partner)

    def start(*name):
        weight_copy(name).start()

    def arrive(*name):
        weight_copy(name).wait_recv()

    for h in (0, 1):
        for s in (1, -1):
            start("own", h, s)
    for h in (0, 1):
        start("core", h, 0, 0)
    for h in (0, 1):
        for s in (1, -1):
            start("early", h, s)

    a, b = iota((CHIPS * 8, CHIPS * 8), 0), iota((CHIPS * 8, CHIPS * 8), 1)
    loads[2].wait()
    groups = group_ref[...].reshape(1, -1)
    group_row = jnp.broadcast_to(groups, a.shape)
    group_col = jnp.sum(jnp.where(a == b, group_row, 0), axis=1, keepdims=True)
    rank = jnp.sum(jnp.where((group_col == group_row) & (a < b), 1, 0), axis=0, keepdims=True)
    slot_row = groups * req_count + rank
    slot_col = jnp.sum(jnp.where(a == b, jnp.broadcast_to(slot_row, a.shape), 0), axis=1, keepdims=True)

    def selector(c):
        arriving = (b // 8 * 2 + c) * req_count + b % 8 // 2
        slot = jnp.sum(jnp.where(a == arriving, slot_col, 0), axis=0, keepdims=True)
        wanted = (a // 8 * 2 + core) * req_count + a % 8 // 2
        return jnp.where((wanted == slot) & (a % 2 == b % 2), 1.0, 0.0).astype(bf16)

    pick_own, pick_other = selector(core), selector(1 - core)

    gathered("first", in1)

    swap = remote(("swap",), in1, partner, swapped)
    swap.start()

    def flat(ref):
        return ref[...].astype(f32).reshape(CHIPS * 8, THIRDS * half).astype(bf16)

    mixed = jnp.dot(pick_own, flat(in1), preferred_element_type=f32)
    swap.wait_recv()
    mixed = mixed + jnp.dot(pick_other, flat(swapped), preferred_element_type=f32)
    out2[...] = mixed.reshape(CHIPS, 8, THIRDS * half).astype(bf16)
    in2[chip] = out2[chip]

    spread("second", out2, in2)

    for h in (0, 1):
        for s in (1, -1):
            start("row", h, 0, s)

    for copy in loads[3:]:
        copy.wait()
    gains[...] = jnp.broadcast_to(gain_ref[...].astype(f32).reshape(1, -1), gains.shape)
    biases[...] = jnp.broadcast_to(bias_ref[...].astype(f32).reshape(1, -1), biases.shape)
    acc[...] = jnp.broadcast_to(by_kind(col_bias_ref[...].astype(f32).reshape(1, -1)), acc.shape)

    lane = iota((1, 128), 1) % 32
    turning = ROT // 2
    inverse = jnp.zeros((1, 128), f32)
    for i in range(turning):
        value = float(np.float32(10000.0) ** np.float32(-2.0 * i / ROT))
        inverse = jnp.where((lane == i) | (lane == i + turning), value, inverse)
    row = iota((tokens, 1), 0)
    request = row % third // CHIPS
    position = row // third * CHIPS + row % CHIPS
    for r in range(req_count):
        position = position + jnp.where(request == r, lengths[r], 0)
    angle = position.astype(f32) * inverse
    cosines[...] = jnp.cos(angle)
    sine = jnp.sin(angle)
    sines[...] = jnp.where(lane < turning, -sine, sine)

    for h in (0, 1):
        for s in (1, -1):
            arrive("own", h, s)
    for h in (0, 1):
        for s in (1, -1):
            start("own on", h, s)
    for h in (0, 1):
        for s in (1, -1):
            start("core", h, -s, 0)
    for s in (1, -1):
        for h in (0, 1):
            start("row", h, -s, 1)
            start("row", h, -s, -1)

    gathered("second", in2)

    m, n = iota((third, CHIPS * 8), 0), iota((third, CHIPS * 8), 1)
    pieces = flat(in2)
    for h in (0, 1):
        chosen = jnp.where(m % CHIPS * 8 + m // CHIPS * 2 + h == n, 1.0, 0.0).astype(bf16)
        rows = jnp.dot(chosen, pieces, preferred_element_type=f32).astype(bf16)
        for t in range(THIRDS):
            slabs[z, pl.ds(t * third, third), h * half : (h + 1) * half] = rows[:, t * half : (t + 1) * half]

    def slab(k, s, t, piece=None):
        ref = slabs.at[(z - k * s + DEPTH) % DEPTH]
        if piece is None:
            return ref.at[pl.ds(t * third, third), :]
        return ref.at[pl.ds(t * third + piece * (third // 2), third // 2), :]

    def z_copy(k, s, t):
        piece = dict(last_parts(s))[t] if k == 4 else None
        return remote(("z", k, s, t), slab(k - 1, s, t, piece), (me, (z + s + DEPTH) % DEPTH))

    for t in range(THIRDS):
        for s in (1, -1):
            z_copy(1, s, t).start()

    def folded(value):
        total = value[:, :128]
        for j in range(1, part // 128):
            total = total + value[:, j * 128 : (j + 1) * 128]
        return total

    for t in range(THIRDS):
        mine = pl.ds(t * third, third)
        own = jnp.sum(folded(slabs[z, mine, :].astype(f32)), axis=1, keepdims=True) * (1.0 / part)
        pivot[mine, :] = jnp.broadcast_to(own, (third, 128))
    sums[...] = jnp.zeros_like(sums)
    squares[...] = jnp.zeros_like(squares)

    def add_sums(number, t):
        @pl.loop(t * third, (t + 1) * third, step=32)
        def _(start_row):
            mine = pl.ds(pl.multiple_of(start_row, 32), 32)
            origin, total, square = pivot[mine, :], sums[mine, :], squares[mine, :]
            for j in range(part // 128):
                apart = slabs[number, mine, j * 128 : (j + 1) * 128].astype(f32) - origin
                total = total + apart
                square = square + apart * apart
            sums[mine, :] = total
            squares[mine, :] = square

    def normalise(t):
        @pl.loop(t * third, (t + 1) * third, step=32)
        def _(start_row):
            mine = pl.ds(pl.multiple_of(start_row, 32), 32)
            shift = jnp.sum(sums[mine, :], axis=1, keepdims=True) * (1.0 / model_width)
            square = jnp.sum(squares[mine, :], axis=1, keepdims=True) * (1.0 / model_width)
            inv = lax.rsqrt(jnp.maximum(square - shift * shift, 0.0) + EPS)
            inv = jnp.broadcast_to(inv, (32, 128))
            mean = pivot[mine, :] + shift
            for j in range(model_width // 128):
                w, lanes = j * 128 // part, slice(j * 128 % part, j * 128 % part + 128)
                value = (slabs[w, mine, lanes].astype(f32) - mean) * inv
                value = value.reshape(4, 8, 128) * gains[:, j * 128 : (j + 1) * 128][None]
                value = value + biases[:, j * 128 : (j + 1) * 128][None]
                normed[w, mine, lanes] = value.reshape(32, 128).astype(bf16)

    def from_core(h, du, dv):
        if (du, dv) != (2, 2):
            remote(("core", h, du, dv), block(h, du, dv, 1 - core), partner).wait_recv()
            return
        for s in (1, -1):
            for p in (0, 1):
                ref = block(h, 2, 2, 1 - core, *sub_rows(s, p))
                remote(("core", h, 2, 2, s, p), ref, partner).wait_recv()

    def multiply_pair(pair):
        acc[...] += jnp.dot(normed[pair], weights[pair], preferred_element_type=f32)

    def multiply(dy, what):
        for dx in OFFSETS:
            if (dx == 2 and what != "near") or (dx != 2 and what != "far"):
                from_core(0, dx, dy)
                from_core(1, dy, dx)
        first_pair = (y + dy + SIDE) % SIDE * 2
        if what == "row":
            pl.loop(first_pair, first_pair + 2)(multiply_pair)
        elif what == "near":
            multiply_pair(first_pair + x // 2)
        else:
            multiply_pair(first_pair + 1 - x // 2)

    for t in range(THIRDS):
        add_sums(z, t)

    seen = set()
    for event in arrivals_in_order():
        seen.add(event)
        if event[0] == "own on":
            h = event[1]
            arrive("own on", h, 1)
            arrive("own on", h, -1)
            start("row", h, 2, 1)
            start("row", h, 2, -1)
            start("core", h, 2, 0)
        elif event[0] == "row":
            arrive(*event)
            _, h, du, s = event
            if du == 0:
                arrive("early", h, s)
            if du == 2:
                start("row on", h, 2, s, 0)
                start("row on", h, 2, s, 1)
            else:
                start("row on", h, du, s)
            start("core", h, du, -s)
        elif event[0] == "last":
            for h in (1, 0):
                for s in (1, -1):
                    arrive("row on", h, 2, s, event[1])
                    start("core", h, 2, 2, s, event[1])
        elif event[0] == "row on":
            _, h, du = event
            arrive("row on", h, du, 1)
            arrive("row on", h, du, -1)
            start("core", h, du, 2)
        elif event[0] == "z":
            _, k, s, t = event
            z_copy(k, s, t).wait_recv()
            if k < 3 or (k == 3 and t in dict(last_parts(s))):
                z_copy(k + 1, s, t).start()
            if k < 4:
                add_sums((z - k * s + DEPTH) % DEPTH, t)
            elif all(("z", 4, d, t) in seen for d in (1, -1) if t in dict(last_parts(d))):
                add_sums((z + 4) % DEPTH, t)
                normalise(t)
        else:
            what, dy = event.split()
            multiply(int(dy), what)

    lanes = iota((1, width), 1) % HEAD
    rotated = [lanes[:, j * 128 : (j + 1) * 128] for j in range(width // 128)]
    for t in range(THIRDS):
        for r in range(req_count):
            here = pl.ds(t * third + r * CHIPS, CHIPS)
            there = pl.ds(r * fresh + t * CHIPS, CHIPS)
            cosine, sine = cosines[here, :], sines[here, :]
            for kind, ref in enumerate((q_ref, k_ref, v_ref)):
                for j in range(width // 128):
                    column = kind * width + j * 128
                    value = acc[here, column : column + 128]
                    if kind < 2:
                        near = jnp.where(
                            rotated[j] < turning,
                            pltpu.roll(value, 128 - turning, 1),
                            pltpu.roll(value, turning, 1),
                        )
                        value = jnp.where(rotated[j] < ROT, value * cosine + near * sine, value)
                    ref[there, j * 128 : (j + 1) * 128] = value.astype(bf16)

    def sent(kind, ref):
        name = ("z", 4, 1, 0) if kind == "z last" else next(n for n in NUMBER if n[0] == kind)
        remote(name, ref, partner).wait_send()

    sent("own", weights.at[0, pl.ds(0, 2 * depth), :])
    sent("own on", weights.at[0, pl.ds(0, depth), :])
    sent("row", weights.at[pl.ds(0, 2)])
    sent("row on", weights.at[0])
    sent("core", weights.at[pl.ds(0, 4)])
    sent("z", slabs.at[pl.ds(0, 6)])
    sent("z last", slabs.at[0])
    sent("swap", in1)
    sent("first", in1.at[pl.ds(0, CHIPS - 1)])
    sent("second", in1.at[pl.ds(0, CHIPS - 1)])


def project(lengths, x, w, group_of, gain, bias, col_bias):
    tokens, part = x.shape
    depth, cols = w.shape
    width = cols // 3
    lanes = tokens * part // (CHIPS * 8)
    f32, bf16 = jnp.float32, jnp.bfloat16
    out = jax.ShapeDtypeStruct((tokens, width), bf16)
    anywhere = pl.BlockSpec(memory_space=pl.ANY)
    vmem = pl.BlockSpec(memory_space=pltpu.VMEM)
    message = pltpu.VMEM((CHIPS, 8, lanes), bf16)
    wide = pltpu.VMEM((tokens, 128), f32)
    copies = pltpu.SemaphoreType.DMA((len(NUMBER),))
    return pl.pallas_call(
        project_kernel,
        out_shape=(out, out, out),
        in_specs=[anywhere] * 7,
        out_specs=(vmem, vmem, vmem),
        scratch_shapes=[
            pltpu.SMEM(lengths.shape, jnp.int32),
            pltpu.VMEM((tokens, part), bf16),
            pltpu.VMEM((depth, cols), bf16),
            pltpu.VMEM(group_of.shape, jnp.int32),
            pltpu.VMEM(gain.shape, bf16),
            pltpu.VMEM(bias.shape, bf16),
            pltpu.VMEM(col_bias.shape, bf16),
            pltpu.VMEM((CHIPS // 2, 4 * depth, cols), bf16),
            pltpu.VMEM((DEPTH, tokens, part), bf16),
            pltpu.VMEM((DEPTH, tokens, part), bf16),
            pltpu.VMEM((tokens, cols), f32),
            wide,
            wide,
            wide,
            wide,
            wide,
            pltpu.VMEM((8, part * DEPTH), f32),
            pltpu.VMEM((8, part * DEPTH), f32),
            message,
            message,
            message,
            message,
            message,
            pltpu.SemaphoreType.DMA((7,)),
            pltpu.SemaphoreType.DMA((len(SENDS),)),
            copies,
        ],
        compiler_params=pltpu.CompilerParams(
            collective_id=0, has_side_effects=True, vmem_limit_bytes=40 << 20
        ),
        cost_estimate=pl.CostEstimate(flops=10**11, bytes_accessed=10**8, transcendentals=0),
    )(lengths, x, w, group_of, gain, bias, col_bias)


def per_device(
    arrivals, group_of, lengths, page_table, ln_gain, ln_bias, w_qkv, qkv_bias, key_pool, value_pool
):
    req_count, fresh, part = arrivals.shape
    x = arrivals.reshape(req_count * fresh, part)
    operands = (lengths, x, w_qkv, group_of, ln_gain, ln_bias, qkv_bias)
    q, k, v = project(*(pltpu.with_memory_space_constraint(a, pltpu.HBM) for a in operands))
    outs = attention(lengths, page_table, q, k, v, key_pool, value_pool)
    return tuple(a.reshape(req_count, fresh, -1) for a in outs)


def solution(mesh):
    in_specs = (
        P("req", None, "wgt"),
        P(),
        P("req"),
        P("req", None),
        P(),
        P(),
        P("req", "wgt"),
        P("wgt"),
        P("req", None, "wgt"),
        P("req", None, "wgt"),
    )
    out_specs = (P("req", None, "wgt"), P("req", None, "wgt"), P("req", None, "wgt"))
    return jax.shard_map(
        per_device, mesh=mesh, in_specs=in_specs, out_specs=out_specs, check_vma=False
    )
```

```python
import math

import jax
import jax.numpy as jnp
from jax import lax
from jax.experimental import pallas as pl
from jax.experimental.pallas import tpu as pltpu
from jax.sharding import PartitionSpec as P
import numpy as np

HEAD = 96
ROT = 24
EPS = 1e-05
CHUNK_PAGES = 4
VMEM_BYTES = 67043328


def attention_kernel(
    lengths, table, q_ref, k_ref, v_ref, key_pool, value_pool, out_hbm, nk_hbm, nv_hbm,
    out_ref, queries, scores, peaks, offsets, totals, mixed, work, io,
):
    f32, bf16 = jnp.float32, jnp.bfloat16
    req_count, maxp = table.shape
    page, width = key_pool.shape[1], key_pool.shape[2]
    fresh = q_ref.shape[0] // req_count
    heads = width // HEAD
    rows = heads * fresh
    span = CHUNK_PAGES * page
    factor = math.log2(math.e) / math.sqrt(HEAD)
    low = -1e30

    count = 0
    for r in range(req_count):
        chunks = (lengths[r] + (span - 1)) // span

        @pl.loop(0, chunks)
        def _(n):
            i = count + n
            work[0, i] = r
            work[1, i] = n

        count = count + chunks

    def chunk(pool, i):
        r, n = work[0, i], work[1, i]
        pages = [pool[table[r, n * CHUNK_PAGES + p]] for p in range(CHUNK_PAGES)]
        return jnp.concatenate(pages, axis=0)

    stores = [
        pltpu.make_async_copy(k_ref, nk_hbm, io.at[0]),
        pltpu.make_async_copy(v_ref, nv_hbm, io.at[1]),
    ]
    stores[0].start()
    stores[1].start()

    iota = lambda shape, axis: lax.broadcasted_iota(jnp.int32, shape, axis)
    row_head = iota((rows, 256), 0) // fresh
    own_head = (iota((rows, 256), 1) + row_head // 2 * 128) // HEAD == row_head
    half_rows = rows // 2
    halves = ((slice(0, half_rows), slice(0, 256)), (slice(half_rows, rows), slice(128, 384)))
    causal = iota((rows, fresh), 0) % fresh >= iota((rows, fresh), 1)
    column = iota((1, span), 1)

    def fold(value, op):
        folded = value[:, :128]
        for n in range(1, value.shape[1] // 128):
            folded = op(folded, value[:, n * 128 : (n + 1) * 128])
        return folded

    across = (((1,), (1,)), ((), ()))

    def times_keys(query, keys):
        products = [
            lax.dot_general(query[group], keys[:, lanes], across, preferred_element_type=f32)
            for group, lanes in halves
        ]
        return jnp.concatenate(products, axis=0)

    def times_values(weights, values):
        weights = weights.astype(bf16)
        products = [
            jnp.dot(weights[group], values[:, lanes], preferred_element_type=f32)
            for group, lanes in halves
        ]
        return jnp.concatenate(products, axis=0)

    fresh_scores = []
    for r in range(req_count):
        mine = pl.ds(r * fresh, fresh)
        query = jnp.concatenate([q_ref[mine, lanes] for _, lanes in halves for _ in (0, 1)], axis=0)
        query = jnp.where(own_head, query, jnp.zeros_like(query))
        queries[r] = query
        own = times_keys(query, k_ref[mine, :])
        own = jnp.where(causal, own, low)
        fresh_scores.append(own)
        peaks[r] = jnp.broadcast_to(jnp.max(own, axis=1, keepdims=True), (rows, 128))
        totals[r] = jnp.zeros((rows, 128), f32)

    def over_chunks(step):
        @pl.loop(0, count // 2)
        def _(j):
            step((2 * j, 2 * j + 1))

        @pl.when(count % 2 == 1)
        def _():
            step((count - 1,))

    def first(chunks):
        values = []
        for i in chunks:
            r, n = work[0, i], work[1, i]
            keys = chunk(key_pool, i)
            value = times_keys(queries[r], keys)
            values.append(value + jnp.where(column < lengths[r] - n * span, 0.0, low))
        for i, value in zip(chunks, values):
            r = work[0, i]
            scores[i] = value
            peaks[r] = jnp.maximum(peaks[r], fold(value, jnp.maximum))

    over_chunks(first)

    fresh_totals = []
    for r in range(req_count):
        mine = pl.ds(r * fresh, fresh)
        offset = jnp.max(peaks[r], axis=1, keepdims=True) * factor
        offsets[r] = jnp.broadcast_to(offset, (rows, 128))
        weights = jnp.exp2(fresh_scores[r] * factor - offset)
        mixed[r] = times_values(weights, v_ref[mine, :])
        fresh_totals.append(jnp.sum(weights, axis=1, keepdims=True))

    def second(chunks):
        parts = []
        for i in chunks:
            r = work[0, i]
            values = chunk(value_pool, i)
            offset = jnp.concatenate([offsets[r]] * (span // 128), axis=1)
            weights = jnp.exp2(scores[i] * factor - offset)
            part = times_values(weights, values)
            parts.append((part, fold(weights, jnp.add)))
        for i, (part, total) in zip(chunks, parts):
            r = work[0, i]
            mixed[r] += part
            totals[r] += total

    over_chunks(second)

    for r in range(req_count):
        total = jnp.sum(totals[r], axis=1, keepdims=True) + fresh_totals[r]
        part = jnp.where(own_head, mixed[r] * (1.0 / total), 0.0)
        low_pair = part[:fresh] + part[fresh : 2 * fresh]
        high_pair = part[2 * fresh : 3 * fresh] + part[3 * fresh :]
        middle = low_pair[:, 128:] + high_pair[:, :128]
        value = jnp.concatenate([low_pair[:, :128], middle, high_pair[:, 128:]], axis=1)
        mine = pl.ds(r * fresh, fresh)
        out_ref[mine, :] = value.astype(out_ref.dtype)
        stores.append(pltpu.make_async_copy(out_ref.at[mine, :], out_hbm.at[mine, :], io.at[2 + r]))
        stores[-1].start()

    for copy in stores:
        copy.wait()


def attention(lengths, table, q, k, v, key_pool, value_pool):
    rows, width = q.shape
    page = key_pool.shape[1]
    req_count, maxp = table.shape
    chunks = req_count * maxp // CHUNK_PAGES
    wide = width // HEAD * (rows // req_count)
    f32, bf16 = jnp.float32, jnp.bfloat16
    out = jax.ShapeDtypeStruct((rows, width), bf16)
    smem = pl.BlockSpec(memory_space=pltpu.SMEM)
    vmem = pl.BlockSpec(memory_space=pltpu.VMEM)
    anywhere = pl.BlockSpec(memory_space=pl.ANY)
    return pl.pallas_call(
        attention_kernel,
        out_shape=(out, out, out),
        in_specs=[smem, smem] + [vmem] * 5,
        out_specs=(anywhere, anywhere, anywhere),
        scratch_shapes=[
            pltpu.VMEM((rows, width), bf16),
            pltpu.VMEM((req_count, wide, 256), bf16),
            pltpu.VMEM((chunks, wide, CHUNK_PAGES * page), f32),
            pltpu.VMEM((req_count, wide, 128), f32),
            pltpu.VMEM((req_count, wide, 128), f32),
            pltpu.VMEM((req_count, wide, 128), f32),
            pltpu.VMEM((req_count, wide, 256), f32),
            pltpu.SMEM((2, chunks), jnp.int32),
            pltpu.SemaphoreType.DMA((2 + req_count,)),
        ],
        compiler_params=pltpu.CompilerParams(vmem_limit_bytes=30 << 20),
    )(lengths, table, q, k, v, key_pool, value_pool)


MESH = pl.DeviceIdType.MESH
SIDE = 4
CHIPS = SIDE * SIDE
DEPTH = 8
OFFSETS = (0, -1, 1, 2)
THIRDS = 3


def last_parts(s):
    return ((0, None), (1, 0)) if s == 1 else ((2, None), (1, 1))


def copy_numbers():
    names = []
    for h in (0, 1):
        names += [("own", h, s) for s in (1, -1)]
        names += [("own on", h, s) for s in (1, -1)]
        names += [("row", h, du, s) for du in OFFSETS for s in (1, -1)]
        names += [("row on", h, du, s) for du in OFFSETS for s in (1, -1)]
        names += [("core", h, du, dv) for du in OFFSETS for dv in OFFSETS]
    for s in (1, -1):
        names += [("z", k, s, t) for k in (1, 2, 3) for t in range(THIRDS)]
        names += [("z", 4, s, t) for t, _ in last_parts(s)]
    names += [("swap",), ("first",), ("second",)]
    return {name: number for number, name in enumerate(names)}


NUMBER = copy_numbers()
SENDS = ("own", "own on", "row", "row on", "core", "z", "z last", "swap", "first", "second")


def send_number(name):
    return SENDS.index("z last" if name[:2] == ("z", 4) else name[0])


def arrivals_in_order():
    rows = lambda du: [("row", h, du, s) for h in (1, 0) for s in (1, -1)]
    rows_on = lambda du: [("row on", 1, du), ("row on", 0, du)]
    thirds = lambda k, *ts: [("z", k, s, t) for t in ts for s in (1, -1)]
    order = rows(0) + thirds(1, 0) + [("own on", 0), ("own on", 1)] + thirds(1, 1, 2)
    order += rows(-1) + thirds(2, 0, 1, 2) + rows(1) + thirds(3, 0) + rows_on(0) + thirds(3, 1, 2)
    order += rows(2) + [("z", 4, -1, 1), ("z", 4, 1, 0), ("z", 4, 1, 1), ("z", 4, -1, 2)]
    order += rows_on(-1) + ["row 0"] + rows_on(1) + ["row -1"] + rows_on(2) + ["row 1", "near 2", "far 2"]
    return order


def project_kernel(
    lengths_hbm, x_hbm, w_hbm, group_hbm, gain_hbm, bias_hbm, col_bias_hbm, q_ref, k_ref, v_ref,
    lengths, x_ref, w_ref, group_ref, gain_ref, bias_ref, col_bias_ref, weights, slabs, normed, acc, cosines, sines, pivot, sums, squares, gains, biases,
    out1, in1, swapped, out2, in2, load, send, recv,
):
    f32, bf16, i32 = jnp.float32, jnp.bfloat16, jnp.int32
    tokens, part = x_ref.shape
    depth, cols = w_ref.shape
    model_width = part * DEPTH
    req_count = lengths.shape[0]
    fresh = tokens // req_count
    half = part // 2
    third = tokens // THIRDS
    width = cols // 3
    rows_half, rows_sub = depth // 2, depth // 4
    me, z = lax.axis_index("req"), lax.axis_index("wgt")
    core = me % 2
    chip = me // 2
    y, x = chip // SIDE, chip % SIDE
    iota = lambda shape, axis: lax.broadcasted_iota(i32, shape, axis)

    def device(number, c=core):
        return (number * 2 + c, z)

    partner = device(chip, 1 - core)

    pairs = (
        (x_hbm, x_ref), (w_hbm, w_ref), (group_hbm, group_ref), (lengths_hbm, lengths),
        (gain_hbm, gain_ref), (bias_hbm, bias_ref), (col_bias_hbm, col_bias_ref),
    )
    loads = [pltpu.make_async_copy(a, b, load.at[n]) for n, (a, b) in enumerate(pairs)]
    loads[0].start()

    barrier = pltpu.get_barrier_semaphore()

    for d in range(1, CHIPS):
        pl.semaphore_signal(barrier, 1, device_id=device((chip + d) % CHIPS), device_id_type=MESH)

    pl.semaphore_signal(barrier, 1, device_id=partner, device_id_type=MESH)
    for s in (1, DEPTH - 1):
        pl.semaphore_signal(barrier, 1, device_id=(me, (z + s) % DEPTH), device_id_type=MESH)

    for copy in loads[1:]:
        copy.start()

    loads[0].wait()
    m, n = iota((CHIPS * 8, tokens), 0), iota((CHIPS * 8, tokens), 1)
    for t in range(THIRDS):
        take = (m % 8) // 2 * fresh + t * CHIPS + m // 8 == n
        piece = jnp.zeros((CHIPS * 8, half), f32)
        for h in (0, 1):
            chosen = jnp.where(take & (m % 2 == h), 1.0, 0.0).astype(bf16)
            piece += jnp.dot(chosen, x_ref[:, h * half : (h + 1) * half], preferred_element_type=f32)
        out1[:, :, t * half : (t + 1) * half] = piece.reshape(CHIPS, 8, half).astype(bf16)
    in1[chip] = out1[chip]

    pl.semaphore_wait(barrier, CHIPS - 1 + 3)

    def spread(name, source, target):
        for d in range(1, CHIPS):
            other = (chip + d) % CHIPS
            remote((name,), source.at[other], device(other), target.at[chip]).start()

    def gathered(name, target):
        ref = target.at[pl.ds(0, CHIPS - 1)]
        remote((name,), ref, partner).wait_recv()

    def remote(name, ref, target, dst=None):
        return pltpu.make_async_remote_copy(
            src_ref=ref,
            dst_ref=ref if dst is None else dst,
            send_sem=send.at[send_number(name)],
            recv_sem=recv.at[NUMBER[name]],
            device_id=target,
            device_id_type=MESH,
        )

    spread("first", out1, in1)

    def by_kind(value):
        heads = range(width // HEAD)
        return jnp.concatenate(
            [
                value[:, (h * 3 + kind) * HEAD : (h * 3 + kind + 1) * HEAD]
                for kind in range(3)
                for h in heads
            ],
            axis=1,
        )

    def place(number, c):
        return number // 2, (number % 2) * (2 * depth) + c * depth

    loads[1].wait()
    own_pair, own_row = place(chip, core)
    weights[own_pair, pl.ds(pl.multiple_of(own_row, 64), depth), :] = by_kind(w_ref[...])

    where = {0: (x, y), 1: (y, x)}

    def chip_at(h, du, dv):
        u, v = where[h]
        u, v = (u + du + SIDE) % SIDE, (v + dv + SIDE) % SIDE
        return v * SIDE + u if h == 0 else u * SIDE + v

    def block(h, du, dv, c=core, sub=None):
        pair, row = place(chip_at(h, du, dv), c)
        row = row + h * rows_half + (0 if sub in (None, 1) else rows_sub)
        return weights.at[pair, pl.ds(pl.multiple_of(row, 16), rows_half if sub is None else rows_sub), :]

    def weight_copy(name):
        kind, h = name[0], name[1]
        if kind == "own":
            return remote(name, block(h, 0, 0), device(chip_at(h, name[2], 0)))
        if kind == "own on":
            s = name[2]
            return remote(name, block(h, -s, 0, sub=s), device(chip_at(h, s, 0)))
        if kind == "row":
            du, s = name[2], name[3]
            return remote(name, block(h, du, 0), device(chip_at(h, 0, s)))
        if kind == "row on":
            du, s = name[2], name[3]
            return remote(name, block(h, du, -s, sub=s), device(chip_at(h, 0, s)))
        du, dv = name[2], name[3]
        return remote(name, block(h, du, dv), partner)

    def start(*name):
        weight_copy(name).start()

    def arrive(*name):
        weight_copy(name).wait_recv()

    for h in (0, 1):
        for s in (1, -1):
            start("own", h, s)
    for h in (0, 1):
        start("core", h, 0, 0)

    a, b = iota((CHIPS * 8, CHIPS * 8), 0), iota((CHIPS * 8, CHIPS * 8), 1)
    loads[2].wait()
    groups = group_ref[...].reshape(1, -1)
    group_row = jnp.broadcast_to(groups, a.shape)
    group_col = jnp.sum(jnp.where(a == b, group_row, 0), axis=1, keepdims=True)
    rank = jnp.sum(jnp.where((group_col == group_row) & (a < b), 1, 0), axis=0, keepdims=True)
    slot_row = groups * req_count + rank
    slot_col = jnp.sum(jnp.where(a == b, jnp.broadcast_to(slot_row, a.shape), 0), axis=1, keepdims=True)

    def selector(c):
        arriving = (b // 8 * 2 + c) * req_count + b % 8 // 2
        slot = jnp.sum(jnp.where(a == arriving, slot_col, 0), axis=0, keepdims=True)
        wanted = (a // 8 * 2 + core) * req_count + a % 8 // 2
        return jnp.where((wanted == slot) & (a % 2 == b % 2), 1.0, 0.0).astype(bf16)

    pick_own, pick_other = selector(core), selector(1 - core)

    gathered("first", in1)

    swap = remote(("swap",), in1, partner, swapped)
    swap.start()

    def flat(ref):
        return ref[...].astype(f32).reshape(CHIPS * 8, THIRDS * half).astype(bf16)

    mixed = jnp.dot(pick_own, flat(in1), preferred_element_type=f32)
    swap.wait_recv()
    mixed = mixed + jnp.dot(pick_other, flat(swapped), preferred_element_type=f32)
    out2[...] = mixed.reshape(CHIPS, 8, THIRDS * half).astype(bf16)
    in2[chip] = out2[chip]

    spread("second", out2, in2)

    for h in (0, 1):
        for s in (1, -1):
            start("row", h, 0, s)

    for copy in loads[3:]:
        copy.wait()
    gains[...] = jnp.broadcast_to(gain_ref[...].astype(f32).reshape(1, -1), gains.shape)
    biases[...] = jnp.broadcast_to(bias_ref[...].astype(f32).reshape(1, -1), biases.shape)
    acc[...] = jnp.broadcast_to(by_kind(col_bias_ref[...].astype(f32).reshape(1, -1)), acc.shape)

    lane = iota((1, 128), 1) % 32
    turning = ROT // 2
    inverse = jnp.zeros((1, 128), f32)
    for i in range(turning):
        value = float(np.float32(10000.0) ** np.float32(-2.0 * i / ROT))
        inverse = jnp.where((lane == i) | (lane == i + turning), value, inverse)
    row = iota((tokens, 1), 0)
    request = row % third // CHIPS
    position = row // third * CHIPS + row % CHIPS
    for r in range(req_count):
        position = position + jnp.where(request == r, lengths[r], 0)
    angle = position.astype(f32) * inverse
    cosines[...] = jnp.cos(angle)
    sine = jnp.sin(angle)
    sines[...] = jnp.where(lane < turning, -sine, sine)

    for h in (0, 1):
        for s in (1, -1):
            arrive("own", h, s)
    for h in (0, 1):
        for s in (1, -1):
            start("own on", h, s)
    for h in (0, 1):
        for s in (1, -1):
            start("core", h, -s, 0)
    for s in (1, -1):
        for h in (0, 1):
            start("row", h, -s, 1)
            start("row", h, -s, -1)

    gathered("second", in2)

    m, n = iota((third, CHIPS * 8), 0), iota((third, CHIPS * 8), 1)
    pieces = flat(in2)
    for h in (0, 1):
        chosen = jnp.where(m % CHIPS * 8 + m // CHIPS * 2 + h == n, 1.0, 0.0).astype(bf16)
        rows = jnp.dot(chosen, pieces, preferred_element_type=f32).astype(bf16)
        for t in range(THIRDS):
            slabs[z, pl.ds(t * third, third), h * half : (h + 1) * half] = rows[:, t * half : (t + 1) * half]

    def slab(k, s, t, piece=None):
        ref = slabs.at[(z - k * s + DEPTH) % DEPTH]
        if piece is None:
            return ref.at[pl.ds(t * third, third), :]
        return ref.at[pl.ds(t * third + piece * (third // 2), third // 2), :]

    def z_copy(k, s, t):
        piece = dict(last_parts(s))[t] if k == 4 else None
        return remote(("z", k, s, t), slab(k - 1, s, t, piece), (me, (z + s + DEPTH) % DEPTH))

    for t in range(THIRDS):
        for s in (1, -1):
            z_copy(1, s, t).start()

    def folded(value):
        total = value[:, :128]
        for j in range(1, part // 128):
            total = total + value[:, j * 128 : (j + 1) * 128]
        return total

    for t in range(THIRDS):
        mine = pl.ds(t * third, third)
        own = jnp.sum(folded(slabs[z, mine, :].astype(f32)), axis=1, keepdims=True) * (1.0 / part)
        pivot[mine, :] = jnp.broadcast_to(own, (third, 128))
    sums[...] = jnp.zeros_like(sums)
    squares[...] = jnp.zeros_like(squares)

    def add_sums(number, t):
        @pl.loop(t * third, (t + 1) * third, step=32)
        def _(start_row):
            mine = pl.ds(pl.multiple_of(start_row, 32), 32)
            origin, total, square = pivot[mine, :], sums[mine, :], squares[mine, :]
            for j in range(part // 128):
                apart = slabs[number, mine, j * 128 : (j + 1) * 128].astype(f32) - origin
                total = total + apart
                square = square + apart * apart
            sums[mine, :] = total
            squares[mine, :] = square

    def normalise(t):
        @pl.loop(t * third, (t + 1) * third, step=32)
        def _(start_row):
            mine = pl.ds(pl.multiple_of(start_row, 32), 32)
            shift = jnp.sum(sums[mine, :], axis=1, keepdims=True) * (1.0 / model_width)
            square = jnp.sum(squares[mine, :], axis=1, keepdims=True) * (1.0 / model_width)
            inv = lax.rsqrt(jnp.maximum(square - shift * shift, 0.0) + EPS)
            inv = jnp.broadcast_to(inv, (32, 128))
            mean = pivot[mine, :] + shift
            for j in range(model_width // 128):
                w, lanes = j * 128 // part, slice(j * 128 % part, j * 128 % part + 128)
                value = (slabs[w, mine, lanes].astype(f32) - mean) * inv
                value = value.reshape(4, 8, 128) * gains[:, j * 128 : (j + 1) * 128][None]
                value = value + biases[:, j * 128 : (j + 1) * 128][None]
                normed[w, mine, lanes] = value.reshape(32, 128).astype(bf16)

    def from_core(h, du, dv):
        remote(("core", h, du, dv), block(h, du, dv, c=1 - core), partner).wait_recv()

    def multiply_pair(pair):
        acc[...] += jnp.dot(normed[pair], weights[pair], preferred_element_type=f32)

    def multiply(dy, what):
        for dx in OFFSETS:
            if (dx == 2 and what != "near") or (dx != 2 and what != "far"):
                from_core(0, dx, dy)
                from_core(1, dy, dx)
        first_pair = (y + dy + SIDE) % SIDE * 2
        if what == "row":
            pl.loop(first_pair, first_pair + 2)(multiply_pair)
        elif what == "near":
            multiply_pair(first_pair + x // 2)
        else:
            multiply_pair(first_pair + 1 - x // 2)

    for t in range(THIRDS):
        add_sums(z, t)

    seen = set()
    for event in arrivals_in_order():
        seen.add(event)
        if event[0] == "own on":
            h = event[1]
            arrive("own on", h, 1)
            arrive("own on", h, -1)
            start("row", h, 2, 1)
            start("row", h, 2, -1)
            start("core", h, 2, 0)
        elif event[0] == "row":
            arrive(*event)
            _, h, du, s = event
            start("row on", h, du, s)
            start("core", h, du, -s)
        elif event[0] == "row on":
            _, h, du = event
            arrive("row on", h, du, 1)
            arrive("row on", h, du, -1)
            start("core", h, du, 2)
        elif event[0] == "z":
            _, k, s, t = event
            z_copy(k, s, t).wait_recv()
            if k < 3 or (k == 3 and t in dict(last_parts(s))):
                z_copy(k + 1, s, t).start()
            if k < 4:
                add_sums((z - k * s + DEPTH) % DEPTH, t)
            elif all(("z", 4, d, t) in seen for d in (1, -1) if t in dict(last_parts(d))):
                add_sums((z + 4) % DEPTH, t)
                normalise(t)
        else:
            what, dy = event.split()
            multiply(int(dy), what)

    lanes = iota((1, width), 1) % HEAD
    rotated = [lanes[:, j * 128 : (j + 1) * 128] for j in range(width // 128)]
    for t in range(THIRDS):
        for r in range(req_count):
            here = pl.ds(t * third + r * CHIPS, CHIPS)
            there = pl.ds(r * fresh + t * CHIPS, CHIPS)
            cosine, sine = cosines[here, :], sines[here, :]
            for kind, ref in enumerate((q_ref, k_ref, v_ref)):
                for j in range(width // 128):
                    column = kind * width + j * 128
                    value = acc[here, column : column + 128]
                    if kind < 2:
                        near = jnp.where(
                            rotated[j] < turning,
                            pltpu.roll(value, 128 - turning, 1),
                            pltpu.roll(value, turning, 1),
                        )
                        value = jnp.where(rotated[j] < ROT, value * cosine + near * sine, value)
                    ref[there, j * 128 : (j + 1) * 128] = value.astype(bf16)

    def sent(kind, ref):
        name = ("z", 4, 1, 0) if kind == "z last" else next(n for n in NUMBER if n[0] == kind)
        remote(name, ref, partner).wait_send()

    sent("own", weights.at[0, pl.ds(0, 2 * depth), :])
    sent("own on", weights.at[0, pl.ds(0, depth), :])
    sent("row", weights.at[pl.ds(0, 2)])
    sent("row on", weights.at[0])
    sent("core", weights.at[pl.ds(0, 4)])
    sent("z", slabs.at[pl.ds(0, 6)])
    sent("z last", slabs.at[0])
    sent("swap", in1)
    sent("first", in1.at[pl.ds(0, CHIPS - 1)])
    sent("second", in1.at[pl.ds(0, CHIPS - 1)])


def project(lengths, x, w, group_of, gain, bias, col_bias):
    tokens, part = x.shape
    depth, cols = w.shape
    width = cols // 3
    lanes = tokens * part // (CHIPS * 8)
    f32, bf16 = jnp.float32, jnp.bfloat16
    out = jax.ShapeDtypeStruct((tokens, width), bf16)
    anywhere = pl.BlockSpec(memory_space=pl.ANY)
    vmem = pl.BlockSpec(memory_space=pltpu.VMEM)
    message = pltpu.VMEM((CHIPS, 8, lanes), bf16)
    wide = pltpu.VMEM((tokens, 128), f32)
    copies = pltpu.SemaphoreType.DMA((len(NUMBER),))
    return pl.pallas_call(
        project_kernel,
        out_shape=(out, out, out),
        in_specs=[anywhere] * 7,
        out_specs=(vmem, vmem, vmem),
        scratch_shapes=[
            pltpu.SMEM(lengths.shape, jnp.int32),
            pltpu.VMEM((tokens, part), bf16),
            pltpu.VMEM((depth, cols), bf16),
            pltpu.VMEM(group_of.shape, jnp.int32),
            pltpu.VMEM(gain.shape, bf16),
            pltpu.VMEM(bias.shape, bf16),
            pltpu.VMEM(col_bias.shape, bf16),
            pltpu.VMEM((CHIPS // 2, 4 * depth, cols), bf16),
            pltpu.VMEM((DEPTH, tokens, part), bf16),
            pltpu.VMEM((DEPTH, tokens, part), bf16),
            pltpu.VMEM((tokens, cols), f32),
            wide,
            wide,
            wide,
            wide,
            wide,
            pltpu.VMEM((8, part * DEPTH), f32),
            pltpu.VMEM((8, part * DEPTH), f32),
            message,
            message,
            message,
            message,
            message,
            pltpu.SemaphoreType.DMA((7,)),
            pltpu.SemaphoreType.DMA((len(SENDS),)),
            copies,
        ],
        compiler_params=pltpu.CompilerParams(
            collective_id=0, has_side_effects=True, vmem_limit_bytes=40 << 20
        ),
        cost_estimate=pl.CostEstimate(flops=10**11, bytes_accessed=10**8, transcendentals=0),
    )(lengths, x, w, group_of, gain, bias, col_bias)


def per_device(
    arrivals, group_of, lengths, page_table, ln_gain, ln_bias, w_qkv, qkv_bias, key_pool, value_pool
):
    req_count, fresh, part = arrivals.shape
    x = arrivals.reshape(req_count * fresh, part)
    operands = (lengths, x, w_qkv, group_of, ln_gain, ln_bias, qkv_bias)
    q, k, v = project(*(pltpu.with_memory_space_constraint(a, pltpu.HBM) for a in operands))
    outs = attention(lengths, page_table, q, k, v, key_pool, value_pool)
    return tuple(a.reshape(req_count, fresh, -1) for a in outs)


def solution(mesh):
    in_specs = (
        P("req", None, "wgt"),
        P(),
        P("req"),
        P("req", None),
        P(),
        P(),
        P("req", "wgt"),
        P("wgt"),
        P("req", None, "wgt"),
        P("req", None, "wgt"),
    )
    out_specs = (P("req", None, "wgt"), P("req", None, "wgt"), P("req", None, "wgt"))
    return jax.shard_map(
        per_device, mesh=mesh, in_specs=in_specs, out_specs=out_specs, check_vma=False
    )
```

```python
import math

import jax
import jax.numpy as jnp
from jax import lax
from jax.experimental import pallas as pl
from jax.experimental.pallas import tpu as pltpu
from jax.sharding import PartitionSpec as P
import numpy as np

HEAD = 96
ROT = 24
EPS = 1e-05
CHUNK_PAGES = 4
VMEM_BYTES = 67043328


def attention_kernel(
    lengths, table, q_ref, k_ref, v_ref, key_pool, value_pool, out_hbm, nk_hbm, nv_hbm,
    out_ref, queries, scores, peaks, offsets, totals, mixed, work, io,
):
    f32, bf16 = jnp.float32, jnp.bfloat16
    req_count, maxp = table.shape
    page, width = key_pool.shape[1], key_pool.shape[2]
    fresh = q_ref.shape[0] // req_count
    heads = width // HEAD
    rows = heads * fresh
    span = CHUNK_PAGES * page
    factor = math.log2(math.e) / math.sqrt(HEAD)
    low = -1e30

    count = 0
    for r in range(req_count):
        chunks = (lengths[r] + (span - 1)) // span

        @pl.loop(0, chunks)
        def _(n):
            i = count + n
            work[0, i] = r
            work[1, i] = n

        count = count + chunks

    def chunk(pool, i):
        r, n = work[0, i], work[1, i]
        pages = [pool[table[r, n * CHUNK_PAGES + p]] for p in range(CHUNK_PAGES)]
        return jnp.concatenate(pages, axis=0)

    stores = [
        pltpu.make_async_copy(k_ref, nk_hbm, io.at[0]),
        pltpu.make_async_copy(v_ref, nv_hbm, io.at[1]),
        pltpu.make_async_copy(out_ref, out_hbm, io.at[2]),
    ]
    stores[0].start()
    stores[1].start()

    iota = lambda shape, axis: lax.broadcasted_iota(jnp.int32, shape, axis)
    row_head = iota((rows, 256), 0) // fresh
    own_head = (iota((rows, 256), 1) + row_head // 2 * 128) // HEAD == row_head
    half_rows = rows // 2
    halves = ((slice(0, half_rows), slice(0, 256)), (slice(half_rows, rows), slice(128, 384)))
    causal = iota((rows, fresh), 0) % fresh >= iota((rows, fresh), 1)
    column = iota((1, span), 1)

    def fold(value, op):
        folded = value[:, :128]
        for n in range(1, value.shape[1] // 128):
            folded = op(folded, value[:, n * 128 : (n + 1) * 128])
        return folded

    across = (((1,), (1,)), ((), ()))

    def times_keys(query, keys):
        products = [
            lax.dot_general(query[group], keys[:, lanes], across, preferred_element_type=f32)
            for group, lanes in halves
        ]
        return jnp.concatenate(products, axis=0)

    def times_values(weights, values):
        weights = weights.astype(bf16)
        products = [
            jnp.dot(weights[group], values[:, lanes], preferred_element_type=f32)
            for group, lanes in halves
        ]
        return jnp.concatenate(products, axis=0)

    fresh_scores = []
    for r in range(req_count):
        mine = pl.ds(r * fresh, fresh)
        query = jnp.concatenate([q_ref[mine, lanes] for _, lanes in halves for _ in (0, 1)], axis=0)
        query = jnp.where(own_head, query, jnp.zeros_like(query))
        queries[r] = query
        own = times_keys(query, k_ref[mine, :])
        own = jnp.where(causal, own, low)
        fresh_scores.append(own)
        peaks[r] = jnp.broadcast_to(jnp.max(own, axis=1, keepdims=True), (rows, 128))
        totals[r] = jnp.zeros((rows, 128), f32)

    def over_chunks(step):
        @pl.loop(0, count // 2)
        def _(j):
            step((2 * j, 2 * j + 1))

        @pl.when(count % 2 == 1)
        def _():
            step((count - 1,))

    def first(chunks):
        values = []
        for i in chunks:
            r, n = work[0, i], work[1, i]
            keys = chunk(key_pool, i)
            value = times_keys(queries[r], keys)
            values.append(value + jnp.where(column < lengths[r] - n * span, 0.0, low))
        for i, value in zip(chunks, values):
            r = work[0, i]
            scores[i] = value
            peaks[r] = jnp.maximum(peaks[r], fold(value, jnp.maximum))

    over_chunks(first)

    fresh_totals = []
    for r in range(req_count):
        mine = pl.ds(r * fresh, fresh)
        offset = jnp.max(peaks[r], axis=1, keepdims=True) * factor
        offsets[r] = jnp.broadcast_to(offset, (rows, 128))
        weights = jnp.exp2(fresh_scores[r] * factor - offset)
        mixed[r] = times_values(weights, v_ref[mine, :])
        fresh_totals.append(jnp.sum(weights, axis=1, keepdims=True))

    def second(chunks):
        parts = []
        for i in chunks:
            r = work[0, i]
            values = chunk(value_pool, i)
            offset = jnp.concatenate([offsets[r]] * (span // 128), axis=1)
            weights = jnp.exp2(scores[i] * factor - offset)
            part = times_values(weights, values)
            parts.append((part, fold(weights, jnp.add)))
        for i, (part, total) in zip(chunks, parts):
            r = work[0, i]
            mixed[r] += part
            totals[r] += total

    over_chunks(second)

    for r in range(req_count):
        total = jnp.sum(totals[r], axis=1, keepdims=True) + fresh_totals[r]
        part = jnp.where(own_head, mixed[r] * (1.0 / total), 0.0)
        low_pair = part[:fresh] + part[fresh : 2 * fresh]
        high_pair = part[2 * fresh : 3 * fresh] + part[3 * fresh :]
        middle = low_pair[:, 128:] + high_pair[:, :128]
        value = jnp.concatenate([low_pair[:, :128], middle, high_pair[:, 128:]], axis=1)
        out_ref[pl.ds(r * fresh, fresh), :] = value.astype(out_ref.dtype)

    stores[2].start()
    for copy in stores:
        copy.wait()


def attention(lengths, table, q, k, v, key_pool, value_pool):
    rows, width = q.shape
    page = key_pool.shape[1]
    req_count, maxp = table.shape
    chunks = req_count * maxp // CHUNK_PAGES
    wide = width // HEAD * (rows // req_count)
    f32, bf16 = jnp.float32, jnp.bfloat16
    out = jax.ShapeDtypeStruct((rows, width), bf16)
    smem = pl.BlockSpec(memory_space=pltpu.SMEM)
    vmem = pl.BlockSpec(memory_space=pltpu.VMEM)
    anywhere = pl.BlockSpec(memory_space=pl.ANY)
    return pl.pallas_call(
        attention_kernel,
        out_shape=(out, out, out),
        in_specs=[smem, smem] + [vmem] * 5,
        out_specs=(anywhere, anywhere, anywhere),
        scratch_shapes=[
            pltpu.VMEM((rows, width), bf16),
            pltpu.VMEM((req_count, wide, 256), bf16),
            pltpu.VMEM((chunks, wide, CHUNK_PAGES * page), f32),
            pltpu.VMEM((req_count, wide, 128), f32),
            pltpu.VMEM((req_count, wide, 128), f32),
            pltpu.VMEM((req_count, wide, 128), f32),
            pltpu.VMEM((req_count, wide, 256), f32),
            pltpu.SMEM((2, chunks), jnp.int32),
            pltpu.SemaphoreType.DMA((3,)),
        ],
        compiler_params=pltpu.CompilerParams(vmem_limit_bytes=30 << 20),
    )(lengths, table, q, k, v, key_pool, value_pool)


MESH = pl.DeviceIdType.MESH
SIDE = 4
CHIPS = SIDE * SIDE
DEPTH = 8
OFFSETS = (0, -1, 1, 2)
THIRDS = 3


def last_parts(s):
    return ((0, None), (1, 0)) if s == 1 else ((2, None), (1, 1))


def copy_numbers():
    names = []
    for h in (0, 1):
        names += [("own", h, s) for s in (1, -1)]
        names += [("own on", h, s) for s in (1, -1)]
        names += [("row", h, du, s) for du in OFFSETS for s in (1, -1)]
        names += [("row on", h, du, s) for du in OFFSETS[:-1] for s in (1, -1)]
        names += [("row on", h, 2, s, p) for s in (1, -1) for p in (0, 1)]
        names += [("core", h, du, dv) for du in OFFSETS for dv in OFFSETS if (du, dv) != (2, 2)]
        names += [("core", h, 2, 2, s, p) for s in (1, -1) for p in (0, 1)]
    for s in (1, -1):
        names += [("z", k, s, t) for k in (1, 2, 3) for t in range(THIRDS)]
        names += [("z", 4, s, t) for t, _ in last_parts(s)]
    names += [("swap",), ("first",), ("second",)]
    return {name: number for number, name in enumerate(names)}


NUMBER = copy_numbers()
SENDS = ("own", "own on", "row", "row on", "core", "z", "z last", "swap", "first", "second")


def send_number(name):
    if name[:2] == ("z", 4):
        return SENDS.index("z last")
    return SENDS.index(name[0])


def arrivals_in_order():
    rows = lambda du: [("row", h, du, s) for h in (1, 0) for s in (1, -1)]
    rows_on = lambda du: [("row on", 1, du), ("row on", 0, du)]
    thirds = lambda k, *ts: [("z", k, s, t) for t in ts for s in (1, -1)]
    order = rows(0) + thirds(1, 0) + [("own on", 0), ("own on", 1)] + thirds(1, 1, 2)
    order += rows(-1) + thirds(2, 0, 1, 2) + rows(1) + thirds(3, 0) + rows_on(0) + thirds(3, 1, 2)
    order += rows(2) + [("z", 4, -1, 1), ("z", 4, 1, 0), ("z", 4, 1, 1), ("z", 4, -1, 2)]
    order += rows_on(-1) + ["row 0"] + rows_on(1) + ["row -1"]
    order += [("last", 0), ("last", 1), "row 1", "near 2", "far 2"]
    return order


def project_kernel(
    lengths_hbm, x_hbm, w_hbm, group_hbm, gain_hbm, bias_hbm, col_bias_hbm, q_ref, k_ref, v_ref,
    lengths, x_ref, w_ref, group_ref, gain_ref, bias_ref, col_bias_ref, weights, slabs, normed, acc, cosines, sines, pivot, sums, squares, gains, biases,
    out1, in1, swapped, out2, in2, load, send, recv,
):
    f32, bf16, i32 = jnp.float32, jnp.bfloat16, jnp.int32
    tokens, part = x_ref.shape
    depth, cols = w_ref.shape
    model_width = part * DEPTH
    req_count = lengths.shape[0]
    fresh = tokens // req_count
    half = part // 2
    third = tokens // THIRDS
    width = cols // 3
    rows_half, rows_sub = depth // 2, depth // 4
    me, z = lax.axis_index("req"), lax.axis_index("wgt")
    core = me % 2
    chip = me // 2
    y, x = chip // SIDE, chip % SIDE
    iota = lambda shape, axis: lax.broadcasted_iota(i32, shape, axis)

    def device(number, c=core):
        return (number * 2 + c, z)

    partner = device(chip, 1 - core)

    pairs = (
        (x_hbm, x_ref), (w_hbm, w_ref), (group_hbm, group_ref), (lengths_hbm, lengths),
        (gain_hbm, gain_ref), (bias_hbm, bias_ref), (col_bias_hbm, col_bias_ref),
    )
    loads = [pltpu.make_async_copy(a, b, load.at[n]) for n, (a, b) in enumerate(pairs)]
    loads[0].start()

    barrier = pltpu.get_barrier_semaphore()

    for d in range(1, CHIPS):
        pl.semaphore_signal(barrier, 1, device_id=device((chip + d) % CHIPS), device_id_type=MESH)

    pl.semaphore_signal(barrier, 1, device_id=partner, device_id_type=MESH)
    for s in (1, DEPTH - 1):
        pl.semaphore_signal(barrier, 1, device_id=(me, (z + s) % DEPTH), device_id_type=MESH)

    for copy in loads[1:]:
        copy.start()

    loads[0].wait()
    m, n = iota((CHIPS * 8, tokens), 0), iota((CHIPS * 8, tokens), 1)
    for t in range(THIRDS):
        take = (m % 8) // 2 * fresh + t * CHIPS + m // 8 == n
        piece = jnp.zeros((CHIPS * 8, half), f32)
        for h in (0, 1):
            chosen = jnp.where(take & (m % 2 == h), 1.0, 0.0).astype(bf16)
            piece += jnp.dot(chosen, x_ref[:, h * half : (h + 1) * half], preferred_element_type=f32)
        out1[:, :, t * half : (t + 1) * half] = piece.reshape(CHIPS, 8, half).astype(bf16)
    in1[chip] = out1[chip]

    pl.semaphore_wait(barrier, CHIPS - 1 + 3)

    def spread(name, source, target):
        for d in range(1, CHIPS):
            other = (chip + d) % CHIPS
            remote((name,), source.at[other], device(other), target.at[chip]).start()

    def gathered(name, target):
        ref = target.at[pl.ds(0, CHIPS - 1)]
        remote((name,), ref, partner).wait_recv()

    def remote(name, ref, target, dst=None):
        return pltpu.make_async_remote_copy(
            src_ref=ref,
            dst_ref=ref if dst is None else dst,
            send_sem=send.at[send_number(name)],
            recv_sem=recv.at[NUMBER[name]],
            device_id=target,
            device_id_type=MESH,
        )

    spread("first", out1, in1)

    def by_kind(value):
        heads = range(width // HEAD)
        return jnp.concatenate(
            [
                value[:, (h * 3 + kind) * HEAD : (h * 3 + kind + 1) * HEAD]
                for kind in range(3)
                for h in heads
            ],
            axis=1,
        )

    def place(number, c):
        return number // 2, (number % 2) * (2 * depth) + c * depth

    loads[1].wait()
    own_pair, own_row = place(chip, core)
    weights[own_pair, pl.ds(pl.multiple_of(own_row, 64), depth), :] = by_kind(w_ref[...])

    where = {0: (x, y), 1: (y, x)}

    def chip_at(h, du, dv):
        u, v = where[h]
        u, v = (u + du + SIDE) % SIDE, (v + dv + SIDE) % SIDE
        return v * SIDE + u if h == 0 else u * SIDE + v

    def block(h, du, dv, c=core, start_row=0, count=rows_half):
        pair, row = place(chip_at(h, du, dv), c)
        row = row + h * rows_half + start_row
        return weights.at[pair, pl.ds(pl.multiple_of(row, 16), count), :]

    def sub_rows(s, p=None):
        start_row = 0 if s == 1 else rows_sub
        if p is None:
            return start_row, rows_sub
        return (start_row, rows_sub - 16) if p == 0 else (start_row + rows_sub - 16, 16)

    def weight_copy(name):
        kind, h = name[0], name[1]
        if kind == "own":
            return remote(name, block(h, 0, 0), device(chip_at(h, name[2], 0)))
        if kind == "own on":
            s = name[2]
            return remote(name, block(h, -s, 0, core, *sub_rows(s)), device(chip_at(h, s, 0)))
        if kind == "row":
            du, s = name[2], name[3]
            return remote(name, block(h, du, 0), device(chip_at(h, 0, s)))
        if kind == "row on":
            du, s = name[2], name[3]
            return remote(name, block(h, du, -s, core, *sub_rows(*name[3:])), device(chip_at(h, 0, s)))
        du, dv = name[2], name[3]
        rows = sub_rows(*name[4:]) if len(name) > 4 else ()
        return remote(name, block(h, du, dv, core, *rows), partner)

    def start(*name):
        weight_copy(name).start()

    def arrive(*name):
        weight_copy(name).wait_recv()

    for h in (0, 1):
        for s in (1, -1):
            start("own", h, s)
    for h in (0, 1):
        start("core", h, 0, 0)

    a, b = iota((CHIPS * 8, CHIPS * 8), 0), iota((CHIPS * 8, CHIPS * 8), 1)
    loads[2].wait()
    groups = group_ref[...].reshape(1, -1)
    group_row = jnp.broadcast_to(groups, a.shape)
    group_col = jnp.sum(jnp.where(a == b, group_row, 0), axis=1, keepdims=True)
    rank = jnp.sum(jnp.where((group_col == group_row) & (a < b), 1, 0), axis=0, keepdims=True)
    slot_row = groups * req_count + rank
    slot_col = jnp.sum(jnp.where(a == b, jnp.broadcast_to(slot_row, a.shape), 0), axis=1, keepdims=True)

    def selector(c):
        arriving = (b // 8 * 2 + c) * req_count + b % 8 // 2
        slot = jnp.sum(jnp.where(a == arriving, slot_col, 0), axis=0, keepdims=True)
        wanted = (a // 8 * 2 + core) * req_count + a % 8 // 2
        return jnp.where((wanted == slot) & (a % 2 == b % 2), 1.0, 0.0).astype(bf16)

    pick_own, pick_other = selector(core), selector(1 - core)

    gathered("first", in1)

    swap = remote(("swap",), in1, partner, swapped)
    swap.start()

    def flat(ref):
        return ref[...].astype(f32).reshape(CHIPS * 8, THIRDS * half).astype(bf16)

    mixed = jnp.dot(pick_own, flat(in1), preferred_element_type=f32)
    swap.wait_recv()
    mixed = mixed + jnp.dot(pick_other, flat(swapped), preferred_element_type=f32)
    out2[...] = mixed.reshape(CHIPS, 8, THIRDS * half).astype(bf16)
    in2[chip] = out2[chip]

    spread("second", out2, in2)

    for h in (0, 1):
        for s in (1, -1):
            start("row", h, 0, s)

    for copy in loads[3:]:
        copy.wait()
    gains[...] = jnp.broadcast_to(gain_ref[...].astype(f32).reshape(1, -1), gains.shape)
    biases[...] = jnp.broadcast_to(bias_ref[...].astype(f32).reshape(1, -1), biases.shape)
    acc[...] = jnp.broadcast_to(by_kind(col_bias_ref[...].astype(f32).reshape(1, -1)), acc.shape)

    lane = iota((1, 128), 1) % 32
    turning = ROT // 2
    inverse = jnp.zeros((1, 128), f32)
    for i in range(turning):
        value = float(np.float32(10000.0) ** np.float32(-2.0 * i / ROT))
        inverse = jnp.where((lane == i) | (lane == i + turning), value, inverse)
    row = iota((tokens, 1), 0)
    request = row % third // CHIPS
    position = row // third * CHIPS + row % CHIPS
    for r in range(req_count):
        position = position + jnp.where(request == r, lengths[r], 0)
    angle = position.astype(f32) * inverse
    cosines[...] = jnp.cos(angle)
    sine = jnp.sin(angle)
    sines[...] = jnp.where(lane < turning, -sine, sine)

    for h in (0, 1):
        for s in (1, -1):
            arrive("own", h, s)
    for h in (0, 1):
        for s in (1, -1):
            start("own on", h, s)
    for h in (0, 1):
        for s in (1, -1):
            start("core", h, -s, 0)
    for s in (1, -1):
        for h in (0, 1):
            start("row", h, -s, 1)
            start("row", h, -s, -1)

    gathered("second", in2)

    m, n = iota((third, CHIPS * 8), 0), iota((third, CHIPS * 8), 1)
    pieces = flat(in2)
    for h in (0, 1):
        chosen = jnp.where(m % CHIPS * 8 + m // CHIPS * 2 + h == n, 1.0, 0.0).astype(bf16)
        rows = jnp.dot(chosen, pieces, preferred_element_type=f32).astype(bf16)
        for t in range(THIRDS):
            slabs[z, pl.ds(t * third, third), h * half : (h + 1) * half] = rows[:, t * half : (t + 1) * half]

    def slab(k, s, t, piece=None):
        ref = slabs.at[(z - k * s + DEPTH) % DEPTH]
        if piece is None:
            return ref.at[pl.ds(t * third, third), :]
        return ref.at[pl.ds(t * third + piece * (third // 2), third // 2), :]

    def z_copy(k, s, t):
        piece = dict(last_parts(s))[t] if k == 4 else None
        return remote(("z", k, s, t), slab(k - 1, s, t, piece), (me, (z + s + DEPTH) % DEPTH))

    for t in range(THIRDS):
        for s in (1, -1):
            z_copy(1, s, t).start()

    def folded(value):
        total = value[:, :128]
        for j in range(1, part // 128):
            total = total + value[:, j * 128 : (j + 1) * 128]
        return total

    for t in range(THIRDS):
        mine = pl.ds(t * third, third)
        own = jnp.sum(folded(slabs[z, mine, :].astype(f32)), axis=1, keepdims=True) * (1.0 / part)
        pivot[mine, :] = jnp.broadcast_to(own, (third, 128))
    sums[...] = jnp.zeros_like(sums)
    squares[...] = jnp.zeros_like(squares)

    def add_sums(number, t):
        @pl.loop(t * third, (t + 1) * third, step=32)
        def _(start_row):
            mine = pl.ds(pl.multiple_of(start_row, 32), 32)
            origin, total, square = pivot[mine, :], sums[mine, :], squares[mine, :]
            for j in range(part // 128):
                apart = slabs[number, mine, j * 128 : (j + 1) * 128].astype(f32) - origin
                total = total + apart
                square = square + apart * apart
            sums[mine, :] = total
            squares[mine, :] = square

    def normalise(t):
        @pl.loop(t * third, (t + 1) * third, step=32)
        def _(start_row):
            mine = pl.ds(pl.multiple_of(start_row, 32), 32)
            shift = jnp.sum(sums[mine, :], axis=1, keepdims=True) * (1.0 / model_width)
            square = jnp.sum(squares[mine, :], axis=1, keepdims=True) * (1.0 / model_width)
            inv = lax.rsqrt(jnp.maximum(square - shift * shift, 0.0) + EPS)
            inv = jnp.broadcast_to(inv, (32, 128))
            mean = pivot[mine, :] + shift
            for j in range(model_width // 128):
                w, lanes = j * 128 // part, slice(j * 128 % part, j * 128 % part + 128)
                value = (slabs[w, mine, lanes].astype(f32) - mean) * inv
                value = value.reshape(4, 8, 128) * gains[:, j * 128 : (j + 1) * 128][None]
                value = value + biases[:, j * 128 : (j + 1) * 128][None]
                normed[w, mine, lanes] = value.reshape(32, 128).astype(bf16)

    def from_core(h, du, dv):
        if (du, dv) != (2, 2):
            remote(("core", h, du, dv), block(h, du, dv, 1 - core), partner).wait_recv()
            return
        for s in (1, -1):
            for p in (0, 1):
                ref = block(h, 2, 2, 1 - core, *sub_rows(s, p))
                remote(("core", h, 2, 2, s, p), ref, partner).wait_recv()

    def multiply_pair(pair):
        acc[...] += jnp.dot(normed[pair], weights[pair], preferred_element_type=f32)

    def multiply(dy, what):
        for dx in OFFSETS:
            if (dx == 2 and what != "near") or (dx != 2 and what != "far"):
                from_core(0, dx, dy)
                from_core(1, dy, dx)
        first_pair = (y + dy + SIDE) % SIDE * 2
        if what == "row":
            pl.loop(first_pair, first_pair + 2)(multiply_pair)
        elif what == "near":
            multiply_pair(first_pair + x // 2)
        else:
            multiply_pair(first_pair + 1 - x // 2)

    for t in range(THIRDS):
        add_sums(z, t)

    seen = set()
    for event in arrivals_in_order():
        seen.add(event)
        if event[0] == "own on":
            h = event[1]
            arrive("own on", h, 1)
            arrive("own on", h, -1)
            start("row", h, 2, 1)
            start("row", h, 2, -1)
            start("core", h, 2, 0)
        elif event[0] == "row":
            arrive(*event)
            _, h, du, s = event
            if du == 2:
                start("row on", h, 2, s, 0)
                start("row on", h, 2, s, 1)
            else:
                start("row on", h, du, s)
            start("core", h, du, -s)
        elif event[0] == "last":
            for h in (1, 0):
                for s in (1, -1):
                    arrive("row on", h, 2, s, event[1])
                    start("core", h, 2, 2, s, event[1])
        elif event[0] == "row on":
            _, h, du = event
            arrive("row on", h, du, 1)
            arrive("row on", h, du, -1)
            start("core", h, du, 2)
        elif event[0] == "z":
            _, k, s, t = event
            z_copy(k, s, t).wait_recv()
            if k < 3 or (k == 3 and t in dict(last_parts(s))):
                z_copy(k + 1, s, t).start()
            if k < 4:
                add_sums((z - k * s + DEPTH) % DEPTH, t)
            elif all(("z", 4, d, t) in seen for d in (1, -1) if t in dict(last_parts(d))):
                add_sums((z + 4) % DEPTH, t)
                normalise(t)
        else:
            what, dy = event.split()
            multiply(int(dy), what)

    lanes = iota((1, width), 1) % HEAD
    rotated = [lanes[:, j * 128 : (j + 1) * 128] for j in range(width // 128)]
    for t in range(THIRDS):
        for r in range(req_count):
            here = pl.ds(t * third + r * CHIPS, CHIPS)
            there = pl.ds(r * fresh + t * CHIPS, CHIPS)
            cosine, sine = cosines[here, :], sines[here, :]
            for kind, ref in enumerate((q_ref, k_ref, v_ref)):
                for j in range(width // 128):
                    column = kind * width + j * 128
                    value = acc[here, column : column + 128]
                    if kind < 2:
                        near = jnp.where(
                            rotated[j] < turning,
                            pltpu.roll(value, 128 - turning, 1),
                            pltpu.roll(value, turning, 1),
                        )
                        value = jnp.where(rotated[j] < ROT, value * cosine + near * sine, value)
                    ref[there, j * 128 : (j + 1) * 128] = value.astype(bf16)

    def sent(kind, ref):
        name = ("z", 4, 1, 0) if kind == "z last" else next(n for n in NUMBER if n[0] == kind)
        remote(name, ref, partner).wait_send()

    sent("own", weights.at[0, pl.ds(0, 2 * depth), :])
    sent("own on", weights.at[0, pl.ds(0, depth), :])
    sent("row", weights.at[pl.ds(0, 2)])
    sent("row on", weights.at[0])
    sent("core", weights.at[pl.ds(0, 4)])
    sent("z", slabs.at[pl.ds(0, 6)])
    sent("z last", slabs.at[0])
    sent("swap", in1)
    sent("first", in1.at[pl.ds(0, CHIPS - 1)])
    sent("second", in1.at[pl.ds(0, CHIPS - 1)])


def project(lengths, x, w, group_of, gain, bias, col_bias):
    tokens, part = x.shape
    depth, cols = w.shape
    width = cols // 3
    lanes = tokens * part // (CHIPS * 8)
    f32, bf16 = jnp.float32, jnp.bfloat16
    out = jax.ShapeDtypeStruct((tokens, width), bf16)
    anywhere = pl.BlockSpec(memory_space=pl.ANY)
    vmem = pl.BlockSpec(memory_space=pltpu.VMEM)
    message = pltpu.VMEM((CHIPS, 8, lanes), bf16)
    wide = pltpu.VMEM((tokens, 128), f32)
    copies = pltpu.SemaphoreType.DMA((len(NUMBER),))
    return pl.pallas_call(
        project_kernel,
        out_shape=(out, out, out),
        in_specs=[anywhere] * 7,
        out_specs=(vmem, vmem, vmem),
        scratch_shapes=[
            pltpu.SMEM(lengths.shape, jnp.int32),
            pltpu.VMEM((tokens, part), bf16),
            pltpu.VMEM((depth, cols), bf16),
            pltpu.VMEM(group_of.shape, jnp.int32),
            pltpu.VMEM(gain.shape, bf16),
            pltpu.VMEM(bias.shape, bf16),
            pltpu.VMEM(col_bias.shape, bf16),
            pltpu.VMEM((CHIPS // 2, 4 * depth, cols), bf16),
            pltpu.VMEM((DEPTH, tokens, part), bf16),
            pltpu.VMEM((DEPTH, tokens, part), bf16),
            pltpu.VMEM((tokens, cols), f32),
            wide,
            wide,
            wide,
            wide,
            wide,
            pltpu.VMEM((8, part * DEPTH), f32),
            pltpu.VMEM((8, part * DEPTH), f32),
            message,
            message,
            message,
            message,
            message,
            pltpu.SemaphoreType.DMA((7,)),
            pltpu.SemaphoreType.DMA((len(SENDS),)),
            copies,
        ],
        compiler_params=pltpu.CompilerParams(
            collective_id=0, has_side_effects=True, vmem_limit_bytes=40 << 20
        ),
        cost_estimate=pl.CostEstimate(flops=10**11, bytes_accessed=10**8, transcendentals=0),
    )(lengths, x, w, group_of, gain, bias, col_bias)


def per_device(
    arrivals, group_of, lengths, page_table, ln_gain, ln_bias, w_qkv, qkv_bias, key_pool, value_pool
):
    req_count, fresh, part = arrivals.shape
    x = arrivals.reshape(req_count * fresh, part)
    operands = (lengths, x, w_qkv, group_of, ln_gain, ln_bias, qkv_bias)
    q, k, v = project(*(pltpu.with_memory_space_constraint(a, pltpu.HBM) for a in operands))
    outs = attention(lengths, page_table, q, k, v, key_pool, value_pool)
    return tuple(a.reshape(req_count, fresh, -1) for a in outs)


def solution(mesh):
    in_specs = (
        P("req", None, "wgt"),
        P(),
        P("req"),
        P("req", None),
        P(),
        P(),
        P("req", "wgt"),
        P("wgt"),
        P("req", None, "wgt"),
        P("req", None, "wgt"),
    )
    out_specs = (P("req", None, "wgt"), P("req", None, "wgt"), P("req", None, "wgt"))
    return jax.shard_map(
        per_device, mesh=mesh, in_specs=in_specs, out_specs=out_specs, check_vma=False
    )
```
